32 devices in a mesh: gx: 8 (over y, x, core), gy: 4 (over z).
Axes of the slice: x: 2, y: 2, z: 4, core: 2. Of those that a mesh axis runs over, the one named last changes fastest.
Arguments:
- checkpoint: float32 [19, 32, 64, 256], P(None, 'gx', 'gy'), may hold values from 0 to 1, as said below
- adjoint_end: float32 [19, 32, 64, 256], P(None, 'gx', 'gy'), may hold values from -6 to 6
- resistance: float32 [32, 64, 256], P('gx', 'gy'), may hold values from 0 to 0.4
- solid_mask: int32 [32, 64, 256], P('gx', 'gy'), may hold values 0 or 1
- flags: int32 [32, 64, 256], P('gx', 'gy'), may hold values from 0 to 2
Outputs:
- adjoint_start: float32 [19, 32, 64, 256], P(None, 'gx', 'gy')
- sensitivity: float32 [32, 64, 256], P('gx', 'gy')
The draws below stay inside these ranges and needn't reach their ends.
Inputs may be any that keep to these rules, and one draw needn't show every extreme that they name: `checkpoint`: every population is positive.
All inputs are finite; a program needn't handle non-finite values. No bound on the sum of `solid_mask` on one device may be relied on, other than what follows from the above.
Results may differ from the reference program's by a relative error of at most 0.0003.
Values sent between devices are 32-bit elements; how exact they have to be, the bound alone decides.
No kernel may reach another device: no remote copies, remote signals or barrier semaphores. Data moves between devices by JAX's collectives and lax.ppermute only.
A program may use at most 128 MiB of HBM per device.

```python
import jax
import jax.numpy as jnp
import numpy as np
from jax import lax

CX = 4
NZ = 256
NX = 32
NY = 64


VELOCITY = np.array([[0, 0, 0], [1, 0, 0], [-1, 0, 0], [0, 1, 0], [0, -1, 0], [0, 0, 1], [0, 0, -1], [1, 1, 0], [-1, -1, 0], [1, -1, 0], [-1, 1, 0], [1, 0, 1], [-1, 0, -1], [1, 0, -1], [-1, 0, 1], [0, 1, 1], [0, -1, -1], [0, 1, -1], [0, -1, 1]])


WEIGHTS = np.array([1.0 / 3.0] + [1.0 / 18.0] * 6 + [1.0 / 36.0] * 12)


def draw_checkpoint(key, part):
    keys = jax.random.split(jax.random.fold_in(key, 11), 3)
    density = jax.random.uniform(keys[0], (NX, NY, NZ), jnp.float32, 0.8, 1.2)
    flow = jax.random.uniform(keys[1], (3, NX, NY, NZ), jnp.float32, -0.1, 0.1)
    rough = jax.random.uniform(keys[2], (19, NX, NY, NZ), jnp.float32, 0.5, 1.5)
    velocities = jnp.asarray(VELOCITY, jnp.float32)
    projected = velocities[:, 0, None, None, None] * flow[0] + velocities[:, 1, None, None, None] * flow[1] + velocities[:, 2, None, None, None] * flow[2]
    weights_col = jnp.asarray(WEIGHTS, jnp.float32)[:, None, None, None]
    return (weights_col * density * (1.0 + 3.0 * projected) * rough).astype(jnp.float32)


def with_ends(values, own_key, smallest, top_value):
    longest = values.shape.index(max(values.shape))
    spots = []
    for shift in (0, 1):
        where = [jax.random.randint(jax.random.fold_in(own_key, axis), (), 0, length) for axis, length in enumerate(values.shape)]
        where[longest] = (where[longest] + shift) % values.shape[longest]
        spots.append(tuple(where))
    return values.at[spots[0]].set(smallest).at[spots[1]].set(top_value)


def levels(rng, extent, cuts, low, top_value):
    def one(axis_at, parts):
        heights = jax.random.uniform(jax.random.fold_in(jax.random.fold_in(rng, 6), axis_at), (parts,), jnp.float32, low / len(cuts), top_value / len(cuts))
        return jnp.repeat(jnp.exp(heights), extent[axis_at] // parts).reshape((-1,) + (1,) * (len(extent) - axis_at - 1))

    factor_of = one(*cuts[0])
    for cut in cuts[1:]:
        factor_of = factor_of * one(*cut)
    return factor_of


def noise(stream_key, extent, width, most, cuts=(), dtype=jnp.bfloat16):
    loudness = levels(stream_key, extent, cuts, -0.22, 0.18) if cuts else 1.0
    drawn = jax.random.normal(stream_key, extent, jnp.float32) * width * loudness
    return jnp.minimum(jnp.maximum(drawn, -most), most).astype(dtype)


def setup_inputs(seed: int = 0) -> dict:
    seeds = jax.random.split(jax.random.key(seed), 6)
    checkpoint = draw_checkpoint(jax.random.fold_in(seeds[5], 71), 0)
    adjoint_end = noise(seeds[1], (19, NX, NY, NZ), 1.0, 6.0, ((1, 8), (2, 4)), jnp.float32)
    resistance = jnp.clip(0.4 * jax.random.uniform(seeds[2], (NX, NY, NZ), jnp.float32) ** levels(seeds[2], (NX, NY, NZ), ((0, 8), (1, 4)), -0.2, 0.2), 0.0, 0.4)
    solid_mask = with_ends((jax.random.randint(seeds[3], (NX, NY, NZ), 0, 4) < 1).astype(jnp.int32), jax.random.fold_in(seeds[3], 1), 0, 1)
    flags = with_ends(jax.random.randint(seeds[4], (NX, NY, NZ), 0, 3), jax.random.fold_in(seeds[4], 1), 0, 2).astype(jnp.int32)
    return {"checkpoint": checkpoint, "adjoint_end": adjoint_end, "resistance": resistance, "solid_mask": solid_mask, "flags": flags}


VELOCITY = np.array([[0, 0, 0], [1, 0, 0], [-1, 0, 0], [0, 1, 0], [0, -1, 0], [0, 0, 1], [0, 0, -1], [1, 1, 0], [-1, -1, 0], [1, -1, 0], [-1, 1, 0], [1, 0, 1], [-1, 0, -1], [1, 0, -1], [-1, 0, 1], [0, 1, 1], [0, -1, -1], [0, 1, -1], [0, -1, 1]])
WEIGHTS = np.array([1.0 / 3.0] + [1.0 / 18.0] * 6 + [1.0 / 36.0] * 12)
OPPOSITE = np.array([0, 2, 1, 4, 3, 6, 5, 8, 7, 10, 9, 12, 11, 14, 13, 16, 15, 18, 17])
BASE_RATES = np.array([0.0, 1.19, 1.4, 0.0, 1.2, 0.0, 1.2, 0.0, 1.2, 0.0, 1.4, 0.0, 1.4, 0.0, 0.0, 0.0, 1.98, 1.98, 1.98])
SHEAR_ROWS = np.array([0.0] * 9 + [1.0, 0.0, 1.0, 0.0, 1.0, 1.0, 1.0, 0.0, 0.0, 0.0])

def moment_matrix():
    along_x = VELOCITY[:, 0] * 1.0
    along_y = VELOCITY[:, 1] * 1.0
    along_z = VELOCITY[:, 2] * 1.0
    square = along_x * along_x + along_y * along_y + along_z * along_z
    ones_row = np.ones(19)
    stacked = [ones_row, 19.0 * square - 30.0, (21.0 * square * square - 53.0 * square + 24.0) / 2.0, along_x, (5.0 * square - 9.0) * along_x, along_y, (5.0 * square - 9.0) * along_y, along_z, (5.0 * square - 9.0) * along_z, 3.0 * along_x * along_x - square, (3.0 * square - 5.0) * (3.0 * along_x * along_x - square), along_y * along_y - along_z * along_z, (3.0 * square - 5.0) * (along_y * along_y - along_z * along_z), along_x * along_y, along_y * along_z, along_x * along_z, (along_y * along_y - along_z * along_z) * along_x, (along_z * along_z - along_x * along_x) * along_y, (along_x * along_x - along_y * along_y) * along_z]
    return np.stack(stacked)

def collide(states, grey_level, solid, classes):
    highest = lax.Precision.HIGHEST
    moments = moment_matrix()
    inverse_moments = moments.T / np.sum(moments * moments, axis=1)
    velocities = jnp.asarray(VELOCITY, jnp.float32)
    weights_col = jnp.asarray(WEIGHTS, jnp.float32)[:, None, None, None]
    density = lax.optimization_barrier(jnp.sum(states, axis=0))
    velocity_field = jnp.einsum('qd,qxyz->dxyz', velocities, states, precision=highest) / density
    projected = jnp.einsum('qd,dxyz->qxyz', velocities, velocity_field, precision=highest)
    kinetic = lax.optimization_barrier(jnp.sum(velocity_field * velocity_field, axis=0))
    equilibrium = weights_col * density * (1.0 + 3.0 * projected + 4.5 * projected * projected - 1.5 * kinetic)
    departure = jnp.einsum('pq,qxyz->pxyz', jnp.asarray(moments, jnp.float32), states - equilibrium, precision=highest)
    shear_rate = jnp.where(classes == 0, 1.25, jnp.where(classes == 1, 0.9, 1.7)).astype(jnp.float32)
    relax_rates = jnp.asarray(BASE_RATES, jnp.float32)[:, None, None, None] + jnp.asarray(SHEAR_ROWS, jnp.float32)[:, None, None, None] * shear_rate
    relaxed = states - jnp.einsum('pq,qxyz->pxyz', jnp.asarray(inverse_moments, jnp.float32), relax_rates * departure, precision=highest)
    greyness = jnp.where(solid == 1, jnp.float32(1.0), grey_level)
    return (1.0 - greyness) * relaxed + greyness * states[OPPOSITE]

def stream(states, direction_sign):
    shifted = []
    for direction in range(19):
        offset = tuple((int(direction_sign * component) for component in VELOCITY[direction]))
        shifted.append(jnp.roll(states[direction], offset, axis=(0, 1, 2)))
    return jnp.stack(shifted)

def split_states(states):
    count_blocks = states.shape[1] // CX
    return jnp.moveaxis(states.reshape(19, count_blocks, CX, states.shape[2], states.shape[3]), 1, 0)

def join_states(blocked):
    return jnp.moveaxis(blocked, 0, 1).reshape(19, -1, blocked.shape[3], blocked.shape[4])

def split_cells(field):
    return field.reshape(-1, CX, field.shape[1], field.shape[2])

def join_cells(blocked):
    return blocked.reshape(-1, blocked.shape[2], blocked.shape[3])

def adjoint_local(states, cotangent, grey_level, solid, classes):

    def relax_at(inner_states, inner_grey):
        return collide(inner_states, inner_grey, solid, classes)
    _, backward = jax.vjp(relax_at, states, grey_level)
    return backward(cotangent)

def reference(checkpoint, adjoint_end, resistance, solid_mask, flags):
    grey_blocks = split_cells(resistance)
    solid_blocks = split_cells(solid_mask)
    class_blocks = split_cells(flags)
    post_start = lax.map(lambda packed: collide(*packed), (split_states(checkpoint), grey_blocks, solid_blocks, class_blocks))
    middle = stream(join_states(post_start), 1)
    pulled_end = stream(adjoint_end, -1)
    adjoint_blocks, sens_blocks = lax.map(lambda packed: adjoint_local(*packed), (split_states(middle), split_states(pulled_end), grey_blocks, solid_blocks, class_blocks))
    adjoint_middle = join_states(adjoint_blocks)
    sens_middle = join_cells(sens_blocks)
    pulled_middle = stream(adjoint_middle, -1)
    start_blocks, start_sens = lax.map(lambda packed: adjoint_local(*packed), (split_states(checkpoint), split_states(pulled_middle), grey_blocks, solid_blocks, class_blocks))
    return (join_states(start_blocks), sens_middle + join_cells(start_sens))
```

```python
import jax
import jax.numpy as jnp
import numpy as np
from jax import lax
from jax.sharding import PartitionSpec as P

VELOCITY = np.array(
    [
        [0, 0, 0],
        [1, 0, 0],
        [-1, 0, 0],
        [0, 1, 0],
        [0, -1, 0],
        [0, 0, 1],
        [0, 0, -1],
        [1, 1, 0],
        [-1, -1, 0],
        [1, -1, 0],
        [-1, 1, 0],
        [1, 0, 1],
        [-1, 0, -1],
        [1, 0, -1],
        [-1, 0, 1],
        [0, 1, 1],
        [0, -1, -1],
        [0, 1, -1],
        [0, -1, 1],
    ]
)
VELOCITY_LIST = [
    [0, 0, 0],
    [1, 0, 0],
    [-1, 0, 0],
    [0, 1, 0],
    [0, -1, 0],
    [0, 0, 1],
    [0, 0, -1],
    [1, 1, 0],
    [-1, -1, 0],
    [1, -1, 0],
    [-1, 1, 0],
    [1, 0, 1],
    [-1, 0, -1],
    [1, 0, -1],
    [-1, 0, 1],
    [0, 1, 1],
    [0, -1, -1],
    [0, 1, -1],
    [0, -1, 1],
]
WEIGHTS = np.array([1.0 / 3.0] + [1.0 / 18.0] * 6 + [1.0 / 36.0] * 12)
OPPOSITE = np.array([0, 2, 1, 4, 3, 6, 5, 8, 7, 10, 9, 12, 11, 14, 13, 16, 15, 18, 17])
BASE_RATES = np.array(
    [
        0.0,
        1.19,
        1.4,
        0.0,
        1.2,
        0.0,
        1.2,
        0.0,
        1.2,
        0.0,
        1.4,
        0.0,
        1.4,
        0.0,
        0.0,
        0.0,
        1.98,
        1.98,
        1.98,
    ]
)
SHEAR_ROWS = np.array([0.0] * 9 + [1.0, 0.0, 1.0, 0.0, 1.0, 1.0, 1.0, 0.0, 0.0, 0.0])


def padded_2(block, sides, width):
    for axis, dim in sides:
        count = lax.axis_size(axis)
        forward = [(i, i + 1) for i in range(count - 1)]
        forward.append((count - 1, 0))
        backward = [(target, source) for source, target in forward]
        low = lax.ppermute(
            lax.slice_in_dim(block, block.shape[dim] - width, None, axis=dim), axis, forward
        )
        high = lax.ppermute(lax.slice_in_dim(block, 0, width, axis=dim), axis, backward)
        block = jnp.concatenate([low, block, high], axis=dim)
    return block


def moment_matrix():
    along_x = VELOCITY[:, 0] * 1.0
    along_y = VELOCITY[:, 1] * 1.0
    along_z = VELOCITY[:, 2] * 1.0
    square = along_x * along_x + along_y * along_y + along_z * along_z
    ones_row = np.ones(19)
    stacked = [
        ones_row,
        19.0 * square - 30.0,
        (21.0 * square * square - 53.0 * square + 24.0) / 2.0,
        along_x,
        (5.0 * square - 9.0) * along_x,
        along_y,
        (5.0 * square - 9.0) * along_y,
        along_z,
        (5.0 * square - 9.0) * along_z,
        3.0 * along_x * along_x - square,
        (3.0 * square - 5.0) * (3.0 * along_x * along_x - square),
        along_y * along_y - along_z * along_z,
        (3.0 * square - 5.0) * (along_y * along_y - along_z * along_z),
        along_x * along_y,
        along_y * along_z,
        along_x * along_z,
        (along_y * along_y - along_z * along_z) * along_x,
        (along_z * along_z - along_x * along_x) * along_y,
        (along_x * along_x - along_y * along_y) * along_z,
    ]
    return np.stack(stacked)


def collide(states, grey_level, solid, classes):
    highest = lax.Precision.HIGHEST
    moments = moment_matrix()
    inverse_moments = moments.T / np.sum(moments * moments, axis=1)
    velocities = jnp.asarray(VELOCITY, jnp.float32)
    weights_col = jnp.asarray(WEIGHTS, jnp.float32)[:, None, None, None]
    density = jnp.sum(states, axis=0)
    velocity_field = jnp.einsum("qd,qxyz->dxyz", velocities, states, precision=highest) / density
    projected = jnp.einsum("qd,dxyz->qxyz", velocities, velocity_field, precision=highest)
    kinetic = jnp.sum(velocity_field * velocity_field, axis=0)
    equilibrium = (
        weights_col
        * density
        * (1.0 + 3.0 * projected + 4.5 * projected * projected - 1.5 * kinetic)
    )
    departure = jnp.einsum(
        "pq,qxyz->pxyz", jnp.asarray(moments, jnp.float32), states - equilibrium, precision=highest
    )
    shear_rate = jnp.where(classes == 0, 1.25, jnp.where(classes == 1, 0.9, 1.7)).astype(
        jnp.float32
    )
    relax_rates = (
        jnp.asarray(BASE_RATES, jnp.float32)[:, None, None, None]
        + jnp.asarray(SHEAR_ROWS, jnp.float32)[:, None, None, None] * shear_rate
    )
    relaxed = states - jnp.einsum(
        "pq,qxyz->pxyz",
        jnp.asarray(inverse_moments, jnp.float32),
        relax_rates * departure,
        precision=highest,
    )
    greyness = jnp.where(solid == 1, jnp.float32(1.0), grey_level)
    return (1.0 - greyness) * relaxed + greyness * jnp.stack([states[int(o)] for o in OPPOSITE])


def extend(states):
    return padded_2(states, (("gx", 1), ("gy", 2)), 1)


def advance(padded, direction_sign):
    width_x = padded.shape[1] - 2
    width_y = padded.shape[2] - 2
    shifted = []
    for direction in range(19):
        offset = [int(direction_sign * component) for component in VELOCITY_LIST[direction]]
        window = padded[
            direction,
            1 - offset[0] : 1 - offset[0] + width_x,
            1 - offset[1] : 1 - offset[1] + width_y,
        ]
        shifted.append(jnp.roll(window, offset[2], axis=2))
    return jnp.stack(shifted)


def body(checkpoint, adjoint_end, resistance, solid_mask, flags):

    def relax_at(states, grey_level):
        return collide(states, grey_level, solid_mask, flags)

    post_start, back_start = jax.vjp(relax_at, checkpoint, resistance)
    middle = advance(extend(post_start), 1)
    _, back_middle = jax.vjp(relax_at, middle, resistance)
    adjoint_middle, sens_middle = back_middle(advance(extend(adjoint_end), -1))
    adjoint_start, sens_start = back_start(advance(extend(adjoint_middle), -1))
    return (adjoint_start, sens_middle + sens_start)


def solution(mesh):
    return jax.shard_map(
        body,
        mesh=mesh,
        in_specs=(
            P(None, "gx", "gy", None),
            P(None, "gx", "gy", None),
            P("gx", "gy", None),
            P("gx", "gy", None),
            P("gx", "gy", None),
        ),
        out_specs=(P(None, "gx", "gy", None), P("gx", "gy", None)),
        check_vma=False,
    )
```

```python
import jax
import jax.numpy as jnp
from jax import lax
from jax.experimental import pallas as pl
from jax.experimental.pallas import tpu as pltpu
from jax.sharding import PartitionSpec as P

VELOCITY = (
    (0, 0, 0),
    (1, 0, 0),
    (-1, 0, 0),
    (0, 1, 0),
    (0, -1, 0),
    (0, 0, 1),
    (0, 0, -1),
    (1, 1, 0),
    (-1, -1, 0),
    (1, -1, 0),
    (-1, 1, 0),
    (1, 0, 1),
    (-1, 0, -1),
    (1, 0, -1),
    (-1, 0, 1),
    (0, 1, 1),
    (0, -1, -1),
    (0, 1, -1),
    (0, -1, 1),
)


def pair_sums(f):
    even = [f[2 * k + 1] + f[2 * k + 2] for k in range(9)]
    odd = [f[2 * k + 1] - f[2 * k + 2] for k in range(9)]
    return even, odd


def grouped(f):
    even, odd = pair_sums(f)
    faces = even[:3]
    planes = [even[7] + even[8], even[5] + even[6], even[3] + even[4]]
    shears = [even[7] - even[8], even[5] - even[6], even[3] - even[4]]
    axes = [
        (odd[0], odd[3] + odd[4], odd[5] + odd[6]),
        (odd[1], odd[3] - odd[4], odd[7] + odd[8]),
        (odd[2], odd[5] - odd[6], odd[7] - odd[8]),
    ]
    return faces, planes, shears, axes, odd


def half_pairs(faces, planes, shears, axes):
    even = [0.5 * v for v in faces]
    for a in (2, 1, 0):
        even += [0.25 * (planes[a] + shears[a]), 0.25 * (planes[a] - shears[a])]
    odd = [0.5 * axes[a][0] for a in range(3)]
    for one, two in ((axes[0][1], axes[1][1]), (axes[0][2], axes[2][1]), (axes[1][2], axes[2][2])):
        odd += [0.25 * (one + two), 0.25 * (one - two)]
    return even, odd


def finish(rest, f, odd_sums, even, odd, grey, free):
    out = [f[0] - free * rest]
    for k in range(9):
        e = free * even[k]
        o = free * odd[k] + grey * odd_sums[k]
        out += [f[2 * k + 1] - (e + o), f[2 * k + 2] - (e - o)]
    return out


def collide_tile(f, grey, rate):
    faces, planes, shears, axes, odd_sums = grouped(f)
    total = faces[0] + faces[1] + faces[2]
    edges = planes[0] + planes[1] + planes[2]
    momentum = [d + a + b for d, a, b in axes]
    inverse = 1.0 / (f[0] + total + edges)
    u = [m * inverse for m in momentum]
    q = [m * v for m, v in zip(momentum, u)]
    q_all = q[0] + q[1] + q[2]
    energy = (1.19 * 19.0 / 2394.0) * (edges - f[0] - q_all)
    square = (1.4 / 252.0) * (9.0 * f[0] - 7.0 * total - 2.0 * edges + 5.5 * q_all)
    rest = 12.0 * square - 30.0 * energy
    d_total = -22.0 * energy - 8.0 * square
    d_edges = 32.0 * energy + 4.0 * square
    d_faces, d_planes = [], []
    for a in range(3):
        x = 3.0 * faces[a] - total
        y = edges - 3.0 * planes[a]
        eq = 3.0 * q[a] - q_all
        stress = rate * (x + y - eq)
        other = 1.4 * (y - 2.0 * x + 0.5 * eq)
        d_faces.append(d_total + (1.0 / 9.0) * (stress - other))
        d_planes.append(d_edges - (1.0 / 9.0) * (2.0 * stress + other))
    d_shears = [
        rate * (shears[0] - momentum[1] * u[2]),
        rate * (shears[1] - momentum[0] * u[2]),
        rate * (shears[2] - momentum[0] * u[1]),
    ]
    d_axes = []
    for d, a, b in axes:
        t = 0.2 * (a + b - 2.0 * d)
        v = 0.99 * (a - b)
        d_axes.append((-2.0 * t, t + v, t - v))
    even, odd = half_pairs(d_faces, d_planes, d_shears, d_axes)
    return finish(rest, f, odd_sums, even, odd, grey, 1.0 - grey)


def adjoint_tile(lam, f, grey, rate):
    f_faces, f_planes, f_shears, f_axes, _ = grouped(f)
    momentum = [d + a + b for d, a, b in f_axes]
    density = f[0] + (f_faces[0] + f_faces[1] + f_faces[2]) + (f_planes[0] + f_planes[1] + f_planes[2])
    inverse = 1.0 / density
    u = [m * inverse for m in momentum]
    faces, planes, shears, axes, odd_sums = grouped(lam)
    total = faces[0] + faces[1] + faces[2]
    edges = planes[0] + planes[1] + planes[2]
    energy = (1.19 / 2394.0) * (8.0 * edges - 11.0 * total - 30.0 * lam[0])
    square = (1.4 / 252.0) * (edges - 4.0 * total + 12.0 * lam[0])
    bulk = 19.0 * energy - 5.5 * square
    weights, w_faces, w_planes, slopes, w_axes = [], [], [], [], []
    w_total = -22.0 * energy - 8.0 * square
    w_edges = 32.0 * energy + 4.0 * square
    for a in range(3):
        x = 3.0 * faces[a] - total
        y = edges - 3.0 * planes[a]
        stress = rate * (x + y)
        other = 1.4 * (y - 2.0 * x)
        w_faces.append(w_total + (1.0 / 9.0) * (stress - other))
        w_planes.append(w_edges - (1.0 / 9.0) * (2.0 * stress + other))
        weights.append(2.0 * bulk + (1.0 / 9.0) * stress - (1.0 / 36.0) * other)
    w_shears = [rate * v for v in shears]
    cross = [0.25 * v for v in w_shears]
    pull = [
        weights[0] * u[0] + cross[2] * u[1] + cross[1] * u[2],
        weights[1] * u[1] + cross[2] * u[0] + cross[0] * u[2],
        weights[2] * u[2] + cross[1] * u[0] + cross[0] * u[1],
    ]
    by_density = 3.0 * square - 11.0 * energy - 0.5 * (u[0] * pull[0] + u[1] * pull[1] + u[2] * pull[2])
    for a in range(3):
        d, p, r = axes[a]
        flux = p + r - 4.0 * d
        v = 0.99 * (p - r)
        slope = pull[a] - 0.02 * flux
        t = 0.12 * flux - 4.0 * slope
        w_axes.append((-0.24 * flux - 2.0 * slope, t + v, t - v))
    rest = 12.0 * square - 30.0 * energy - by_density
    w_faces = [v - 2.0 * by_density for v in w_faces]
    w_planes = [v - 4.0 * by_density for v in w_planes]
    even, odd = half_pairs(w_faces, w_planes, w_shears, w_axes)
    out = finish(rest, lam, odd_sums, even, odd, grey, 1.0 - grey)
    near = rest * f[0]
    far = 0.0
    for a in range(3):
        near += 0.5 * (w_faces[a] * f_faces[a])
        far += w_planes[a] * f_planes[a] + w_shears[a] * f_shears[a]
        (wd, wa, wb), (d, p, r), (ld, lp, lr) = w_axes[a], f_axes[a], axes[a]
        near += (0.5 * wd - ld) * d
        far += (wa - 2.0 * lp) * p + (wb - 2.0 * lr) * r
    return out, near + 0.25 * far


def greyness(resistance, solid):
    return jnp.where(solid == 1, 1.0, resistance)


def shear_rate(flags):
    return jnp.where(flags == 0, 1.25, jnp.where(flags == 1, 0.9, 1.7))


def moving(sign, dim, step):
    return [i for i in range(19) if sign * VELOCITY[i][dim] == step]


def near_plane(field, step, i):
    sign = 1 - 2 * field
    return 19 * field + (moving(sign, 1, 0) + moving(sign, 1, step)).index(i)


def edge_plane(field, step, i):
    return 19 * field + 14 + moving(1 - 2 * field, 1, step).index(i)


def shifted_y(block, step, below, above):
    rows = block.shape[0]
    if step == 0:
        return block
    row = lax.broadcasted_iota(jnp.int32, block.shape, 0)
    if step == 1:
        return jnp.where(row == 0, below, pltpu.roll(block, 1, 0))
    return jnp.where(row == rows - 1, above, pltpu.roll(block, rows - 1, 0))


def shifted_z(block, step):
    return pltpu.roll(block, step % block.shape[1], 1) if step else block


def post_kernel(state, adjoint, resistance, solid, flags, post, up, down):
    nx, ny, nz = resistance.shape
    tiles = ny // 8

    def step(n, carry):
        x, rows = n // tiles, pl.ds(pl.multiple_of(n % tiles * 8, 8), 8)
        for half in range(nz // 128):
            at = (x, rows, pl.ds(half * 128, 128))
            out = collide_tile(
                [state[(i, *at)] for i in range(19)],
                greyness(resistance[at], solid[at]),
                shear_rate(flags[at]),
            )
            for i in range(19):
                post[(i, *at)] = out[i]
        return carry

    lax.fori_loop(0, nx * tiles, step, 0)
    for message, way, last, second in ((up, 1, ny - 1, ny - 2), (down, -1, 0, 1)):
        for field, source in ((0, post), (1, adjoint)):
            sign = 1 - 2 * field
            for i in moving(sign, 1, 0):
                message[near_plane(field, way, i)] = source[i, :, last, :]
            for i in moving(sign, 1, way):
                message[near_plane(field, way, i)] = source[i, :, second, :]
                message[edge_plane(field, way, i)] = source[i, :, last, :]
        message[38] = greyness(resistance[:, last, :], solid[:, last, :])
        message[39] = shear_rate(flags[:, last, :])


def halo_rows(source, below, above, field, i, side):
    step = (1 - 2 * field) * VELOCITY[i][1]
    if side == 0:
        if step == -1:
            return source[i, :, 0, :]
        return below[near_plane(field, 1, i)]
    if step == 1:
        return source[i, :, source.shape[2] - 1, :]
    return above[near_plane(field, -1, i)]


def column(source, below, above, field, i, x):
    step = (1 - 2 * field) * VELOCITY[i][1]
    if step == 0:
        return source[i, x]
    low = below[edge_plane(field, 1, i), pl.ds(x, 1), :] if step == 1 else None
    high = above[edge_plane(field, -1, i), pl.ds(x, 1), :] if step == -1 else None
    return shifted_y(source[i, x], step, low, high)


def pack_kernel(post, adjoint, below, above, right, left):
    nx, ny = post.shape[1:3]
    for message, way, x in ((right, 1, nx - 1), (left, -1, 0)):
        for field, source in ((0, post), (1, adjoint)):
            sign = 1 - 2 * field
            for k, i in enumerate(moving(sign, 0, way)):
                at = 5 * field + k
                message[at] = column(source, below, above, field, i, x)
                for side in range(2):
                    step = sign * VELOCITY[i][1]
                    if (side, step) == (0, -1):
                        line = source[i, x, pl.ds(0, 1), :]
                    elif (side, step) == (1, 1):
                        line = source[i, x, pl.ds(ny - 1, 1), :]
                    else:
                        halo, to = ((below, 1), (above, -1))[side]
                        line = halo[near_plane(field, to, i), pl.ds(x, 1), :]
                    message[10 + side, pl.ds(at, 1), :] = line


def middle_kernel(
    post, adjoint, resistance, solid, flags, below, above, from_left, from_right,
    pulled, sensitivity, right, left, middle, cotangent, out, grey, rate, sens,
):
    nx, ny, nz = resistance.shape
    tiles = ny // 8
    halo = nx * tiles

    for field, source, target in ((0, post, middle), (1, adjoint, cotangent)):
        sign = 1 - 2 * field
        for i in range(19):
            vx, _, vz = (sign * v for v in VELOCITY[i])
            outer = {1: from_left, -1: from_right}.get(vx)
            at = 5 * field + moving(sign, 0, vx).index(i) if vx else None
            for x in range(nx):
                if 0 <= x - vx < nx:
                    block = column(source, below, above, field, i, x - vx)
                else:
                    block = outer[at]
                block = shifted_z(block, vz)
                for t in range(tiles):
                    target[i, x * tiles + t] = block[8 * t : 8 * t + 8]
            for side in range(2):
                rows = halo_rows(source, below, above, field, i, side)
                base = side * nx
                if vx == 0:
                    target[i, halo, base : base + nx, :] = rows
                else:
                    first = 0 if vx == 1 else nx - 1
                    keep = rows[: nx - 1] if vx == 1 else rows[1:]
                    to = base + (1 if vx == 1 else 0)
                    target[i, halo, to : to + nx - 1, :] = keep
                    target[i, halo, base + first : base + first + 1, :] = outer[10 + side, at : at + 1, :]
            if vz:
                target[i, halo] = shifted_z(target[i, halo], vz)
    for x in range(nx):
        for t in range(tiles):
            at = (x, slice(8 * t, 8 * t + 8), slice(None))
            grey[x * tiles + t] = greyness(resistance[at], solid[at])
            rate[x * tiles + t] = shear_rate(flags[at])
    for side, line in enumerate((below, above)):
        grey[halo, side * nx : side * nx + nx, :] = line[38]
        rate[halo, side * nx : side * nx + nx, :] = line[39]

    def step(t, carry):
        for half in range(nz // 128):
            at = (t, slice(None), pl.ds(half * 128, 128))
            new, sens[at] = adjoint_tile(
                [cotangent[(i, *at)] for i in range(19)],
                [middle[(i, *at)] for i in range(19)],
                grey[at],
                rate[at],
            )
            for i in range(19):
                out[(i, *at)] = new[i]
        return carry

    lax.fori_loop(0, halo + 1, step, 0)
    for x in range(nx):
        for t in range(tiles):
            at = (x, slice(8 * t, 8 * t + 8), slice(None))
            sensitivity[at] = jnp.where(solid[at] == 1, 0.0, sens[x * tiles + t])
        for i in range(19):
            vx, vy, vz = (-v for v in VELOCITY[i])
            block = out[i, x * tiles : x * tiles + tiles].reshape(ny, nz)
            block = shifted_y(
                block, vy, out[i, halo, x : x + 1, :], out[i, halo, nx + x : nx + x + 1, :]
            )
            block = shifted_z(block, vz)
            pulled[i, x] = block
            if vx == 1 and x == nx - 1:
                right[moving(-1, 0, 1).index(i)] = block
            if vx == -1 and x == 0:
                left[moving(-1, 0, -1).index(i)] = block


def start_kernel(state, pulled, resistance, solid, flags, partial, from_left, from_right, start, sensitivity):
    nx, ny, nz = resistance.shape

    for x in range(nx):

        def step(t, carry, x=x):
            rows = pl.ds(pl.multiple_of(t * 8, 8), 8)
            for half in range(nz // 128):
                lanes = pl.ds(half * 128, 128)
                at = (x, rows, lanes)
                cotangent = []
                for i in range(19):
                    source = x + VELOCITY[i][0]
                    if source < 0:
                        cotangent.append(from_left[moving(-1, 0, 1).index(i), rows, lanes])
                    elif source == nx:
                        cotangent.append(from_right[moving(-1, 0, -1).index(i), rows, lanes])
                    else:
                        cotangent.append(pulled[i, source, rows, lanes])
                new, sens = adjoint_tile(
                    cotangent,
                    [state[(i, *at)] for i in range(19)],
                    greyness(resistance[at], solid[at]),
                    shear_rate(flags[at]),
                )
                for i in range(19):
                    start[(i, *at)] = new[i]
                sensitivity[at] = partial[at] + jnp.where(solid[at] == 1, 0.0, sens)
            return carry

        lax.fori_loop(0, ny // 8, step, 0)


def call(kernel, outs, *args, scratch=()):
    whole = pl.BlockSpec(memory_space=pltpu.VMEM)
    return pl.pallas_call(
        kernel,
        out_shape=[jax.ShapeDtypeStruct(s, jnp.float32) for s in outs],
        in_specs=[whole] * len(args),
        out_specs=[whole] * len(outs),
        scratch_shapes=[pltpu.VMEM(s, jnp.float32) for s in scratch],
        compiler_params=pltpu.CompilerParams(vmem_limit_bytes=VMEM_LIMIT),
    )(*args)


VMEM_LIMIT = 40 * 1024 * 1024


def exchange(axis, onward, backward):
    count = lax.axis_size(axis)
    ahead = [(i, (i + 1) % count) for i in range(count)]
    behind = [(i, (i - 1) % count) for i in range(count)]
    return lax.ppermute(onward, axis, ahead), lax.ppermute(backward, axis, behind)


def body(checkpoint, adjoint_end, resistance, solid_mask, flags):
    nx, ny, nz = resistance.shape
    whole = checkpoint.shape
    cells = (resistance, solid_mask, flags)
    post, up, down = call(
        post_kernel, [whole, (40, nx, nz), (40, nx, nz)], checkpoint, adjoint_end, *cells
    )
    below, above = exchange("gy", up, down)
    right, left = call(
        pack_kernel, [(12, ny, nz)] * 2, post, adjoint_end, below, above
    )
    from_left, from_right = exchange("gx", right, left)
    tiled = (nx * ny // 8 + 1, 8, nz)
    pulled, partial, right, left = call(
        middle_kernel,
        [whole, (nx, ny, nz), (5, ny, nz), (5, ny, nz)],
        post, adjoint_end, *cells, below, above, from_left, from_right,
        scratch=[(19, *tiled)] * 3 + [tiled] * 3,
    )
    from_left, from_right = exchange("gx", right, left)
    start, sensitivity = call(
        start_kernel,
        [whole, (nx, ny, nz)],
        checkpoint, pulled, *cells, partial, from_left, from_right,
    )
    return start, sensitivity


def solution(mesh):
    state, cell = P(None, "gx", "gy", None), P("gx", "gy", None)
    return jax.shard_map(
        body,
        mesh=mesh,
        in_specs=(state, state, cell, cell, cell),
        out_specs=(state, cell),
        check_vma=False,
    )
```

```python
import jax
import jax.numpy as jnp
from jax import lax
from jax.experimental import pallas as pl
from jax.experimental.pallas import tpu as pltpu
from jax.sharding import PartitionSpec as P

VELOCITY = (
    (0, 0, 0),
    (1, 0, 0),
    (-1, 0, 0),
    (0, 1, 0),
    (0, -1, 0),
    (0, 0, 1),
    (0, 0, -1),
    (1, 1, 0),
    (-1, -1, 0),
    (1, -1, 0),
    (-1, 1, 0),
    (1, 0, 1),
    (-1, 0, -1),
    (1, 0, -1),
    (-1, 0, 1),
    (0, 1, 1),
    (0, -1, -1),
    (0, 1, -1),
    (0, -1, 1),
)


def pair_sums(f):
    even = [f[2 * k + 1] + f[2 * k + 2] for k in range(9)]
    odd = [f[2 * k + 1] - f[2 * k + 2] for k in range(9)]
    return even, odd


def grouped(f):
    even, odd = pair_sums(f)
    faces = even[:3]
    planes = [even[7] + even[8], even[5] + even[6], even[3] + even[4]]
    shears = [even[7] - even[8], even[5] - even[6], even[3] - even[4]]
    axes = [
        (odd[0], odd[3] + odd[4], odd[5] + odd[6]),
        (odd[1], odd[3] - odd[4], odd[7] + odd[8]),
        (odd[2], odd[5] - odd[6], odd[7] - odd[8]),
    ]
    return faces, planes, shears, axes, odd


def half_pairs(faces, planes, shears, axes):
    even = [0.5 * v for v in faces]
    for a in (2, 1, 0):
        even += [0.25 * (planes[a] + shears[a]), 0.25 * (planes[a] - shears[a])]
    odd = [0.5 * axes[a][0] for a in range(3)]
    for one, two in ((axes[0][1], axes[1][1]), (axes[0][2], axes[2][1]), (axes[1][2], axes[2][2])):
        odd += [0.25 * (one + two), 0.25 * (one - two)]
    return even, odd


def finish(rest, f, odd_sums, even, odd, grey, free):
    out = [f[0] - free * rest]
    for k in range(9):
        e = free * even[k]
        o = free * odd[k] + grey * odd_sums[k]
        out += [f[2 * k + 1] - (e + o), f[2 * k + 2] - (e - o)]
    return out


def collide_tile(f, grey, rate):
    faces, planes, shears, axes, odd_sums = grouped(f)
    total = faces[0] + faces[1] + faces[2]
    edges = planes[0] + planes[1] + planes[2]
    momentum = [d + a + b for d, a, b in axes]
    inverse = 1.0 / (f[0] + total + edges)
    u = [m * inverse for m in momentum]
    q = [m * v for m, v in zip(momentum, u)]
    q_all = q[0] + q[1] + q[2]
    energy = (1.19 * 19.0 / 2394.0) * (edges - f[0] - q_all)
    square = (1.4 / 252.0) * (9.0 * f[0] - 7.0 * total - 2.0 * edges + 5.5 * q_all)
    rest = 12.0 * square - 30.0 * energy
    d_total = -22.0 * energy - 8.0 * square
    d_edges = 32.0 * energy + 4.0 * square
    d_faces, d_planes = [], []
    for a in range(3):
        x = 3.0 * faces[a] - total
        y = edges - 3.0 * planes[a]
        eq = 3.0 * q[a] - q_all
        stress = rate * (x + y - eq)
        other = 1.4 * (y - 2.0 * x + 0.5 * eq)
        d_faces.append(d_total + (1.0 / 9.0) * (stress - other))
        d_planes.append(d_edges - (1.0 / 9.0) * (2.0 * stress + other))
    d_shears = [
        rate * (shears[0] - momentum[1] * u[2]),
        rate * (shears[1] - momentum[0] * u[2]),
        rate * (shears[2] - momentum[0] * u[1]),
    ]
    d_axes = []
    for d, a, b in axes:
        t = 0.2 * (a + b - 2.0 * d)
        v = 0.99 * (a - b)
        d_axes.append((-2.0 * t, t + v, t - v))
    even, odd = half_pairs(d_faces, d_planes, d_shears, d_axes)
    return finish(rest, f, odd_sums, even, odd, grey, 1.0 - grey)


def adjoint_tile(lam, f, grey, rate):
    f_faces, f_planes, f_shears, f_axes, _ = grouped(f)
    momentum = [d + a + b for d, a, b in f_axes]
    density = f[0] + (f_faces[0] + f_faces[1] + f_faces[2]) + (f_planes[0] + f_planes[1] + f_planes[2])
    inverse = 1.0 / density
    u = [m * inverse for m in momentum]
    faces, planes, shears, axes, odd_sums = grouped(lam)
    total = faces[0] + faces[1] + faces[2]
    edges = planes[0] + planes[1] + planes[2]
    energy = (1.19 / 2394.0) * (8.0 * edges - 11.0 * total - 30.0 * lam[0])
    square = (1.4 / 252.0) * (edges - 4.0 * total + 12.0 * lam[0])
    bulk = 19.0 * energy - 5.5 * square
    weights, w_faces, w_planes, slopes, w_axes = [], [], [], [], []
    w_total = -22.0 * energy - 8.0 * square
    w_edges = 32.0 * energy + 4.0 * square
    for a in range(3):
        x = 3.0 * faces[a] - total
        y = edges - 3.0 * planes[a]
        stress = rate * (x + y)
        other = 1.4 * (y - 2.0 * x)
        w_faces.append(w_total + (1.0 / 9.0) * (stress - other))
        w_planes.append(w_edges - (1.0 / 9.0) * (2.0 * stress + other))
        weights.append(2.0 * bulk + (1.0 / 9.0) * stress - (1.0 / 36.0) * other)
    w_shears = [rate * v for v in shears]
    cross = [0.25 * v for v in w_shears]
    pull = [
        weights[0] * u[0] + cross[2] * u[1] + cross[1] * u[2],
        weights[1] * u[1] + cross[2] * u[0] + cross[0] * u[2],
        weights[2] * u[2] + cross[1] * u[0] + cross[0] * u[1],
    ]
    by_density = 3.0 * square - 11.0 * energy - 0.5 * (u[0] * pull[0] + u[1] * pull[1] + u[2] * pull[2])
    for a in range(3):
        d, p, r = axes[a]
        flux = p + r - 4.0 * d
        v = 0.99 * (p - r)
        slope = pull[a] - 0.02 * flux
        t = 0.12 * flux - 4.0 * slope
        w_axes.append((-0.24 * flux - 2.0 * slope, t + v, t - v))
    rest = 12.0 * square - 30.0 * energy - by_density
    w_faces = [v - 2.0 * by_density for v in w_faces]
    w_planes = [v - 4.0 * by_density for v in w_planes]
    even, odd = half_pairs(w_faces, w_planes, w_shears, w_axes)
    out = finish(rest, lam, odd_sums, even, odd, grey, 1.0 - grey)
    near = rest * f[0]
    far = 0.0
    for a in range(3):
        near += 0.5 * (w_faces[a] * f_faces[a])
        far += w_planes[a] * f_planes[a] + w_shears[a] * f_shears[a]
        (wd, wa, wb), (d, p, r), (ld, lp, lr) = w_axes[a], f_axes[a], axes[a]
        near += (0.5 * wd - ld) * d
        far += (wa - 2.0 * lp) * p + (wb - 2.0 * lr) * r
    return out, near + 0.25 * far


def greyness(resistance, solid):
    return jnp.where(solid == 1, 1.0, resistance)


def shear_rate(flags):
    return jnp.where(flags == 0, 1.25, jnp.where(flags == 1, 0.9, 1.7))


def moving(sign, dim, step):
    return [i for i in range(19) if sign * VELOCITY[i][dim] == step]


def near_plane(field, step, i):
    sign = 1 - 2 * field
    return 19 * field + (moving(sign, 1, 0) + moving(sign, 1, step)).index(i)


def edge_plane(field, step, i):
    return 19 * field + 14 + moving(1 - 2 * field, 1, step).index(i)


def shifted_y(block, step, below, above):
    rows = block.shape[0]
    if step == 0:
        return block
    row = lax.broadcasted_iota(jnp.int32, block.shape, 0)
    if step == 1:
        return jnp.where(row == 0, below, pltpu.roll(block, 1, 0))
    return jnp.where(row == rows - 1, above, pltpu.roll(block, rows - 1, 0))


def shifted_z(block, step):
    return pltpu.roll(block, step % block.shape[1], 1) if step else block


def post_kernel(
    far_state, far_adjoint, far_resistance, far_solid, far_flags, post, up, down,
    state, adjoint, resistance, solid, flags, done,
):
    nx, ny, nz = resistance.shape
    tiles = ny // 8
    cells = ((far_resistance, resistance), (far_solid, solid), (far_flags, flags))
    copies = [pltpu.make_async_copy(*pair, done.at[k]) for k, pair in enumerate(cells)]
    for x in range(nx):
        copies.append(pltpu.make_async_copy(far_state.at[:, x], state.at[:, x], done.at[3 + x]))
    copies.append(pltpu.make_async_copy(far_adjoint, adjoint, done.at[3 + nx]))
    for copy in copies:
        copy.start()
    for copy in copies[:3]:
        copy.wait()

    for x in range(nx):
        copies[3 + x].wait()

        def step(t, carry, x=x):
            rows = pl.ds(pl.multiple_of(t * 8, 8), 8)
            for half in range(nz // 128):
                at = (x, rows, pl.ds(half * 128, 128))
                out = collide_tile(
                    [state[(i, *at)] for i in range(19)],
                    greyness(resistance[at], solid[at]),
                    shear_rate(flags[at]),
                )
                for i in range(19):
                    post[(i, *at)] = out[i]
            return carry

        lax.fori_loop(0, tiles, step, 0)
    copies[3 + nx].wait()
    for message, way, last, second in ((up, 1, ny - 1, ny - 2), (down, -1, 0, 1)):
        for field, source in ((0, post), (1, adjoint)):
            sign = 1 - 2 * field
            for i in moving(sign, 1, 0):
                message[near_plane(field, way, i)] = source[i, :, last, :]
            for i in moving(sign, 1, way):
                message[near_plane(field, way, i)] = source[i, :, second, :]
                message[edge_plane(field, way, i)] = source[i, :, last, :]
        message[38] = greyness(resistance[:, last, :], solid[:, last, :])
        message[39] = shear_rate(flags[:, last, :])


def halo_rows(source, below, above, field, i, side):
    step = (1 - 2 * field) * VELOCITY[i][1]
    if side == 0:
        if step == -1:
            return source[i, :, 0, :]
        return below[near_plane(field, 1, i)]
    if step == 1:
        return source[i, :, source.shape[2] - 1, :]
    return above[near_plane(field, -1, i)]


def column(source, below, above, field, i, x):
    step = (1 - 2 * field) * VELOCITY[i][1]
    if step == 0:
        return source[i, x]
    low = below[edge_plane(field, 1, i), pl.ds(x, 1), :] if step == 1 else None
    high = above[edge_plane(field, -1, i), pl.ds(x, 1), :] if step == -1 else None
    return shifted_y(source[i, x], step, low, high)


def pack_kernel(post, adjoint, below, above, right, left):
    nx, ny = post.shape[1:3]
    for message, way, x in ((right, 1, nx - 1), (left, -1, 0)):
        for field, source in ((0, post), (1, adjoint)):
            sign = 1 - 2 * field
            for k, i in enumerate(moving(sign, 0, way)):
                at = 5 * field + k
                message[at] = column(source, below, above, field, i, x)
                for side in range(2):
                    step = sign * VELOCITY[i][1]
                    if (side, step) == (0, -1):
                        line = source[i, x, pl.ds(0, 1), :]
                    elif (side, step) == (1, 1):
                        line = source[i, x, pl.ds(ny - 1, 1), :]
                    else:
                        halo, to = ((below, 1), (above, -1))[side]
                        line = halo[near_plane(field, to, i), pl.ds(x, 1), :]
                    message[10 + side, pl.ds(at, 1), :] = line


def middle_kernel(
    post, adjoint, resistance, solid, flags, below, above, from_left, from_right,
    pulled, sensitivity, right, left, middle, cotangent, out, grey, rate, sens,
):
    nx, ny, nz = resistance.shape
    tiles = ny // 8
    halo = nx * tiles

    for field, source, target in ((0, post, middle), (1, adjoint, cotangent)):
        sign = 1 - 2 * field
        for i in range(19):
            vx, _, vz = (sign * v for v in VELOCITY[i])
            outer = {1: from_left, -1: from_right}.get(vx)
            at = 5 * field + moving(sign, 0, vx).index(i) if vx else None
            for x in range(nx):
                if 0 <= x - vx < nx:
                    block = column(source, below, above, field, i, x - vx)
                else:
                    block = outer[at]
                block = shifted_z(block, vz)
                for t in range(tiles):
                    target[i, x * tiles + t] = block[8 * t : 8 * t + 8]
            for side in range(2):
                rows = halo_rows(source, below, above, field, i, side)
                base = side * nx
                if vx == 0:
                    target[i, halo, base : base + nx, :] = rows
                else:
                    first = 0 if vx == 1 else nx - 1
                    keep = rows[: nx - 1] if vx == 1 else rows[1:]
                    to = base + (1 if vx == 1 else 0)
                    target[i, halo, to : to + nx - 1, :] = keep
                    target[i, halo, base + first : base + first + 1, :] = outer[10 + side, at : at + 1, :]
            if vz:
                target[i, halo] = shifted_z(target[i, halo], vz)
    for x in range(nx):
        for t in range(tiles):
            at = (x, slice(8 * t, 8 * t + 8), slice(None))
            grey[x * tiles + t] = greyness(resistance[at], solid[at])
            rate[x * tiles + t] = shear_rate(flags[at])
    for side, line in enumerate((below, above)):
        grey[halo, side * nx : side * nx + nx, :] = line[38]
        rate[halo, side * nx : side * nx + nx, :] = line[39]

    def step(t, carry):
        for half in range(nz // 128):
            at = (t, slice(None), pl.ds(half * 128, 128))
            new, sens[at] = adjoint_tile(
                [cotangent[(i, *at)] for i in range(19)],
                [middle[(i, *at)] for i in range(19)],
                grey[at],
                rate[at],
            )
            for i in range(19):
                out[(i, *at)] = new[i]
        return carry

    lax.fori_loop(0, halo + 1, step, 0)
    for x in range(nx):
        for t in range(tiles):
            at = (x, slice(8 * t, 8 * t + 8), slice(None))
            sensitivity[at] = jnp.where(solid[at] == 1, 0.0, sens[x * tiles + t])
        for i in range(19):
            vx, vy, vz = (-v for v in VELOCITY[i])
            block = out[i, x * tiles : x * tiles + tiles].reshape(ny, nz)
            block = shifted_y(
                block, vy, out[i, halo, x : x + 1, :], out[i, halo, nx + x : nx + x + 1, :]
            )
            block = shifted_z(block, vz)
            pulled[i, x] = block
            if vx == 1 and x == nx - 1:
                right[moving(-1, 0, 1).index(i)] = block
            if vx == -1 and x == 0:
                left[moving(-1, 0, -1).index(i)] = block


def start_kernel(state, pulled, resistance, solid, flags, partial, from_left, from_right, start, sensitivity):
    nx, ny, nz = resistance.shape

    for x in range(nx):

        def step(t, carry, x=x):
            rows = pl.ds(pl.multiple_of(t * 8, 8), 8)
            for half in range(nz // 128):
                lanes = pl.ds(half * 128, 128)
                at = (x, rows, lanes)
                cotangent = []
                for i in range(19):
                    source = x + VELOCITY[i][0]
                    if source < 0:
                        cotangent.append(from_left[moving(-1, 0, 1).index(i), rows, lanes])
                    elif source == nx:
                        cotangent.append(from_right[moving(-1, 0, -1).index(i), rows, lanes])
                    else:
                        cotangent.append(pulled[i, source, rows, lanes])
                new, sens = adjoint_tile(
                    cotangent,
                    [state[(i, *at)] for i in range(19)],
                    greyness(resistance[at], solid[at]),
                    shear_rate(flags[at]),
                )
                for i in range(19):
                    start[(i, *at)] = new[i]
                sensitivity[at] = partial[at] + jnp.where(solid[at] == 1, 0.0, sens)
            return carry

        lax.fori_loop(0, ny // 8, step, 0)


def call(kernel, outs, *args, scratch=(), far=0):
    whole = pl.BlockSpec(memory_space=pltpu.VMEM)
    return pl.pallas_call(
        kernel,
        out_shape=[jax.ShapeDtypeStruct(s, jnp.float32) for s in outs],
        in_specs=[pl.BlockSpec(memory_space=pltpu.HBM)] * far + [whole] * (len(args) - far),
        out_specs=[whole] * len(outs),
        scratch_shapes=[pltpu.VMEM(s, jnp.float32) if isinstance(s, tuple) else s for s in scratch],
        compiler_params=pltpu.CompilerParams(vmem_limit_bytes=VMEM_LIMIT),
    )(*args)


VMEM_LIMIT = 40 * 1024 * 1024


def exchange(axis, onward, backward):
    count = lax.axis_size(axis)
    ahead = [(i, (i + 1) % count) for i in range(count)]
    behind = [(i, (i - 1) % count) for i in range(count)]
    return lax.ppermute(onward, axis, ahead), lax.ppermute(backward, axis, behind)


def body(checkpoint, adjoint_end, resistance, solid_mask, flags):
    nx, ny, nz = resistance.shape
    whole = checkpoint.shape
    cells = (resistance, solid_mask, flags)
    post, up, down = call(
        post_kernel, [whole, (40, nx, nz), (40, nx, nz)],
        *(pltpu.with_memory_space_constraint(v, pltpu.HBM) for v in (checkpoint, adjoint_end, *cells)), far=5,
        scratch=[whole, whole, (nx, ny, nz), *[pltpu.VMEM((nx, ny, nz), jnp.int32)] * 2, pltpu.SemaphoreType.DMA((nx + 4,))],
    )
    below, above = exchange("gy", up, down)
    right, left = call(
        pack_kernel, [(12, ny, nz)] * 2, post, adjoint_end, below, above
    )
    from_left, from_right = exchange("gx", right, left)
    tiled = (nx * ny // 8 + 1, 8, nz)
    pulled, partial, right, left = call(
        middle_kernel,
        [whole, (nx, ny, nz), (5, ny, nz), (5, ny, nz)],
        post, adjoint_end, *cells, below, above, from_left, from_right,
        scratch=[(19, *tiled)] * 3 + [tiled] * 3,
    )
    from_left, from_right = exchange("gx", right, left)
    start, sensitivity = call(
        start_kernel,
        [whole, (nx, ny, nz)],
        checkpoint, pulled, *cells, partial, from_left, from_right,
    )
    return start, sensitivity


def solution(mesh):
    state, cell = P(None, "gx", "gy", None), P("gx", "gy", None)
    return jax.shard_map(
        body,
        mesh=mesh,
        in_specs=(state, state, cell, cell, cell),
        out_specs=(state, cell),
        check_vma=False,
    )
```

```python
import jax
import jax.numpy as jnp
from jax import lax
from jax.experimental import pallas as pl
from jax.experimental.pallas import tpu as pltpu
from jax.sharding import PartitionSpec as P

VELOCITY = (
    (0, 0, 0),
    (1, 0, 0),
    (-1, 0, 0),
    (0, 1, 0),
    (0, -1, 0),
    (0, 0, 1),
    (0, 0, -1),
    (1, 1, 0),
    (-1, -1, 0),
    (1, -1, 0),
    (-1, 1, 0),
    (1, 0, 1),
    (-1, 0, -1),
    (1, 0, -1),
    (-1, 0, 1),
    (0, 1, 1),
    (0, -1, -1),
    (0, 1, -1),
    (0, -1, 1),
)


def pair_sums(f):
    even = [f[2 * k + 1] + f[2 * k + 2] for k in range(9)]
    odd = [f[2 * k + 1] - f[2 * k + 2] for k in range(9)]
    return even, odd


def grouped(f):
    even, odd = pair_sums(f)
    faces = even[:3]
    planes = [even[7] + even[8], even[5] + even[6], even[3] + even[4]]
    shears = [even[7] - even[8], even[5] - even[6], even[3] - even[4]]
    axes = [
        (odd[0], odd[3] + odd[4], odd[5] + odd[6]),
        (odd[1], odd[3] - odd[4], odd[7] + odd[8]),
        (odd[2], odd[5] - odd[6], odd[7] - odd[8]),
    ]
    return faces, planes, shears, axes, odd


def half_pairs(faces, planes, shears, axes):
    even = [0.5 * v for v in faces]
    for a in (2, 1, 0):
        even += [0.25 * (planes[a] + shears[a]), 0.25 * (planes[a] - shears[a])]
    odd = [0.5 * axes[a][0] for a in range(3)]
    for one, two in ((axes[0][1], axes[1][1]), (axes[0][2], axes[2][1]), (axes[1][2], axes[2][2])):
        odd += [0.25 * (one + two), 0.25 * (one - two)]
    return even, odd


def finish(rest, f, odd_sums, even, odd, grey, free):
    out = [f[0] - free * rest]
    for k in range(9):
        e = free * even[k]
        o = free * odd[k] + grey * odd_sums[k]
        out += [f[2 * k + 1] - (e + o), f[2 * k + 2] - (e - o)]
    return out


def collide_tile(f, grey, rate):
    faces, planes, shears, axes, odd_sums = grouped(f)
    total = faces[0] + faces[1] + faces[2]
    edges = planes[0] + planes[1] + planes[2]
    momentum = [d + a + b for d, a, b in axes]
    inverse = 1.0 / (f[0] + total + edges)
    u = [m * inverse for m in momentum]
    q = [m * v for m, v in zip(momentum, u)]
    q_all = q[0] + q[1] + q[2]
    energy = (1.19 * 19.0 / 2394.0) * (edges - f[0] - q_all)
    square = (1.4 / 252.0) * (9.0 * f[0] - 7.0 * total - 2.0 * edges + 5.5 * q_all)
    rest = 12.0 * square - 30.0 * energy
    d_total = -22.0 * energy - 8.0 * square
    d_edges = 32.0 * energy + 4.0 * square
    d_faces, d_planes = [], []
    for a in range(3):
        x = 3.0 * faces[a] - total
        y = edges - 3.0 * planes[a]
        eq = 3.0 * q[a] - q_all
        stress = rate * (x + y - eq)
        other = 1.4 * (y - 2.0 * x + 0.5 * eq)
        d_faces.append(d_total + (1.0 / 9.0) * (stress - other))
        d_planes.append(d_edges - (1.0 / 9.0) * (2.0 * stress + other))
    d_shears = [
        rate * (shears[0] - momentum[1] * u[2]),
        rate * (shears[1] - momentum[0] * u[2]),
        rate * (shears[2] - momentum[0] * u[1]),
    ]
    d_axes = []
    for d, a, b in axes:
        t = 0.2 * (a + b - 2.0 * d)
        v = 0.99 * (a - b)
        d_axes.append((-2.0 * t, t + v, t - v))
    even, odd = half_pairs(d_faces, d_planes, d_shears, d_axes)
    return finish(rest, f, odd_sums, even, odd, grey, 1.0 - grey)


def adjoint_at(lam, density, momentum, grey, rate):
    inverse = 1.0 / density
    u = [m * inverse for m in momentum]
    faces, planes, shears, axes, odd_sums = grouped(lam)
    total = faces[0] + faces[1] + faces[2]
    edges = planes[0] + planes[1] + planes[2]
    energy = (1.19 / 2394.0) * (8.0 * edges - 11.0 * total - 30.0 * lam[0])
    square = (1.4 / 252.0) * (edges - 4.0 * total + 12.0 * lam[0])
    bulk = 19.0 * energy - 5.5 * square
    weights, w_faces, w_planes, slopes, w_axes = [], [], [], [], []
    w_total = -22.0 * energy - 8.0 * square
    w_edges = 32.0 * energy + 4.0 * square
    for a in range(3):
        x = 3.0 * faces[a] - total
        y = edges - 3.0 * planes[a]
        stress = rate * (x + y)
        other = 1.4 * (y - 2.0 * x)
        w_faces.append(w_total + (1.0 / 9.0) * (stress - other))
        w_planes.append(w_edges - (1.0 / 9.0) * (2.0 * stress + other))
        weights.append(2.0 * bulk + (1.0 / 9.0) * stress - (1.0 / 36.0) * other)
    w_shears = [rate * v for v in shears]
    cross = [0.25 * v for v in w_shears]
    pull = [
        weights[0] * u[0] + cross[2] * u[1] + cross[1] * u[2],
        weights[1] * u[1] + cross[2] * u[0] + cross[0] * u[2],
        weights[2] * u[2] + cross[1] * u[0] + cross[0] * u[1],
    ]
    by_density = 3.0 * square - 11.0 * energy - 0.5 * (u[0] * pull[0] + u[1] * pull[1] + u[2] * pull[2])
    for a in range(3):
        d, p, r = axes[a]
        flux = p + r - 4.0 * d
        v = 0.99 * (p - r)
        slope = pull[a] - 0.02 * flux
        t = 0.12 * flux - 4.0 * slope
        w_axes.append((-0.24 * flux - 2.0 * slope, t + v, t - v))
    rest = 12.0 * square - 30.0 * energy - by_density
    w_faces = [v - 2.0 * by_density for v in w_faces]
    w_planes = [v - 4.0 * by_density for v in w_planes]
    even, odd = half_pairs(w_faces, w_planes, w_shears, w_axes)
    out = finish(rest, lam, odd_sums, even, odd, grey, 1.0 - grey)
    for a in range(3):
        (wd, wa, wb), (ld, lp, lr) = w_axes[a], axes[a]
        w_axes[a] = (wd - 2.0 * ld, wa - 2.0 * lp, wb - 2.0 * lr)
    return out, (rest, w_faces, w_planes, w_shears, w_axes)


def adjoint_tile(lam, f, grey, rate):
    faces, planes, shears, axes, _ = grouped(f)
    momentum = [d + a + b for d, a, b in axes]
    density = f[0] + (faces[0] + faces[1] + faces[2]) + (planes[0] + planes[1] + planes[2])
    out, (rest, w_faces, w_planes, w_shears, w_axes) = adjoint_at(lam, density, momentum, grey, rate)
    near, far = 0.0, 0.0
    for a in range(3):
        (wd, wa, wb), (d, p, r) = w_axes[a], axes[a]
        near = near + w_faces[a] * faces[a] + wd * d
        far = far + w_planes[a] * planes[a] + w_shears[a] * shears[a] + wa * p + wb * r
    return out, rest * f[0] + 0.5 * near + 0.25 * far


def greyness(resistance, solid):
    return jnp.where(solid == 1, 1.0, resistance)


def shear_rate(flags):
    return jnp.where(flags == 0, 1.25, jnp.where(flags == 1, 0.9, 1.7))


def moving(sign, dim, step):
    return [i for i in range(19) if sign * VELOCITY[i][dim] == step]


NEAR, FAR_EDGE, GREY, RATE = 9, 23, 28, 29


def edge_plane(field, way, i):
    return (4, FAR_EDGE)[field] + moving(1 - 2 * field, 1, way).index(i)


def near_plane(way, i):
    return NEAR + (moving(-1, 1, 0) + moving(-1, 1, way)).index(i)


def x_plane(field, i):
    return 5 * field + moving(1 - 2 * field, 0, (1 - 2 * field) * VELOCITY[i][0]).index(i)


def velocity(field, i):
    return tuple((1 - 2 * field) * v for v in VELOCITY[i])


def rolled_y(block, step):
    return pltpu.roll(block, step % block.shape[0], 0) if step else block


def shifted_y(block, step, below, above):
    if step == 0:
        return block
    row = lax.broadcasted_iota(jnp.int32, block.shape, 0)
    if step == 1:
        return jnp.where(row == 0, below, rolled_y(block, 1))
    return jnp.where(row == block.shape[0] - 1, above, rolled_y(block, -1))


def shifted_z(block, step):
    return pltpu.roll(block, step % block.shape[1], 1) if step else block


def face_kernel(
    far_state, far_adjoint, far_resistance, far_solid, far_flags, right, left,
    state, resistance, solid, flags, done,
):
    nx, ny, nz = far_resistance.shape
    sides = ((right, 1, nx - 1), (left, -1, 0))
    copies, first = [], []
    for side, (message, way, x) in enumerate(sides):
        pairs = [
            (far_state.at[:, x], state.at[side]),
            (far_resistance.at[x], resistance.at[side]),
            (far_solid.at[x], solid.at[side]),
            (far_flags.at[x], flags.at[side]),
        ]
        pairs += [(far_adjoint.at[i, x], message.at[x_plane(1, i)]) for i in moving(-1, 0, way)]
        first.append(len(copies))
        for source, target in pairs:
            copies.append(pltpu.make_async_copy(source, target, done.at[len(copies)]))
    for copy in copies:
        copy.start()
    for side, (message, way, _) in enumerate(sides):
        for copy in copies[first[side] : first[side] + 4]:
            copy.wait()

        def step(t, carry, side=side, message=message, way=way):
            rows = pl.ds(pl.multiple_of(t * 8, 8), 8)
            for half in range(nz // 128):
                at = (rows, pl.ds(half * 128, 128))
                out = collide_tile(
                    [state[(side, i, *at)] for i in range(19)],
                    greyness(resistance[(side, *at)], solid[(side, *at)]),
                    shear_rate(flags[(side, *at)]),
                )
                for i in moving(1, 0, way):
                    message[(x_plane(0, i), *at)] = out[i]
            return carry

        lax.fori_loop(0, ny // 8, step, 0)
    for side in range(2):
        for copy in copies[first[side] + 4 : first[side] + 9]:
            copy.wait()


def post_kernel(state, resistance, solid, flags, post):
    nx, ny, nz = resistance.shape
    tiles = ny // 8

    def step(n, carry):
        x, rows = n // tiles, pl.ds(pl.multiple_of(n % tiles * 8, 8), 8)
        for half in range(nz // 128):
            at = (x, rows, pl.ds(half * 128, 128))
            out = collide_tile(
                [state[(i, *at)] for i in range(19)],
                greyness(resistance[at], solid[at]),
                shear_rate(flags[at]),
            )
            for i in range(19):
                post[(i, *at)] = out[i]
        return carry

    lax.fori_loop(0, nx * tiles, step, 0)


def rim_kernel(post, adjoint, resistance, solid, flags, from_left, from_right, up, down, work):
    nx, ny, nz = resistance.shape
    shares = {1: [0.0] * 4, -1: [0.0] * 4}
    for field, source in ((0, post), (1, adjoint)):
        for i in range(19):
            vx, vy, vz = velocity(field, i)
            picks = {0: (ny - 1, 0), 1: (ny - 2, ny - 1), -1: (1, 0)}[vy]
            tile = work.at[19 * field + i]
            for half, row in enumerate(picks):
                base = half * nx
                if vx == 0:
                    tile[base : base + nx, :] = source[i, :, row, :]
                    continue
                outer = from_left if vx == 1 else from_right
                edge = outer[x_plane(field, i), pl.ds(row, 1), :]
                lines = source[i, :, row, :]
                if vx == 1:
                    tile[base + 1 : base + nx, :] = lines[: nx - 1]
                    tile[base : base + 1, :] = edge
                else:
                    tile[base : base + nx - 1, :] = lines[1:]
                    tile[base + nx - 1 : base + nx, :] = edge
            if vz:
                tile[...] = shifted_z(tile[...], vz)
            for half in range(2):
                value = tile[half * nx : half * nx + nx, :]
                way = vy if vy else 1 - 2 * half
                message = up if way == 1 else down
                if vy and half == 1:
                    message[edge_plane(field, way, i)] = value
                elif field == 1:
                    message[near_plane(way, i)] = value
                else:
                    share = shares[way]
                    for k, factor in enumerate((1, vx, vy, vz)):
                        if factor:
                            share[k] = share[k] + factor * value
    for way, message, row in ((1, up, ny - 1), (-1, down, 0)):
        for k in range(4):
            message[k] = shares[way][k]
        message[GREY] = greyness(resistance[:, row, :], solid[:, row, :])
        message[RATE] = shear_rate(flags[:, row, :])


def middle_kernel(
    post, adjoint, resistance, solid, flags, from_left, from_right,
    out, sensitivity, rim_middle, rim_cotangent, middle, cotangent,
):
    nx, ny, nz = resistance.shape
    tiles = ny // 8
    for field, source, target, rim in (
        (0, post, middle, rim_middle),
        (1, adjoint, cotangent, rim_cotangent),
    ):
        for i in range(19):
            vx, vy, vz = velocity(field, i)
            for x in range(nx):
                if 0 <= x - vx < nx:
                    block = source[i, x - vx]
                else:
                    block = (from_left if vx == 1 else from_right)[x_plane(field, i)]
                block = rolled_y(shifted_z(block, vz), vy)
                target[i, x] = block
                rim[i, x : x + 1, :] = block[:1]
                rim[i, nx + x : nx + x + 1, :] = block[ny - 1 :]

    def step(n, carry):
        x, rows = n // tiles, pl.ds(pl.multiple_of(n % tiles * 8, 8), 8)
        for half in range(nz // 128):
            at = (x, rows, pl.ds(half * 128, 128))
            state = [middle[(i, *at)] for i in range(19)]
            new, sens = adjoint_tile(
                [cotangent[(i, *at)] for i in range(19)],
                state,
                greyness(resistance[at], solid[at]),
                shear_rate(flags[at]),
            )
            sensitivity[at] = jnp.where(solid[at] == 1, 0.0, sens)
            for i in range(19):
                out[(i, *at)] = new[i]
        return carry

    lax.fori_loop(0, nx * tiles, step, 0)


def pulled_block(out, outer_rows, halo_rows, i, x):
    nx, ny = out.shape[1:3]
    _, vy, vz = velocity(1, i)
    block = out[i, x]
    row = lax.broadcasted_iota(jnp.int32, block.shape, 0)
    block = jnp.where(row == 0, outer_rows[i, pl.ds(x, 1), :], block)
    block = jnp.where(row == ny - 1, outer_rows[i, pl.ds(nx + x, 1), :], block)
    low = halo_rows[i, pl.ds(x, 1), :] if vy == 1 else None
    high = halo_rows[i, pl.ds(nx + x, 1), :] if vy == -1 else None
    return shifted_z(shifted_y(block, vy, low, high), vz)


def edge_kernel(
    out, resistance, solid, flags, rim_middle, rim_cotangent, up, down, below, above,
    outer_rows, halo_rows, outer_sens, right, left, middle, cotangent, halo, cells,
):
    nx, ny, nz = resistance.shape
    low, high = slice(0, nx), slice(nx, 2 * nx)
    for field, rim, target in ((0, rim_middle, middle), (1, rim_cotangent, cotangent)):
        for i in range(19):
            vy = velocity(field, i)[1]
            target[i] = rim[i]
            if vy == 1:
                target[i, low, :] = below[edge_plane(field, 1, i)]
            if vy == -1:
                target[i, high, :] = above[edge_plane(field, -1, i)]
    for i in range(19):
        vy = velocity(1, i)[1]
        halo[i, low, :] = down[edge_plane(1, -1, i)] if vy == -1 else below[near_plane(1, i)]
        halo[i, high, :] = up[edge_plane(1, 1, i)] if vy == 1 else above[near_plane(-1, i)]
    for rows, way, received, sent in ((low, -1, below, down), (high, 1, above, up)):
        share = [received[k] for k in range(4)]
        for i in moving(1, 1, way):
            value = sent[edge_plane(0, way, i)]
            for k, factor in enumerate((1, *VELOCITY[i])):
                if factor:
                    share[k] = share[k] + factor * value
        for k in range(4):
            cells[k, rows, :] = share[k]
        cells[4, rows, :] = received[GREY]
        cells[5, rows, :] = received[RATE]
        row = 0 if way == -1 else ny - 1
        blocked = solid[:, row, :]
        cells[6, rows, :] = greyness(resistance[:, row, :], blocked)
        cells[7, rows, :] = shear_rate(flags[:, row, :])
        cells[8, rows, :] = jnp.where(blocked == 1, 0.0, 1.0)
    for part in range(nz // 128):
        at = (slice(None), pl.ds(part * 128, 128))
        state = [middle[(i, *at)] for i in range(19)]
        new, sens = adjoint_tile(
            [cotangent[(i, *at)] for i in range(19)], state, cells[(6, *at)], cells[(7, *at)]
        )
        outer_sens[at] = jnp.where(cells[(8, *at)] == 0.0, 0.0, sens)
        for i in range(19):
            outer_rows[(i, *at)] = new[i]
        lam = [halo[(i, *at)] for i in range(19)]
        density, *momentum = [cells[(k, *at)] for k in range(4)]
        new, _ = adjoint_at(lam, density, momentum, cells[(4, *at)], cells[(5, *at)])
        for i in range(19):
            halo_rows[(i, *at)] = new[i]
    for message, way, x in ((right, 1, nx - 1), (left, -1, 0)):
        for k, i in enumerate(moving(-1, 0, way)):
            message[k] = pulled_block(out, outer_rows, halo_rows, i, x)


def start_columns(columns, state, pulled, resistance, solid, flags, partial, from_left, from_right, start, total):
    nx, ny, nz = resistance.shape
    for slot, x in enumerate(columns):

        def step(t, carry, x=x, slot=slot):
            rows = pl.ds(pl.multiple_of(t * 8, 8), 8)
            for half in range(nz // 128):
                lanes = pl.ds(half * 128, 128)
                at = (x, rows, lanes)
                cotangent = []
                for i in range(19):
                    source = x + VELOCITY[i][0]
                    if source < 0:
                        cotangent.append(from_left[moving(-1, 0, 1).index(i), rows, lanes])
                    elif source == nx:
                        cotangent.append(from_right[moving(-1, 0, -1).index(i), rows, lanes])
                    else:
                        cotangent.append(pulled[i, source, rows, lanes])
                new, sens = adjoint_tile(
                    cotangent,
                    [state[(i, *at)] for i in range(19)],
                    greyness(resistance[at], solid[at]),
                    shear_rate(flags[at]),
                )
                for i in range(19):
                    start[slot, i, rows, lanes] = new[i]
                total[at] = partial[at] + jnp.where(solid[at] == 1, 0.0, sens)
            return carry

        lax.fori_loop(0, ny // 8, step, 0)
        yield slot, x


def inner_kernel(
    out, outer_rows, halo_rows, sens, outer_sens, state, resistance, solid, flags,
    far_start, pulled, partial, start, done,
):
    nx, ny = resistance.shape[:2]
    for x in range(nx):
        for i in range(19):
            pulled[i, x] = pulled_block(out, outer_rows, halo_rows, i, x)
        block = sens[x]
        row = lax.broadcasted_iota(jnp.int32, block.shape, 0)
        block = jnp.where(row == 0, outer_sens[pl.ds(x, 1), :], block)
        partial[x] = jnp.where(row == ny - 1, outer_sens[pl.ds(nx + x, 1), :], block)
    copies = []
    for slot, x in start_columns(
        range(1, nx - 1), state, pulled, resistance, solid, flags, partial, None, None, start, partial
    ):
        copies.append(pltpu.make_async_copy(start.at[slot], far_start.at[:, x], done.at[slot]))
        copies[-1].start()
    for copy in copies:
        copy.wait()


def outer_kernel(
    far_inner, state, pulled, resistance, solid, flags, partial, from_left, from_right,
    far_start, total, start, done,
):
    del far_inner
    nx = resistance.shape[0]
    copies = []
    total[...] = partial[...]
    for slot, x in start_columns(
        (0, nx - 1), state, pulled, resistance, solid, flags, partial, from_left, from_right, start, total
    ):
        copies.append(pltpu.make_async_copy(start.at[slot], far_start.at[:, x], done.at[slot]))
        copies[-1].start()
    for copy in copies:
        copy.wait()


VMEM_LIMIT = 40 * 1024 * 1024
VMEM, HBM = (pl.BlockSpec(memory_space=m) for m in (pltpu.VMEM, pltpu.HBM))


def call(kernel, outs, *args, scratch=(), far=(), far_out=(), aliases=None):
    return pl.pallas_call(
        kernel,
        out_shape=[jax.ShapeDtypeStruct(s, jnp.float32) for s in outs],
        in_specs=[HBM if k in far else VMEM for k in range(len(args))],
        out_specs=[HBM if k in far_out else VMEM for k in range(len(outs))],
        scratch_shapes=[pltpu.VMEM(s, jnp.float32) if isinstance(s, tuple) else s for s in scratch],
        input_output_aliases=aliases or {},
        compiler_params=pltpu.CompilerParams(vmem_limit_bytes=VMEM_LIMIT),
    )(*args)


def in_hbm(*arrays):
    return [pltpu.with_memory_space_constraint(v, pltpu.HBM) for v in arrays]


def exchange(axis, onward, backward):
    count = lax.axis_size(axis)
    ahead = [(i, (i + 1) % count) for i in range(count)]
    behind = [(i, (i - 1) % count) for i in range(count)]
    return lax.ppermute(onward, axis, ahead), lax.ppermute(backward, axis, behind)


def body(checkpoint, adjoint_end, resistance, solid_mask, flags):
    nx, ny, nz = resistance.shape
    whole, voxels, rim = checkpoint.shape, resistance.shape, (19, 2 * nx, nz)
    cells = (resistance, solid_mask, flags)
    pair = [pltpu.VMEM((2, ny, nz), jnp.int32)] * 2
    right, left = call(
        face_kernel, [(10, ny, nz)] * 2, *in_hbm(checkpoint, adjoint_end, *cells), far=range(5),
        scratch=[(2, 19, ny, nz), (2, ny, nz), *pair, pltpu.SemaphoreType.DMA((18,))],
    )
    sides = exchange("gx", right, left)
    (post,) = call(post_kernel, [whole], checkpoint, *cells)
    up, down = call(
        rim_kernel, [(30, nx, nz)] * 2, post, adjoint_end, *cells, *sides,
        scratch=[(38, 2 * nx, nz)],
    )
    below, above = exchange("gy", up, down)
    out, sens, *rims = call(
        middle_kernel, [whole, voxels, rim, rim], post, adjoint_end, *cells, *sides,
        scratch=[whole, whole],
    )
    outer_rows, halo_rows, outer_sens, right, left = call(
        edge_kernel, [rim, rim, rim[1:], (5, ny, nz), (5, ny, nz)],
        out, *cells, *rims, up, down, below, above,
        scratch=[rim, rim, rim, (9, *rim[1:])],
    )
    sides = exchange("gx", right, left)
    start, pulled, partial = call(
        inner_kernel, [whole, whole, voxels],
        out, outer_rows, halo_rows, sens, outer_sens, checkpoint, *cells, far_out=(0,),
        scratch=[(nx - 2, 19, ny, nz), pltpu.SemaphoreType.DMA((nx - 2,))],
    )
    start, sensitivity = call(
        outer_kernel, [whole, voxels],
        *in_hbm(start), checkpoint, pulled, *cells, partial, *sides, far=(0,), far_out=(0,), aliases={0: 0},
        scratch=[(2, 19, ny, nz), pltpu.SemaphoreType.DMA((2,))],
    )
    return start, sensitivity


def solution(mesh):
    state, cell = P(None, "gx", "gy", None), P("gx", "gy", None)
    return jax.shard_map(
        body,
        mesh=mesh,
        in_specs=(state, state, cell, cell, cell),
        out_specs=(state, cell),
        check_vma=False,
    )
```

```python
import jax
import jax.numpy as jnp
from jax import lax
from jax.experimental import pallas as pl
from jax.experimental.pallas import tpu as pltpu
from jax.sharding import PartitionSpec as P

VELOCITY = (
    (0, 0, 0),
    (1, 0, 0),
    (-1, 0, 0),
    (0, 1, 0),
    (0, -1, 0),
    (0, 0, 1),
    (0, 0, -1),
    (1, 1, 0),
    (-1, -1, 0),
    (1, -1, 0),
    (-1, 1, 0),
    (1, 0, 1),
    (-1, 0, -1),
    (1, 0, -1),
    (-1, 0, 1),
    (0, 1, 1),
    (0, -1, -1),
    (0, 1, -1),
    (0, -1, 1),
)


def pair_sums(f):
    even = [f[2 * k + 1] + f[2 * k + 2] for k in range(9)]
    odd = [f[2 * k + 1] - f[2 * k + 2] for k in range(9)]
    return even, odd


def grouped(f):
    even, odd = pair_sums(f)
    faces = even[:3]
    planes = [even[7] + even[8], even[5] + even[6], even[3] + even[4]]
    shears = [even[7] - even[8], even[5] - even[6], even[3] - even[4]]
    axes = [
        (odd[0], odd[3] + odd[4], odd[5] + odd[6]),
        (odd[1], odd[3] - odd[4], odd[7] + odd[8]),
        (odd[2], odd[5] - odd[6], odd[7] - odd[8]),
    ]
    return faces, planes, shears, axes, odd


def half_pairs(faces, planes, shears, axes):
    even = [0.5 * v for v in faces]
    for a in (2, 1, 0):
        even += [0.25 * (planes[a] + shears[a]), 0.25 * (planes[a] - shears[a])]
    odd = [0.5 * axes[a][0] for a in range(3)]
    for one, two in ((axes[0][1], axes[1][1]), (axes[0][2], axes[2][1]), (axes[1][2], axes[2][2])):
        odd += [0.25 * (one + two), 0.25 * (one - two)]
    return even, odd


def finish(rest, f, odd_sums, even, odd, grey, free):
    out = [f[0] - free * rest]
    for k in range(9):
        e = free * even[k]
        o = free * odd[k] + grey * odd_sums[k]
        out += [f[2 * k + 1] - (e + o), f[2 * k + 2] - (e - o)]
    return out


def collide_tile(f, grey, rate):
    faces, planes, shears, axes, odd_sums = grouped(f)
    total = faces[0] + faces[1] + faces[2]
    edges = planes[0] + planes[1] + planes[2]
    momentum = [d + a + b for d, a, b in axes]
    inverse = 1.0 / (f[0] + total + edges)
    u = [m * inverse for m in momentum]
    q = [m * v for m, v in zip(momentum, u)]
    q_all = q[0] + q[1] + q[2]
    energy = (1.19 * 19.0 / 2394.0) * (edges - f[0] - q_all)
    square = (1.4 / 252.0) * (9.0 * f[0] - 7.0 * total - 2.0 * edges + 5.5 * q_all)
    rest = 12.0 * square - 30.0 * energy
    d_total = -22.0 * energy - 8.0 * square
    d_edges = 32.0 * energy + 4.0 * square
    d_faces, d_planes = [], []
    for a in range(3):
        x = 3.0 * faces[a] - total
        y = edges - 3.0 * planes[a]
        eq = 3.0 * q[a] - q_all
        stress = rate * (x + y - eq)
        other = 1.4 * (y - 2.0 * x + 0.5 * eq)
        d_faces.append(d_total + (1.0 / 9.0) * (stress - other))
        d_planes.append(d_edges - (1.0 / 9.0) * (2.0 * stress + other))
    d_shears = [
        rate * (shears[0] - momentum[1] * u[2]),
        rate * (shears[1] - momentum[0] * u[2]),
        rate * (shears[2] - momentum[0] * u[1]),
    ]
    d_axes = []
    for d, a, b in axes:
        t = 0.2 * (a + b - 2.0 * d)
        v = 0.99 * (a - b)
        d_axes.append((-2.0 * t, t + v, t - v))
    even, odd = half_pairs(d_faces, d_planes, d_shears, d_axes)
    return finish(rest, f, odd_sums, even, odd, grey, 1.0 - grey)


def by_velocity(weights, cross, u):
    return [
        weights[0] * u[0] + cross[2] * u[1] + cross[1] * u[2],
        weights[1] * u[1] + cross[2] * u[0] + cross[0] * u[2],
        weights[2] * u[2] + cross[1] * u[0] + cross[0] * u[1],
    ]


def adjoint_at(lam, u, grey, rate):
    faces, planes, shears, axes, odd_sums = grouped(lam)
    total = faces[0] + faces[1] + faces[2]
    edges = planes[0] + planes[1] + planes[2]
    energy = (1.19 / 2394.0) * (8.0 * edges - 11.0 * total - 30.0 * lam[0])
    square = (1.4 / 252.0) * (edges - 4.0 * total + 12.0 * lam[0])
    bulk = 19.0 * energy - 5.5 * square
    weights, w_faces, w_planes, slopes, w_axes = [], [], [], [], []
    w_total = -22.0 * energy - 8.0 * square
    w_edges = 32.0 * energy + 4.0 * square
    for a in range(3):
        x = 3.0 * faces[a] - total
        y = edges - 3.0 * planes[a]
        stress = rate * (x + y)
        other = 1.4 * (y - 2.0 * x)
        w_faces.append(w_total + (1.0 / 9.0) * (stress - other))
        w_planes.append(w_edges - (1.0 / 9.0) * (2.0 * stress + other))
        weights.append(2.0 * bulk + (1.0 / 9.0) * stress - (1.0 / 36.0) * other)
    w_shears = [rate * v for v in shears]
    cross = [0.25 * v for v in w_shears]
    pull = by_velocity(weights, cross, u) if u else [0.0] * 3
    by_density = 3.0 * square - 11.0 * energy
    if u:
        by_density = by_density - 0.5 * (u[0] * pull[0] + u[1] * pull[1] + u[2] * pull[2])
    for a in range(3):
        d, p, r = axes[a]
        flux = p + r - 4.0 * d
        v = 0.99 * (p - r)
        slope = pull[a] - 0.02 * flux
        t = 0.12 * flux - 4.0 * slope
        w_axes.append((-0.24 * flux - 2.0 * slope, t + v, t - v))
    rest = 12.0 * square - 30.0 * energy - by_density
    w_faces = [v - 2.0 * by_density for v in w_faces]
    w_planes = [v - 4.0 * by_density for v in w_planes]
    even, odd = half_pairs(w_faces, w_planes, w_shears, w_axes)
    out = finish(rest, lam, odd_sums, even, odd, grey, 1.0 - grey)
    for a in range(3):
        (wd, wa, wb), (ld, lp, lr) = w_axes[a], axes[a]
        w_axes[a] = (wd - 2.0 * ld, wa - 2.0 * lp, wb - 2.0 * lr)
    return out, (rest, w_faces, w_planes, w_shears, w_axes), (weights, cross)


def adjoint_tile(lam, f, grey, rate):
    faces, planes, shears, axes, _ = grouped(f)
    momentum = [d + a + b for d, a, b in axes]
    inverse = 1.0 / (f[0] + (faces[0] + faces[1] + faces[2]) + (planes[0] + planes[1] + planes[2]))
    u = [m * inverse for m in momentum]
    out, (rest, w_faces, w_planes, w_shears, w_axes), _ = adjoint_at(lam, u, grey, rate)
    near, far = 0.0, 0.0
    for a in range(3):
        (wd, wa, wb), (d, p, r) = w_axes[a], axes[a]
        near = near + w_faces[a] * faces[a] + wd * d
        far = far + w_planes[a] * planes[a] + w_shears[a] * shears[a] + wa * p + wb * r
    return out, rest * f[0] + 0.5 * near + 0.25 * far


def greyness(resistance, solid):
    return jnp.where(solid == 1, 1.0, resistance)


def shear_rate(flags):
    return jnp.where(flags == 0, 1.25, jnp.where(flags == 1, 0.9, 1.7))


def moving(sign, dim, step):
    return [i for i in range(19) if sign * VELOCITY[i][dim] == step]


SHARE, AT_REST, WEIGHTS, GREY, RATE, PLANES = 0, 9, 14, 25, 26, 27


def edge_plane(field, way, i):
    return (4, 20)[field] + moving(1 - 2 * field, 1, way).index(i)


def halo_terms(lam, grey, rate):
    out, _, (weights, cross) = adjoint_at(lam, None, grey, rate)
    free = 1.0 - grey
    return out, [free * v for v in (*weights, *cross)]


def x_plane(field, i):
    return 5 * field + moving(1 - 2 * field, 0, (1 - 2 * field) * VELOCITY[i][0]).index(i)


def velocity(field, i):
    return tuple((1 - 2 * field) * v for v in VELOCITY[i])


def rolled_y(block, step):
    return pltpu.roll(block, step % block.shape[0], 0) if step else block


def shifted_y(block, step, below, above):
    if step == 0:
        return block
    row = lax.broadcasted_iota(jnp.int32, block.shape, 0)
    if step == 1:
        return jnp.where(row == 0, below, rolled_y(block, 1))
    return jnp.where(row == block.shape[0] - 1, above, rolled_y(block, -1))


def shifted_z(block, step):
    return pltpu.roll(block, step % block.shape[1], 1) if step else block


def face_kernel(
    far_state, far_adjoint, far_resistance, far_solid, far_flags, right, left,
    state, resistance, solid, flags, done,
):
    nx, ny, nz = far_resistance.shape
    sides = ((right, 1, nx - 1), (left, -1, 0))
    copies, first = [], []
    for side, (message, way, x) in enumerate(sides):
        pairs = [
            (far_state.at[:, x], state.at[side]),
            (far_resistance.at[x], resistance.at[side]),
            (far_solid.at[x], solid.at[side]),
            (far_flags.at[x], flags.at[side]),
        ]
        pairs += [(far_adjoint.at[i, x], message.at[x_plane(1, i)]) for i in moving(-1, 0, way)]
        first.append(len(copies))
        for source, target in pairs:
            copies.append(pltpu.make_async_copy(source, target, done.at[len(copies)]))
    for copy in copies:
        copy.start()
    for side, (message, way, _) in enumerate(sides):
        for copy in copies[first[side] : first[side] + 4]:
            copy.wait()

        def step(t, carry, side=side, message=message, way=way):
            rows = pl.ds(pl.multiple_of(t * 8, 8), 8)
            for half in range(nz // 128):
                at = (rows, pl.ds(half * 128, 128))
                out = collide_tile(
                    [state[(side, i, *at)] for i in range(19)],
                    greyness(resistance[(side, *at)], solid[(side, *at)]),
                    shear_rate(flags[(side, *at)]),
                )
                for i in moving(1, 0, way):
                    message[(x_plane(0, i), *at)] = out[i]
            return carry

        lax.fori_loop(0, ny // 8, step, 0)
    for side in range(2):
        for copy in copies[first[side] + 4 : first[side] + 9]:
            copy.wait()


def post_kernel(
    far_state, far_adjoint, far_resistance, far_solid, far_flags,
    post, state, adjoint, resistance, solid, flags, done,
):
    nx, ny, nz = resistance.shape
    pairs = [(far_resistance, resistance), (far_solid, solid), (far_flags, flags)]
    pairs += [(far_state.at[:, x], state.at[:, x]) for x in range(nx)] + [(far_adjoint, adjoint)]
    copies = [pltpu.make_async_copy(*pair, done.at[k]) for k, pair in enumerate(pairs)]
    for copy in copies:
        copy.start()
    for copy in copies[:3]:
        copy.wait()
    for x in range(nx):
        copies[3 + x].wait()

        def step(t, carry, x=x):
            rows = pl.ds(pl.multiple_of(t * 8, 8), 8)
            for half in range(nz // 128):
                at = (x, rows, pl.ds(half * 128, 128))
                out = collide_tile(
                    [state[(i, *at)] for i in range(19)],
                    greyness(resistance[at], solid[at]),
                    shear_rate(flags[at]),
                )
                for i in range(19):
                    post[(i, *at)] = out[i]
            return carry

        lax.fori_loop(0, ny // 8, step, 0)
    copies[-1].wait()


def rim_kernel(
    post, adjoint, resistance, solid, flags, from_left, from_right, up, down, work, near, cells
):
    nx, ny, nz = resistance.shape
    shares = {1: [0.0] * 4, -1: [0.0] * 4}
    halves = (slice(0, nx), slice(nx, 2 * nx))
    for field, source in ((0, post), (1, adjoint)):
        for i in range(19):
            vx, vy, vz = velocity(field, i)
            picks = {0: (ny - 1, 0), 1: (ny - 2, ny - 1), -1: (1, 0)}[vy]
            tile = work.at[19 * field + i]
            for half, row in enumerate(picks):
                base = half * nx
                if vx == 0:
                    tile[base : base + nx, :] = source[i, :, row, :]
                    continue
                outer = from_left if vx == 1 else from_right
                edge = outer[x_plane(field, i), pl.ds(row, 1), :]
                lines = source[i, :, row, :]
                if vx == 1:
                    tile[base + 1 : base + nx, :] = lines[: nx - 1]
                    tile[base : base + 1, :] = edge
                else:
                    tile[base : base + nx - 1, :] = lines[1:]
                    tile[base + nx - 1 : base + nx, :] = edge
            if vz:
                tile[...] = shifted_z(tile[...], vz)
            for half in range(2):
                value = tile[halves[half]]
                way = vy if vy else 1 - 2 * half
                message = up if way == 1 else down
                if vy and half == 1:
                    message[edge_plane(field, way, i)] = value
                elif field == 1:
                    side = 0 if way == 1 else 1
                    near[i, halves[side], :] = value
                    if vy:
                        near[i, halves[1 - side], :] = jnp.zeros_like(value)
                else:
                    share = shares[way]
                    for k, factor in enumerate((1, vx, vy, vz)):
                        if factor:
                            share[k] = share[k] + factor * value
    for way, message, row, half in ((1, up, ny - 1, halves[0]), (-1, down, 0, halves[1])):
        for k in range(4):
            message[SHARE + k] = shares[way][k]
        cells[0, half, :] = message[GREY] = greyness(resistance[:, row, :], solid[:, row, :])
        cells[1, half, :] = message[RATE] = shear_rate(flags[:, row, :])
    for part in range(nz // 128):
        lanes = pl.ds(part * 128, 128)
        at = (slice(None), lanes)
        out, weights = halo_terms(
            [near[(i, *at)] for i in range(19)], cells[(0, *at)], cells[(1, *at)]
        )
        for way, message, half in ((1, up, halves[0]), (-1, down, halves[1])):
            for k, i in enumerate(moving(-1, 1, way)):
                message[AT_REST + k, :, lanes] = out[i][half]
            for k in range(6):
                message[WEIGHTS + k, :, lanes] = weights[k][half]


def middle_kernel(
    post, adjoint, resistance, solid, flags, from_left, from_right,
    out, sensitivity, rim_middle, rim_cotangent, middle, cotangent,
):
    nx, ny, nz = resistance.shape
    tiles = ny // 8
    for field, source, target, rim in (
        (0, post, middle, rim_middle),
        (1, adjoint, cotangent, rim_cotangent),
    ):
        for i in range(19):
            vx, vy, vz = velocity(field, i)
            for x in range(nx):
                if 0 <= x - vx < nx:
                    block = source[i, x - vx]
                else:
                    block = (from_left if vx == 1 else from_right)[x_plane(field, i)]
                block = rolled_y(shifted_z(block, vz), vy)
                target[i, x] = block
                rim[i, x : x + 1, :] = block[:1]
                rim[i, nx + x : nx + x + 1, :] = block[ny - 1 :]

    def step(n, carry):
        x, rows = n // tiles, pl.ds(pl.multiple_of(n % tiles * 8, 8), 8)
        for half in range(nz // 128):
            at = (x, rows, pl.ds(half * 128, 128))
            state = [middle[(i, *at)] for i in range(19)]
            new, sens = adjoint_tile(
                [cotangent[(i, *at)] for i in range(19)],
                state,
                greyness(resistance[at], solid[at]),
                shear_rate(flags[at]),
            )
            sensitivity[at] = jnp.where(solid[at] == 1, 0.0, sens)
            for i in range(19):
                out[(i, *at)] = new[i]
        return carry

    lax.fori_loop(0, nx * tiles, step, 0)


def pulled_block(out, outer_rows, halo_rows, i, x):
    nx, ny = out.shape[1:3]
    _, vy, vz = velocity(1, i)
    block = out[i, x]
    row = lax.broadcasted_iota(jnp.int32, block.shape, 0)
    block = jnp.where(row == 0, outer_rows[i, pl.ds(x, 1), :], block)
    block = jnp.where(row == ny - 1, outer_rows[i, pl.ds(nx + x, 1), :], block)
    low = halo_rows[i, pl.ds(x, 1), :] if vy == 1 else None
    high = halo_rows[i, pl.ds(nx + x, 1), :] if vy == -1 else None
    return shifted_z(shifted_y(block, vy, low, high), vz)


def edge_kernel(
    out, resistance, solid, flags, rim_middle, rim_cotangent, up, down, below, above,
    outer_rows, halo_rows, outer_sens, right, left, middle, cotangent, cells,
):
    nx, ny, nz = resistance.shape
    low, high = slice(0, nx), slice(nx, 2 * nx)
    for field, rim, target in ((0, rim_middle, middle), (1, rim_cotangent, cotangent)):
        for i in range(19):
            vy = velocity(field, i)[1]
            target[i] = rim[i]
            if vy == 1:
                target[i, low, :] = below[edge_plane(field, 1, i)]
            if vy == -1:
                target[i, high, :] = above[edge_plane(field, -1, i)]
    for rows, way, received, sent in ((low, 1, below, down), (high, -1, above, up)):
        share = [received[SHARE + k] for k in range(4)]
        for i in moving(1, 1, -way):
            value = sent[edge_plane(0, -way, i)]
            for k, factor in enumerate((1, *VELOCITY[i])):
                if factor:
                    share[k] = share[k] + factor * value
        u = [v / share[0] for v in share[1:]]
        lam = [jnp.zeros_like(share[0])] * 19
        for i in moving(-1, 1, -way):
            lam[i] = sent[edge_plane(1, -way, i)]
        own, weights = halo_terms(lam, received[GREY], received[RATE])
        weights = [v + received[WEIGHTS + k] for k, v in enumerate(weights)]
        pull = by_velocity(weights[:3], weights[3:], u)
        scale = 0.5 * (u[0] * pull[0] + u[1] * pull[1] + u[2] * pull[2])
        for k, i in enumerate(moving(-1, 1, way)):
            value = own[i] + received[AT_REST + k] - scale
            for a in range(3):
                if VELOCITY[i][a]:
                    value = value + VELOCITY[i][a] * pull[a]
            halo_rows[i, rows, :] = value
        row = 0 if way == 1 else ny - 1
        blocked = solid[:, row, :]
        cells[0, rows, :] = greyness(resistance[:, row, :], blocked)
        cells[1, rows, :] = shear_rate(flags[:, row, :])
        cells[2, rows, :] = jnp.where(blocked == 1, 0.0, 1.0)
    for part in range(nz // 128):
        at = (slice(None), pl.ds(part * 128, 128))
        state = [middle[(i, *at)] for i in range(19)]
        new, sens = adjoint_tile(
            [cotangent[(i, *at)] for i in range(19)], state, cells[(0, *at)], cells[(1, *at)]
        )
        outer_sens[at] = jnp.where(cells[(2, *at)] == 0.0, 0.0, sens)
        for i in range(19):
            outer_rows[(i, *at)] = new[i]
    for message, way, x in ((right, 1, nx - 1), (left, -1, 0)):
        for k, i in enumerate(moving(-1, 0, way)):
            message[k] = pulled_block(out, outer_rows, halo_rows, i, x)


def start_columns(
    columns, state, pulled, resistance, solid, flags, partial, from_left, from_right,
    start, total, far_start, far_total, done,
):
    nx, ny, nz = resistance.shape
    copies = []
    for slot, x in enumerate(columns):

        def step(t, carry, x=x, slot=slot):
            rows = pl.ds(pl.multiple_of(t * 8, 8), 8)
            for half in range(nz // 128):
                lanes = pl.ds(half * 128, 128)
                at = (x, rows, lanes)
                cotangent = []
                for i in range(19):
                    source = x + VELOCITY[i][0]
                    if source < 0:
                        cotangent.append(from_left[moving(-1, 0, 1).index(i), rows, lanes])
                    elif source == nx:
                        cotangent.append(from_right[moving(-1, 0, -1).index(i), rows, lanes])
                    else:
                        cotangent.append(pulled[i, source, rows, lanes])
                new, sens = adjoint_tile(
                    cotangent,
                    [state[(i, *at)] for i in range(19)],
                    greyness(resistance[at], solid[at]),
                    shear_rate(flags[at]),
                )
                for i in range(19):
                    start[slot, i, rows, lanes] = new[i]
                total[slot, rows, lanes] = partial[at] + jnp.where(solid[at] == 1, 0.0, sens)
            return carry

        lax.fori_loop(0, ny // 8, step, 0)
        pairs = ((start.at[slot], far_start.at[:, x]), (total.at[slot], far_total.at[x]))
        for k, pair in enumerate(pairs):
            copies.append(pltpu.make_async_copy(*pair, done.at[2 * slot + k]))
            copies[-1].start()
    for copy in copies:
        copy.wait()


def inner_kernel(
    out, outer_rows, halo_rows, sens, outer_sens, state, resistance, solid, flags,
    far_start, far_total, pulled, partial, start, total, done,
):
    nx, ny = resistance.shape[:2]
    for x in range(nx):
        for i in range(19):
            pulled[i, x] = pulled_block(out, outer_rows, halo_rows, i, x)
        block = sens[x]
        row = lax.broadcasted_iota(jnp.int32, block.shape, 0)
        block = jnp.where(row == 0, outer_sens[pl.ds(x, 1), :], block)
        partial[x] = jnp.where(row == ny - 1, outer_sens[pl.ds(nx + x, 1), :], block)
    start_columns(
        range(1, nx - 1), state, pulled, resistance, solid, flags, partial, None, None,
        start, total, far_start, far_total, done,
    )


def outer_kernel(
    inner_start, inner_total, state, pulled, resistance, solid, flags, partial, from_left, from_right,
    far_start, far_total, start, total, done,
):
    del inner_start, inner_total
    start_columns(
        (0, resistance.shape[0] - 1), state, pulled, resistance, solid, flags, partial, from_left,
        from_right, start, total, far_start, far_total, done,
    )


VMEM_LIMIT = 40 * 1024 * 1024
VMEM, HBM = (pl.BlockSpec(memory_space=m) for m in (pltpu.VMEM, pltpu.HBM))


def call(kernel, outs, *args, scratch=(), far=(), far_out=(), aliases=None):
    made = [v if isinstance(v, jax.ShapeDtypeStruct) else jax.ShapeDtypeStruct(v, jnp.float32) for v in outs]
    return pl.pallas_call(
        kernel,
        out_shape=made,
        in_specs=[HBM if k in far else VMEM for k in range(len(args))],
        out_specs=[HBM if k in far_out else VMEM for k in range(len(outs))],
        scratch_shapes=[pltpu.VMEM(s, jnp.float32) if isinstance(s, tuple) else s for s in scratch],
        input_output_aliases=aliases or {},
        compiler_params=pltpu.CompilerParams(vmem_limit_bytes=VMEM_LIMIT),
    )(*args)


def in_hbm(*arrays):
    return [pltpu.with_memory_space_constraint(v, pltpu.HBM) for v in arrays]


def exchange(axis, onward, backward):
    count = lax.axis_size(axis)
    ahead = [(i, (i + 1) % count) for i in range(count)]
    behind = [(i, (i - 1) % count) for i in range(count)]
    return lax.ppermute(onward, axis, ahead), lax.ppermute(backward, axis, behind)


def body(checkpoint, adjoint_end, resistance, solid_mask, flags):
    nx, ny, nz = resistance.shape
    whole, voxels, rim = checkpoint.shape, resistance.shape, (19, 2 * nx, nz)
    far = in_hbm(checkpoint, adjoint_end, resistance, solid_mask, flags)
    pair = [pltpu.VMEM((2, ny, nz), jnp.int32)] * 2
    right, left = call(
        face_kernel, [(10, ny, nz)] * 2, *far, far=range(5),
        scratch=[(2, 19, ny, nz), (2, ny, nz), *pair, pltpu.SemaphoreType.DMA((18,))],
    )
    sides = exchange("gx", right, left)
    post, checkpoint, adjoint_end, *cells = call(
        post_kernel, [whole] + [jax.ShapeDtypeStruct(v.shape, v.dtype) for v in far],
        *far, far=range(5), scratch=[pltpu.SemaphoreType.DMA((nx + 4,))],
    )
    up, down = call(
        rim_kernel, [(PLANES, nx, nz)] * 2, post, adjoint_end, *cells, *sides,
        scratch=[(38, *rim[1:]), rim, (2, *rim[1:])],
    )
    below, above = exchange("gy", up, down)
    out, sens, *rims = call(
        middle_kernel, [whole, voxels, rim, rim], post, adjoint_end, *cells, *sides,
        scratch=[whole, whole],
    )
    outer_rows, halo_rows, outer_sens, right, left = call(
        edge_kernel, [rim, rim, rim[1:], (5, ny, nz), (5, ny, nz)],
        out, *cells, *rims, up, down, below, above,
        scratch=[rim, rim, (3, *rim[1:])],
    )
    sides = exchange("gx", right, left)
    *done, pulled, partial = call(
        inner_kernel, [whole, voxels, whole, voxels],
        out, outer_rows, halo_rows, sens, outer_sens, checkpoint, *cells, far_out=(0, 1),
        scratch=[(nx - 2, 19, ny, nz), (nx - 2, ny, nz), pltpu.SemaphoreType.DMA((2 * nx - 4,))],
    )
    start, sensitivity = call(
        outer_kernel, [whole, voxels],
        *in_hbm(*done), checkpoint, pulled, *cells, partial, *sides,
        far=(0, 1), far_out=(0, 1), aliases={0: 0, 1: 1},
        scratch=[(2, 19, ny, nz), (2, ny, nz), pltpu.SemaphoreType.DMA((4,))],
    )
    return start, sensitivity


def solution(mesh):
    state, cell = P(None, "gx", "gy", None), P("gx", "gy", None)
    return jax.shard_map(
        body,
        mesh=mesh,
        in_specs=(state, state, cell, cell, cell),
        out_specs=(state, cell),
        check_vma=False,
    )
```

```python
import jax
import jax.numpy as jnp
from jax import lax
from jax.experimental import pallas as pl
from jax.experimental.pallas import tpu as pltpu
from jax.sharding import PartitionSpec as P

VELOCITY = (
    (0, 0, 0),
    (1, 0, 0),
    (-1, 0, 0),
    (0, 1, 0),
    (0, -1, 0),
    (0, 0, 1),
    (0, 0, -1),
    (1, 1, 0),
    (-1, -1, 0),
    (1, -1, 0),
    (-1, 1, 0),
    (1, 0, 1),
    (-1, 0, -1),
    (1, 0, -1),
    (-1, 0, 1),
    (0, 1, 1),
    (0, -1, -1),
    (0, 1, -1),
    (0, -1, 1),
)


def pair_sums(f):
    even = [f[2 * k + 1] + f[2 * k + 2] for k in range(9)]
    odd = [f[2 * k + 1] - f[2 * k + 2] for k in range(9)]
    return even, odd


def grouped(f):
    even, odd = pair_sums(f)
    faces = even[:3]
    planes = [even[7] + even[8], even[5] + even[6], even[3] + even[4]]
    shears = [even[7] - even[8], even[5] - even[6], even[3] - even[4]]
    axes = [
        (odd[0], odd[3] + odd[4], odd[5] + odd[6]),
        (odd[1], odd[3] - odd[4], odd[7] + odd[8]),
        (odd[2], odd[5] - odd[6], odd[7] - odd[8]),
    ]
    return faces, planes, shears, axes, odd


def half_pairs(faces, planes, shears, axes):
    even = [0.5 * v for v in faces]
    for a in (2, 1, 0):
        even += [0.25 * (planes[a] + shears[a]), 0.25 * (planes[a] - shears[a])]
    odd = [0.5 * axes[a][0] for a in range(3)]
    for one, two in ((axes[0][1], axes[1][1]), (axes[0][2], axes[2][1]), (axes[1][2], axes[2][2])):
        odd += [0.25 * (one + two), 0.25 * (one - two)]
    return even, odd


def finish(rest, f, odd_sums, even, odd, grey, free):
    out = [f[0] - free * rest]
    for k in range(9):
        e = free * even[k]
        o = free * odd[k] + grey * odd_sums[k]
        out += [f[2 * k + 1] - (e + o), f[2 * k + 2] - (e - o)]
    return out


def collide_tile(f, grey, rate):
    faces, planes, shears, axes, odd_sums = grouped(f)
    total = faces[0] + faces[1] + faces[2]
    edges = planes[0] + planes[1] + planes[2]
    momentum = [d + a + b for d, a, b in axes]
    inverse = 1.0 / (f[0] + total + edges)
    u = [m * inverse for m in momentum]
    q = [m * v for m, v in zip(momentum, u)]
    q_all = q[0] + q[1] + q[2]
    energy = (1.19 * 19.0 / 2394.0) * (edges - f[0] - q_all)
    square = (1.4 / 252.0) * (9.0 * f[0] - 7.0 * total - 2.0 * edges + 5.5 * q_all)
    rest = 12.0 * square - 30.0 * energy
    d_total = -22.0 * energy - 8.0 * square
    d_edges = 32.0 * energy + 4.0 * square
    d_faces, d_planes = [], []
    for a in range(3):
        x = 3.0 * faces[a] - total
        y = edges - 3.0 * planes[a]
        eq = 3.0 * q[a] - q_all
        stress = rate * (x + y - eq)
        other = 1.4 * (y - 2.0 * x + 0.5 * eq)
        d_faces.append(d_total + (1.0 / 9.0) * (stress - other))
        d_planes.append(d_edges - (1.0 / 9.0) * (2.0 * stress + other))
    d_shears = [
        rate * (shears[0] - momentum[1] * u[2]),
        rate * (shears[1] - momentum[0] * u[2]),
        rate * (shears[2] - momentum[0] * u[1]),
    ]
    d_axes = []
    for d, a, b in axes:
        t = 0.2 * (a + b - 2.0 * d)
        v = 0.99 * (a - b)
        d_axes.append((-2.0 * t, t + v, t - v))
    even, odd = half_pairs(d_faces, d_planes, d_shears, d_axes)
    return finish(rest, f, odd_sums, even, odd, grey, 1.0 - grey)


def by_velocity(weights, cross, u):
    return [
        weights[0] * u[0] + cross[2] * u[1] + cross[1] * u[2],
        weights[1] * u[1] + cross[2] * u[0] + cross[0] * u[2],
        weights[2] * u[2] + cross[1] * u[0] + cross[0] * u[1],
    ]


def adjoint_at(lam, u, grey, rate):
    faces, planes, shears, axes, odd_sums = grouped(lam)
    total = faces[0] + faces[1] + faces[2]
    edges = planes[0] + planes[1] + planes[2]
    energy = (1.19 / 2394.0) * (8.0 * edges - 11.0 * total - 30.0 * lam[0])
    square = (1.4 / 252.0) * (edges - 4.0 * total + 12.0 * lam[0])
    bulk = 19.0 * energy - 5.5 * square
    weights, w_faces, w_planes, slopes, w_axes = [], [], [], [], []
    w_total = -22.0 * energy - 8.0 * square
    w_edges = 32.0 * energy + 4.0 * square
    for a in range(3):
        x = 3.0 * faces[a] - total
        y = edges - 3.0 * planes[a]
        stress = rate * (x + y)
        other = 1.4 * (y - 2.0 * x)
        w_faces.append(w_total + (1.0 / 9.0) * (stress - other))
        w_planes.append(w_edges - (1.0 / 9.0) * (2.0 * stress + other))
        weights.append(2.0 * bulk + (1.0 / 9.0) * stress - (1.0 / 36.0) * other)
    w_shears = [rate * v for v in shears]
    cross = [0.25 * v for v in w_shears]
    pull = by_velocity(weights, cross, u) if u else [0.0] * 3
    by_density = 3.0 * square - 11.0 * energy
    if u:
        by_density = by_density - 0.5 * (u[0] * pull[0] + u[1] * pull[1] + u[2] * pull[2])
    for a in range(3):
        d, p, r = axes[a]
        flux = p + r - 4.0 * d
        v = 0.99 * (p - r)
        slope = pull[a] - 0.02 * flux
        t = 0.12 * flux - 4.0 * slope
        w_axes.append((-0.24 * flux - 2.0 * slope, t + v, t - v))
    rest = 12.0 * square - 30.0 * energy - by_density
    w_faces = [v - 2.0 * by_density for v in w_faces]
    w_planes = [v - 4.0 * by_density for v in w_planes]
    even, odd = half_pairs(w_faces, w_planes, w_shears, w_axes)
    out = finish(rest, lam, odd_sums, even, odd, grey, 1.0 - grey)
    for a in range(3):
        (wd, wa, wb), (ld, lp, lr) = w_axes[a], axes[a]
        w_axes[a] = (wd - 2.0 * ld, wa - 2.0 * lp, wb - 2.0 * lr)
    return out, (rest, w_faces, w_planes, w_shears, w_axes), (weights, cross)


def adjoint_tile(lam, f, grey, rate):
    faces, planes, shears, axes, _ = grouped(f)
    momentum = [d + a + b for d, a, b in axes]
    inverse = 1.0 / (f[0] + (faces[0] + faces[1] + faces[2]) + (planes[0] + planes[1] + planes[2]))
    u = [m * inverse for m in momentum]
    out, (rest, w_faces, w_planes, w_shears, w_axes), _ = adjoint_at(lam, u, grey, rate)
    near, far = 0.0, 0.0
    for a in range(3):
        (wd, wa, wb), (d, p, r) = w_axes[a], axes[a]
        near = near + w_faces[a] * faces[a] + wd * d
        far = far + w_planes[a] * planes[a] + w_shears[a] * shears[a] + wa * p + wb * r
    return out, rest * f[0] + 0.5 * near + 0.25 * far


def greyness(resistance, solid):
    return jnp.where(solid == 1, 1.0, resistance)


def shear_rate(flags):
    return jnp.where(flags == 0, 1.25, jnp.where(flags == 1, 0.9, 1.7))


def moving(sign, dim, step):
    return [i for i in range(19) if sign * VELOCITY[i][dim] == step]


SHARE, AT_REST, WEIGHTS, GREY, RATE, PLANES = 0, 9, 14, 25, 26, 27


def edge_plane(field, way, i):
    return (4, 20)[field] + moving(1 - 2 * field, 1, way).index(i)


def halo_terms(lam, grey, rate):
    out, _, (weights, cross) = adjoint_at(lam, None, grey, rate)
    free = 1.0 - grey
    return out, [free * v for v in (*weights, *cross)]


def x_plane(field, i):
    return 5 * field + moving(1 - 2 * field, 0, (1 - 2 * field) * VELOCITY[i][0]).index(i)


def velocity(field, i):
    return tuple((1 - 2 * field) * v for v in VELOCITY[i])


def rolled_y(block, step):
    return pltpu.roll(block, step % block.shape[0], 0) if step else block


def shifted_y(block, step, below, above):
    if step == 0:
        return block
    row = lax.broadcasted_iota(jnp.int32, block.shape, 0)
    if step == 1:
        return jnp.where(row == 0, below, rolled_y(block, 1))
    return jnp.where(row == block.shape[0] - 1, above, rolled_y(block, -1))


def shifted_z(block, step):
    return pltpu.roll(block, step % block.shape[1], 1) if step else block


def face_kernel(
    far_state, far_adjoint, far_resistance, far_solid, far_flags, right, left,
    state, resistance, solid, flags, done,
):
    nx, ny, nz = far_resistance.shape
    sides = ((right, 1, nx - 1), (left, -1, 0))
    copies, first = [], []
    for side, (message, way, x) in enumerate(sides):
        pairs = [
            (far_state.at[:, x], state.at[side]),
            (far_resistance.at[x], resistance.at[side]),
            (far_solid.at[x], solid.at[side]),
            (far_flags.at[x], flags.at[side]),
        ]
        pairs += [(far_adjoint.at[i, x], message.at[x_plane(1, i)]) for i in moving(-1, 0, way)]
        first.append(len(copies))
        for source, target in pairs:
            copies.append(pltpu.make_async_copy(source, target, done.at[len(copies)]))
    for copy in copies:
        copy.start()
    for side, (message, way, _) in enumerate(sides):
        for copy in copies[first[side] : first[side] + 4]:
            copy.wait()

        def step(t, carry, side=side, message=message, way=way):
            rows = pl.ds(pl.multiple_of(t * 8, 8), 8)
            for half in range(nz // 128):
                at = (rows, pl.ds(half * 128, 128))
                out = collide_tile(
                    [state[(side, i, *at)] for i in range(19)],
                    greyness(resistance[(side, *at)], solid[(side, *at)]),
                    shear_rate(flags[(side, *at)]),
                )
                for i in moving(1, 0, way):
                    message[(x_plane(0, i), *at)] = out[i]
            return carry

        lax.fori_loop(0, ny // 8, step, 0)
    for side in range(2):
        for copy in copies[first[side] + 4 : first[side] + 9]:
            copy.wait()


def post_kernel(
    far_state, far_adjoint, far_resistance, far_solid, far_flags,
    post, state, adjoint, resistance, solid, flags, done,
):
    nx, ny, nz = resistance.shape
    pairs = [(far_resistance, resistance), (far_solid, solid), (far_flags, flags)]
    pairs += [(far_state.at[:, x], state.at[:, x]) for x in range(nx)] + [(far_adjoint, adjoint)]
    copies = [pltpu.make_async_copy(*pair, done.at[k]) for k, pair in enumerate(pairs)]
    for copy in copies:
        copy.start()
    for copy in copies[:3]:
        copy.wait()
    for x in range(nx):
        copies[3 + x].wait()

        def step(t, carry, x=x):
            rows = pl.ds(pl.multiple_of(t * 8, 8), 8)
            for half in range(nz // 128):
                at = (x, rows, pl.ds(half * 128, 128))
                out = collide_tile(
                    [state[(i, *at)] for i in range(19)],
                    greyness(resistance[at], solid[at]),
                    shear_rate(flags[at]),
                )
                for i in range(19):
                    post[(i, *at)] = out[i]
            return carry

        lax.fori_loop(0, ny // 8, step, 0)
    copies[-1].wait()


def rim_kernel(post, adjoint, resistance, solid, flags, up, down, work, near, cells):
    nx, ny, nz = resistance.shape
    shares = {1: [0.0] * 4, -1: [0.0] * 4}
    halves = (slice(0, nx), slice(nx, 2 * nx))
    for field, source in ((0, post), (1, adjoint)):
        for i in range(19):
            vx, vy, vz = velocity(field, i)
            picks = {0: (ny - 1, 0), 1: (ny - 2, ny - 1), -1: (1, 0)}[vy]
            tile = work.at[19 * field + i]
            for half, row in enumerate(picks):
                base = half * nx
                lines = source[i, :, row, :]
                if vx == 0:
                    tile[base : base + nx, :] = lines
                elif vx == 1:
                    tile[base + 1 : base + nx, :] = lines[: nx - 1]
                    tile[base : base + 1, :] = jnp.zeros_like(lines[:1])
                else:
                    tile[base : base + nx - 1, :] = lines[1:]
                    tile[base + nx - 1 : base + nx, :] = jnp.zeros_like(lines[:1])
            if vz:
                tile[...] = shifted_z(tile[...], vz)
            for half in range(2):
                value = tile[halves[half]]
                way = vy if vy else 1 - 2 * half
                message = up if way == 1 else down
                if vy and half == 1:
                    message[edge_plane(field, way, i)] = value
                elif field == 1:
                    side = 0 if way == 1 else 1
                    near[i, halves[side], :] = value
                    if vy:
                        near[i, halves[1 - side], :] = jnp.zeros_like(value)
                else:
                    share = shares[way]
                    for k, factor in enumerate((1, vx, vy, vz)):
                        if factor:
                            share[k] = share[k] + factor * value
    for way, message, row, half in ((1, up, ny - 1, halves[0]), (-1, down, 0, halves[1])):
        for k in range(4):
            message[SHARE + k] = shares[way][k]
        cells[0, half, :] = message[GREY] = greyness(resistance[:, row, :], solid[:, row, :])
        cells[1, half, :] = message[RATE] = shear_rate(flags[:, row, :])
    for part in range(nz // 128):
        lanes = pl.ds(part * 128, 128)
        at = (slice(None), lanes)
        out, weights = halo_terms(
            [near[(i, *at)] for i in range(19)], cells[(0, *at)], cells[(1, *at)]
        )
        for way, message, half in ((1, up, halves[0]), (-1, down, halves[1])):
            for k, i in enumerate(moving(-1, 1, way)):
                message[AT_REST + k, :, lanes] = out[i][half]
            for k in range(6):
                message[WEIGHTS + k, :, lanes] = weights[k][half]


EXTRA = tuple(range(SHARE, SHARE + 4)) + tuple(range(AT_REST, AT_REST + 5)) + tuple(range(WEIGHTS, WEIGHTS + 6))


def corner(field, vx, vy):
    return next(i for i in range(19) if velocity(field, i) == (vx, vy, 0))


def extra_kernel(resistance, solid, flags, from_left, from_right, up, down, near, cells):
    nx, ny, nz = resistance.shape
    near[...] = jnp.zeros(near.shape, jnp.float32)
    for side, (outer, vx, x) in enumerate(((from_left, 1, 0), (from_right, -1, nx - 1))):
        for half, (message, way, last, second) in enumerate(((up, 1, ny - 1, ny - 2), (down, -1, 0, 1))):
            row = 2 * half + side
            share = [0.0] * 4
            for field in range(2):
                for i in moving(1 - 2 * field, 0, vx):
                    _, vy, vz = velocity(field, i)
                    if vy == -way:
                        continue
                    pick = second if vy == way else last
                    value = shifted_z(outer[x_plane(field, i), pl.ds(pick, 1), :], vz)
                    if field == 1:
                        near[i, row : row + 1, :] = value
                        continue
                    for k, factor in enumerate((1, vx, vy, vz)):
                        if factor:
                            share[k] = share[k] + factor * value
                plane = x_plane(field, corner(field, vx, way))
                message[15 + field, side : side + 1, :] = outer[plane, pl.ds(last, 1), :]
            for k in range(4):
                message[k, side : side + 1, :] = share[k]
            at = (x, slice(last, last + 1), slice(None))
            cells[0, row : row + 1, :] = greyness(resistance[at], solid[at])
            cells[1, row : row + 1, :] = shear_rate(flags[at])
    for part in range(nz // 128):
        lanes = pl.ds(part * 128, 128)
        at = (slice(None), lanes)
        out, weights = halo_terms(
            [near[(i, *at)] for i in range(19)], cells[(0, *at)], cells[(1, *at)]
        )
        for half, (message, way) in enumerate(((up, 1), (down, -1))):
            rows = slice(2 * half, 2 * half + 2)
            for k, i in enumerate(moving(-1, 1, way)):
                message[4 + k, :, lanes] = out[i][rows]
            for k in range(6):
                message[9 + k, :, lanes] = weights[k][rows]


def add_extra(total, message, extra, way, planes):
    nx = total.shape[1]
    total[...] = message[...]
    for side, (vx, x) in enumerate(((1, 0), (-1, nx - 1))):
        places = EXTRA + tuple(edge_plane(f, way, corner(f, vx, way)) for f in range(2))
        for k in planes:
            to = (places[k], slice(x, x + 1), slice(None))
            total[to] = total[to] + extra[k, side : side + 1, :]


def middle_kernel(
    post, adjoint, resistance, solid, flags, from_left, from_right,
    out, sensitivity, rim_middle, rim_cotangent, middle, cotangent,
):
    nx, ny, nz = resistance.shape
    tiles = ny // 8
    for field, source, target, rim in (
        (0, post, middle, rim_middle),
        (1, adjoint, cotangent, rim_cotangent),
    ):
        for i in range(19):
            vx, vy, vz = velocity(field, i)
            for x in range(nx):
                if 0 <= x - vx < nx:
                    block = source[i, x - vx]
                else:
                    block = (from_left if vx == 1 else from_right)[x_plane(field, i)]
                block = rolled_y(shifted_z(block, vz), vy)
                target[i, x] = block
                rim[i, x : x + 1, :] = block[:1]
                rim[i, nx + x : nx + x + 1, :] = block[ny - 1 :]

    def step(n, carry):
        x, rows = n // tiles, pl.ds(pl.multiple_of(n % tiles * 8, 8), 8)
        for half in range(nz // 128):
            at = (x, rows, pl.ds(half * 128, 128))
            state = [middle[(i, *at)] for i in range(19)]
            new, sens = adjoint_tile(
                [cotangent[(i, *at)] for i in range(19)],
                state,
                greyness(resistance[at], solid[at]),
                shear_rate(flags[at]),
            )
            sensitivity[at] = jnp.where(solid[at] == 1, 0.0, sens)
            for i in range(19):
                out[(i, *at)] = new[i]
        return carry

    lax.fori_loop(0, nx * tiles, step, 0)


def pulled_block(out, outer_rows, halo_rows, i, x):
    nx, ny = out.shape[1:3]
    _, vy, vz = velocity(1, i)
    block = out[i, x]
    row = lax.broadcasted_iota(jnp.int32, block.shape, 0)
    block = jnp.where(row == 0, outer_rows[i, pl.ds(x, 1), :], block)
    block = jnp.where(row == ny - 1, outer_rows[i, pl.ds(nx + x, 1), :], block)
    low = halo_rows[i, pl.ds(x, 1), :] if vy == 1 else None
    high = halo_rows[i, pl.ds(nx + x, 1), :] if vy == -1 else None
    return shifted_z(shifted_y(block, vy, low, high), vz)


def edge_kernel(
    out, resistance, solid, flags, rim_middle, rim_cotangent, *refs
):
    messages, extras, refs = refs[:4], refs[4:8], refs[8:]
    outer_rows, halo_rows, outer_sens, right, left, middle, cotangent, cells, *totals = refs
    for k, way in enumerate((1, -1, 1, -1)):
        planes = (15, 16) if k < 2 else range(17)
        add_extra(totals[k], messages[k], extras[k], way, planes)
    up, down, below, above = totals
    nx, ny, nz = resistance.shape
    low, high = slice(0, nx), slice(nx, 2 * nx)
    for field, rim, target in ((0, rim_middle, middle), (1, rim_cotangent, cotangent)):
        for i in range(19):
            vy = velocity(field, i)[1]
            target[i] = rim[i]
            if vy == 1:
                target[i, low, :] = below[edge_plane(field, 1, i)]
            if vy == -1:
                target[i, high, :] = above[edge_plane(field, -1, i)]
    for rows, way, received, sent in ((low, 1, below, down), (high, -1, above, up)):
        share = [received[SHARE + k] for k in range(4)]
        for i in moving(1, 1, -way):
            value = sent[edge_plane(0, -way, i)]
            for k, factor in enumerate((1, *VELOCITY[i])):
                if factor:
                    share[k] = share[k] + factor * value
        u = [v / share[0] for v in share[1:]]
        lam = [jnp.zeros_like(share[0])] * 19
        for i in moving(-1, 1, -way):
            lam[i] = sent[edge_plane(1, -way, i)]
        own, weights = halo_terms(lam, received[GREY], received[RATE])
        weights = [v + received[WEIGHTS + k] for k, v in enumerate(weights)]
        pull = by_velocity(weights[:3], weights[3:], u)
        scale = 0.5 * (u[0] * pull[0] + u[1] * pull[1] + u[2] * pull[2])
        for k, i in enumerate(moving(-1, 1, way)):
            value = own[i] + received[AT_REST + k] - scale
            for a in range(3):
                if VELOCITY[i][a]:
                    value = value + VELOCITY[i][a] * pull[a]
            halo_rows[i, rows, :] = value
        row = 0 if way == 1 else ny - 1
        blocked = solid[:, row, :]
        cells[0, rows, :] = greyness(resistance[:, row, :], blocked)
        cells[1, rows, :] = shear_rate(flags[:, row, :])
        cells[2, rows, :] = jnp.where(blocked == 1, 0.0, 1.0)
    for part in range(nz // 128):
        at = (slice(None), pl.ds(part * 128, 128))
        state = [middle[(i, *at)] for i in range(19)]
        new, sens = adjoint_tile(
            [cotangent[(i, *at)] for i in range(19)], state, cells[(0, *at)], cells[(1, *at)]
        )
        outer_sens[at] = jnp.where(cells[(2, *at)] == 0.0, 0.0, sens)
        for i in range(19):
            outer_rows[(i, *at)] = new[i]
    for message, way, x in ((right, 1, nx - 1), (left, -1, 0)):
        for k, i in enumerate(moving(-1, 0, way)):
            message[k] = pulled_block(out, outer_rows, halo_rows, i, x)


def start_columns(
    columns, state, pulled, resistance, solid, flags, partial, from_left, from_right,
    start, total, far_start, far_total, done,
):
    nx, ny, nz = resistance.shape
    copies = []
    for slot, x in enumerate(columns):

        def step(t, carry, x=x, slot=slot):
            rows = pl.ds(pl.multiple_of(t * 8, 8), 8)
            for half in range(nz // 128):
                lanes = pl.ds(half * 128, 128)
                at = (x, rows, lanes)
                cotangent = []
                for i in range(19):
                    source = x + VELOCITY[i][0]
                    if source < 0:
                        cotangent.append(from_left[moving(-1, 0, 1).index(i), rows, lanes])
                    elif source == nx:
                        cotangent.append(from_right[moving(-1, 0, -1).index(i), rows, lanes])
                    else:
                        cotangent.append(pulled[i, source, rows, lanes])
                new, sens = adjoint_tile(
                    cotangent,
                    [state[(i, *at)] for i in range(19)],
                    greyness(resistance[at], solid[at]),
                    shear_rate(flags[at]),
                )
                for i in range(19):
                    start[slot, i, rows, lanes] = new[i]
                total[slot, rows, lanes] = partial[at] + jnp.where(solid[at] == 1, 0.0, sens)
            return carry

        lax.fori_loop(0, ny // 8, step, 0)
        pairs = ((start.at[slot], far_start.at[:, x]), (total.at[slot], far_total.at[x]))
        for k, pair in enumerate(pairs):
            copies.append(pltpu.make_async_copy(*pair, done.at[2 * slot + k]))
            copies[-1].start()
    for copy in copies:
        copy.wait()


def inner_kernel(
    out, outer_rows, halo_rows, sens, outer_sens, state, resistance, solid, flags,
    far_start, far_total, pulled, partial, start, total, done,
):
    nx, ny = resistance.shape[:2]
    for x in range(nx):
        for i in range(19):
            pulled[i, x] = pulled_block(out, outer_rows, halo_rows, i, x)
        block = sens[x]
        row = lax.broadcasted_iota(jnp.int32, block.shape, 0)
        block = jnp.where(row == 0, outer_sens[pl.ds(x, 1), :], block)
        partial[x] = jnp.where(row == ny - 1, outer_sens[pl.ds(nx + x, 1), :], block)
    start_columns(
        range(1, nx - 1), state, pulled, resistance, solid, flags, partial, None, None,
        start, total, far_start, far_total, done,
    )


def outer_kernel(
    inner_start, inner_total, state, pulled, resistance, solid, flags, partial, from_left, from_right,
    far_start, far_total, start, total, done,
):
    del inner_start, inner_total
    start_columns(
        (0, resistance.shape[0] - 1), state, pulled, resistance, solid, flags, partial, from_left,
        from_right, start, total, far_start, far_total, done,
    )


VMEM_LIMIT = 40 * 1024 * 1024
VMEM, HBM = (pl.BlockSpec(memory_space=m) for m in (pltpu.VMEM, pltpu.HBM))


def call(kernel, outs, *args, scratch=(), far=(), far_out=(), aliases=None):
    made = [v if isinstance(v, jax.ShapeDtypeStruct) else jax.ShapeDtypeStruct(v, jnp.float32) for v in outs]
    return pl.pallas_call(
        kernel,
        out_shape=made,
        in_specs=[HBM if k in far else VMEM for k in range(len(args))],
        out_specs=[HBM if k in far_out else VMEM for k in range(len(outs))],
        scratch_shapes=[pltpu.VMEM(s, jnp.float32) if isinstance(s, tuple) else s for s in scratch],
        input_output_aliases=aliases or {},
        compiler_params=pltpu.CompilerParams(vmem_limit_bytes=VMEM_LIMIT),
    )(*args)


def in_hbm(*arrays):
    return [pltpu.with_memory_space_constraint(v, pltpu.HBM) for v in arrays]


def exchange(axis, onward, backward):
    count = lax.axis_size(axis)
    ahead = [(i, (i + 1) % count) for i in range(count)]
    behind = [(i, (i - 1) % count) for i in range(count)]
    return lax.ppermute(onward, axis, ahead), lax.ppermute(backward, axis, behind)


def body(checkpoint, adjoint_end, resistance, solid_mask, flags):
    nx, ny, nz = resistance.shape
    whole, voxels, rim = checkpoint.shape, resistance.shape, (19, 2 * nx, nz)
    far = in_hbm(checkpoint, adjoint_end, resistance, solid_mask, flags)
    pair = [pltpu.VMEM((2, ny, nz), jnp.int32)] * 2
    right, left = call(
        face_kernel, [(10, ny, nz)] * 2, *far, far=range(5),
        scratch=[(2, 19, ny, nz), (2, ny, nz), *pair, pltpu.SemaphoreType.DMA((18,))],
    )
    sides = exchange("gx", right, left)
    post, checkpoint, adjoint_end, *cells = call(
        post_kernel, [whole] + [jax.ShapeDtypeStruct(v.shape, v.dtype) for v in far],
        *far, far=range(5), scratch=[pltpu.SemaphoreType.DMA((nx + 4,))],
    )
    rims_out = call(
        rim_kernel, [(PLANES, nx, nz)] * 2, post, adjoint_end, *cells,
        scratch=[(38, *rim[1:]), rim, (2, *rim[1:])],
    )
    rims_in = exchange("gy", *rims_out)
    extra_out = call(
        extra_kernel, [(17, 2, nz)] * 2, *cells, *sides,
        scratch=[(19, 4, nz), (2, 4, nz)],
    )
    extra_in = exchange("gy", *extra_out)
    out, sens, *rims = call(
        middle_kernel, [whole, voxels, rim, rim], post, adjoint_end, *cells, *sides,
        scratch=[whole, whole],
    )
    outer_rows, halo_rows, outer_sens, right, left = call(
        edge_kernel, [rim, rim, rim[1:], (5, ny, nz), (5, ny, nz)],
        out, *cells, *rims, *rims_out, *rims_in, *extra_out, *extra_in,
        scratch=[rim, rim, (3, *rim[1:])] + [(PLANES, nx, nz)] * 4,
    )
    sides = exchange("gx", right, left)
    *done, pulled, partial = call(
        inner_kernel, [whole, voxels, whole, voxels],
        out, outer_rows, halo_rows, sens, outer_sens, checkpoint, *cells, far_out=(0, 1),
        scratch=[(nx - 2, 19, ny, nz), (nx - 2, ny, nz), pltpu.SemaphoreType.DMA((2 * nx - 4,))],
    )
    start, sensitivity = call(
        outer_kernel, [whole, voxels],
        *in_hbm(*done), checkpoint, pulled, *cells, partial, *sides,
        far=(0, 1), far_out=(0, 1), aliases={0: 0, 1: 1},
        scratch=[(2, 19, ny, nz), (2, ny, nz), pltpu.SemaphoreType.DMA((4,))],
    )
    return start, sensitivity


def solution(mesh):
    state, cell = P(None, "gx", "gy", None), P("gx", "gy", None)
    return jax.shard_map(
        body,
        mesh=mesh,
        in_specs=(state, state, cell, cell, cell),
        out_specs=(state, cell),
        check_vma=False,
    )
```

```python
import jax
import jax.numpy as jnp
from jax import lax
from jax.experimental import pallas as pl
from jax.experimental.pallas import tpu as pltpu
from jax.sharding import PartitionSpec as P

VELOCITY = (
    (0, 0, 0),
    (1, 0, 0),
    (-1, 0, 0),
    (0, 1, 0),
    (0, -1, 0),
    (0, 0, 1),
    (0, 0, -1),
    (1, 1, 0),
    (-1, -1, 0),
    (1, -1, 0),
    (-1, 1, 0),
    (1, 0, 1),
    (-1, 0, -1),
    (1, 0, -1),
    (-1, 0, 1),
    (0, 1, 1),
    (0, -1, -1),
    (0, 1, -1),
    (0, -1, 1),
)


def pair_sums(f):
    even = [f[2 * k + 1] + f[2 * k + 2] for k in range(9)]
    odd = [f[2 * k + 1] - f[2 * k + 2] for k in range(9)]
    return even, odd


def grouped(f):
    even, odd = pair_sums(f)
    faces = even[:3]
    planes = [even[7] + even[8], even[5] + even[6], even[3] + even[4]]
    shears = [even[7] - even[8], even[5] - even[6], even[3] - even[4]]
    axes = [
        (odd[0], odd[3] + odd[4], odd[5] + odd[6]),
        (odd[1], odd[3] - odd[4], odd[7] + odd[8]),
        (odd[2], odd[5] - odd[6], odd[7] - odd[8]),
    ]
    return faces, planes, shears, axes, odd


def half_pairs(faces, planes, shears, axes):
    even = [0.5 * v for v in faces]
    for a in (2, 1, 0):
        even += [0.25 * (planes[a] + shears[a]), 0.25 * (planes[a] - shears[a])]
    odd = [0.5 * axes[a][0] for a in range(3)]
    for one, two in ((axes[0][1], axes[1][1]), (axes[0][2], axes[2][1]), (axes[1][2], axes[2][2])):
        odd += [0.25 * (one + two), 0.25 * (one - two)]
    return even, odd


def finish(rest, f, odd_sums, even, odd, grey, free):
    out = [f[0] - free * rest]
    for k in range(9):
        e = free * even[k]
        o = free * odd[k] + grey * odd_sums[k]
        out += [f[2 * k + 1] - (e + o), f[2 * k + 2] - (e - o)]
    return out


def collide_tile(f, grey, rate):
    faces, planes, shears, axes, odd_sums = grouped(f)
    total = faces[0] + faces[1] + faces[2]
    edges = planes[0] + planes[1] + planes[2]
    momentum = [d + a + b for d, a, b in axes]
    inverse = 1.0 / (f[0] + total + edges)
    u = [m * inverse for m in momentum]
    q = [m * v for m, v in zip(momentum, u)]
    q_all = q[0] + q[1] + q[2]
    energy = (1.19 * 19.0 / 2394.0) * (edges - f[0] - q_all)
    square = (1.4 / 252.0) * (9.0 * f[0] - 7.0 * total - 2.0 * edges + 5.5 * q_all)
    rest = 12.0 * square - 30.0 * energy
    d_total = -22.0 * energy - 8.0 * square
    d_edges = 32.0 * energy + 4.0 * square
    d_faces, d_planes = [], []
    for a in range(3):
        x = 3.0 * faces[a] - total
        y = edges - 3.0 * planes[a]
        eq = 3.0 * q[a] - q_all
        stress = rate * (x + y - eq)
        other = 1.4 * (y - 2.0 * x + 0.5 * eq)
        d_faces.append(d_total + (1.0 / 9.0) * (stress - other))
        d_planes.append(d_edges - (1.0 / 9.0) * (2.0 * stress + other))
    d_shears = [
        rate * (shears[0] - momentum[1] * u[2]),
        rate * (shears[1] - momentum[0] * u[2]),
        rate * (shears[2] - momentum[0] * u[1]),
    ]
    d_axes = []
    for d, a, b in axes:
        t = 0.2 * (a + b - 2.0 * d)
        v = 0.99 * (a - b)
        d_axes.append((-2.0 * t, t + v, t - v))
    even, odd = half_pairs(d_faces, d_planes, d_shears, d_axes)
    return finish(rest, f, odd_sums, even, odd, grey, 1.0 - grey)


def by_velocity(weights, cross, u):
    return [
        weights[0] * u[0] + cross[2] * u[1] + cross[1] * u[2],
        weights[1] * u[1] + cross[2] * u[0] + cross[0] * u[2],
        weights[2] * u[2] + cross[1] * u[0] + cross[0] * u[1],
    ]


def adjoint_at(lam, u, grey, rate):
    faces, planes, shears, axes, odd_sums = grouped(lam)
    total = faces[0] + faces[1] + faces[2]
    edges = planes[0] + planes[1] + planes[2]
    energy = (1.19 / 2394.0) * (8.0 * edges - 11.0 * total - 30.0 * lam[0])
    square = (1.4 / 252.0) * (edges - 4.0 * total + 12.0 * lam[0])
    bulk = 19.0 * energy - 5.5 * square
    weights, w_faces, w_planes, slopes, w_axes = [], [], [], [], []
    w_total = -22.0 * energy - 8.0 * square
    w_edges = 32.0 * energy + 4.0 * square
    for a in range(3):
        x = 3.0 * faces[a] - total
        y = edges - 3.0 * planes[a]
        stress = rate * (x + y)
        other = 1.4 * (y - 2.0 * x)
        w_faces.append(w_total + (1.0 / 9.0) * (stress - other))
        w_planes.append(w_edges - (1.0 / 9.0) * (2.0 * stress + other))
        weights.append(2.0 * bulk + (1.0 / 9.0) * stress - (1.0 / 36.0) * other)
    w_shears = [rate * v for v in shears]
    cross = [0.25 * v for v in w_shears]
    pull = by_velocity(weights, cross, u) if u else [0.0] * 3
    by_density = 3.0 * square - 11.0 * energy
    if u:
        by_density = by_density - 0.5 * (u[0] * pull[0] + u[1] * pull[1] + u[2] * pull[2])
    for a in range(3):
        d, p, r = axes[a]
        flux = p + r - 4.0 * d
        v = 0.99 * (p - r)
        slope = pull[a] - 0.02 * flux
        t = 0.12 * flux - 4.0 * slope
        w_axes.append((-0.24 * flux - 2.0 * slope, t + v, t - v))
    rest = 12.0 * square - 30.0 * energy - by_density
    w_faces = [v - 2.0 * by_density for v in w_faces]
    w_planes = [v - 4.0 * by_density for v in w_planes]
    even, odd = half_pairs(w_faces, w_planes, w_shears, w_axes)
    out = finish(rest, lam, odd_sums, even, odd, grey, 1.0 - grey)
    for a in range(3):
        (wd, wa, wb), (ld, lp, lr) = w_axes[a], axes[a]
        w_axes[a] = (wd - 2.0 * ld, wa - 2.0 * lp, wb - 2.0 * lr)
    return out, (rest, w_faces, w_planes, w_shears, w_axes), (weights, cross)


def adjoint_tile(lam, f, grey, rate):
    faces, planes, shears, axes, _ = grouped(f)
    momentum = [d + a + b for d, a, b in axes]
    inverse = 1.0 / (f[0] + (faces[0] + faces[1] + faces[2]) + (planes[0] + planes[1] + planes[2]))
    u = [m * inverse for m in momentum]
    out, (rest, w_faces, w_planes, w_shears, w_axes), _ = adjoint_at(lam, u, grey, rate)
    near, far = 0.0, 0.0
    for a in range(3):
        (wd, wa, wb), (d, p, r) = w_axes[a], axes[a]
        near = near + w_faces[a] * faces[a] + wd * d
        far = far + w_planes[a] * planes[a] + w_shears[a] * shears[a] + wa * p + wb * r
    return out, rest * f[0] + 0.5 * near + 0.25 * far


def greyness(resistance, solid):
    return jnp.where(solid == 1, 1.0, resistance)


def shear_rate(flags):
    return jnp.where(flags == 0, 1.25, jnp.where(flags == 1, 0.9, 1.7))


def moving(sign, dim, step):
    return [i for i in range(19) if sign * VELOCITY[i][dim] == step]


SHARE, AT_REST, WEIGHTS, GREY, RATE, PLANES = 0, 9, 14, 25, 26, 27


def edge_plane(field, way, i):
    return (4, 20)[field] + moving(1 - 2 * field, 1, way).index(i)


def halo_terms(lam, grey, rate):
    out, _, (weights, cross) = adjoint_at(lam, None, grey, rate)
    free = 1.0 - grey
    return out, [free * v for v in (*weights, *cross)]


def x_plane(field, i):
    return 5 * field + moving(1 - 2 * field, 0, (1 - 2 * field) * VELOCITY[i][0]).index(i)


def velocity(field, i):
    return tuple((1 - 2 * field) * v for v in VELOCITY[i])


def rolled_y(block, step):
    return pltpu.roll(block, step % block.shape[0], 0) if step else block


def shifted_y(block, step, below, above):
    if step == 0:
        return block
    row = lax.broadcasted_iota(jnp.int32, block.shape, 0)
    if step == 1:
        return jnp.where(row == 0, below, rolled_y(block, 1))
    return jnp.where(row == block.shape[0] - 1, above, rolled_y(block, -1))


def shifted_z(block, step):
    return pltpu.roll(block, step % block.shape[1], 1) if step else block


def face_kernel(
    far_state, far_adjoint, far_resistance, far_solid, far_flags, right, left,
    state, resistance, solid, flags, done,
):
    nx, ny, nz = far_resistance.shape
    sides = ((right, 1, nx - 1), (left, -1, 0))
    copies, first = [], []
    for side, (message, way, x) in enumerate(sides):
        pairs = [
            (far_state.at[:, x], state.at[side]),
            (far_resistance.at[x], resistance.at[side]),
            (far_solid.at[x], solid.at[side]),
            (far_flags.at[x], flags.at[side]),
        ]
        pairs += [(far_adjoint.at[i, x], message.at[x_plane(1, i)]) for i in moving(-1, 0, way)]
        first.append(len(copies))
        for source, target in pairs:
            copies.append(pltpu.make_async_copy(source, target, done.at[len(copies)]))
    for copy in copies:
        copy.start()
    for side, (message, way, _) in enumerate(sides):
        for copy in copies[first[side] : first[side] + 4]:
            copy.wait()

        def step(t, carry, side=side, message=message, way=way):
            rows = pl.ds(pl.multiple_of(t * 8, 8), 8)
            for half in range(nz // 128):
                at = (rows, pl.ds(half * 128, 128))
                out = collide_tile(
                    [state[(side, i, *at)] for i in range(19)],
                    greyness(resistance[(side, *at)], solid[(side, *at)]),
                    shear_rate(flags[(side, *at)]),
                )
                for i in moving(1, 0, way):
                    message[(x_plane(0, i), *at)] = out[i]
            return carry

        lax.fori_loop(0, ny // 8, step, 0)
    for side in range(2):
        for copy in copies[first[side] + 4 : first[side] + 9]:
            copy.wait()


def post_kernel(state, adjoint, resistance, solid, flags, post):
    del adjoint
    nx, ny, nz = resistance.shape
    tiles = ny // 8

    def step(n, carry):
        x, rows = n // tiles, pl.ds(pl.multiple_of(n % tiles * 8, 8), 8)
        for half in range(nz // 128):
            at = (x, rows, pl.ds(half * 128, 128))
            out = collide_tile(
                [state[(i, *at)] for i in range(19)],
                greyness(resistance[at], solid[at]),
                shear_rate(flags[at]),
            )
            for i in range(19):
                post[(i, *at)] = out[i]
        return carry

    lax.fori_loop(0, nx * tiles, step, 0)


def rim_kernel(post, adjoint, resistance, solid, flags, up, down, work, near, cells):
    nx, ny, nz = resistance.shape
    shares = {1: [0.0] * 4, -1: [0.0] * 4}
    halves = (slice(0, nx), slice(nx, 2 * nx))
    for field, source in ((0, post), (1, adjoint)):
        for i in range(19):
            vx, vy, vz = velocity(field, i)
            picks = {0: (ny - 1, 0), 1: (ny - 2, ny - 1), -1: (1, 0)}[vy]
            tile = work.at[19 * field + i]
            for half, row in enumerate(picks):
                base = half * nx
                lines = source[i, :, row, :]
                if vx == 0:
                    tile[base : base + nx, :] = lines
                elif vx == 1:
                    tile[base + 1 : base + nx, :] = lines[: nx - 1]
                    tile[base : base + 1, :] = jnp.zeros_like(lines[:1])
                else:
                    tile[base : base + nx - 1, :] = lines[1:]
                    tile[base + nx - 1 : base + nx, :] = jnp.zeros_like(lines[:1])
            if vz:
                tile[...] = shifted_z(tile[...], vz)
            for half in range(2):
                value = tile[halves[half]]
                way = vy if vy else 1 - 2 * half
                message = up if way == 1 else down
                if vy and half == 1:
                    message[edge_plane(field, way, i)] = value
                elif field == 1:
                    side = 0 if way == 1 else 1
                    near[i, halves[side], :] = value
                    if vy:
                        near[i, halves[1 - side], :] = jnp.zeros_like(value)
                else:
                    share = shares[way]
                    for k, factor in enumerate((1, vx, vy, vz)):
                        if factor:
                            share[k] = share[k] + factor * value
    for way, message, row, half in ((1, up, ny - 1, halves[0]), (-1, down, 0, halves[1])):
        for k in range(4):
            message[SHARE + k] = shares[way][k]
        cells[0, half, :] = message[GREY] = greyness(resistance[:, row, :], solid[:, row, :])
        cells[1, half, :] = message[RATE] = shear_rate(flags[:, row, :])
    for part in range(nz // 128):
        lanes = pl.ds(part * 128, 128)
        at = (slice(None), lanes)
        out, weights = halo_terms(
            [near[(i, *at)] for i in range(19)], cells[(0, *at)], cells[(1, *at)]
        )
        for way, message, half in ((1, up, halves[0]), (-1, down, halves[1])):
            for k, i in enumerate(moving(-1, 1, way)):
                message[AT_REST + k, :, lanes] = out[i][half]
            for k in range(6):
                message[WEIGHTS + k, :, lanes] = weights[k][half]


def beside(field, vx, way):
    return [i for i in moving(1 - 2 * field, 0, vx) if velocity(field, i)[1] in (0, way)]


def corner(field, vx, vy):
    return next(i for i in range(19) if velocity(field, i) == (vx, vy, 0))


def corner_kernel(from_left, from_right, up, down):
    ny = from_left.shape[1]
    for side, (outer, vx) in enumerate(((from_left, 1), (from_right, -1))):
        for message, way, last, second in ((up, 1, ny - 1, ny - 2), (down, -1, 0, 1)):
            for field in range(2):
                for k, i in enumerate(beside(field, vx, way)):
                    _, vy, vz = velocity(field, i)
                    line = outer[x_plane(field, i), pl.ds(second if vy else last, 1), :]
                    message[4 * field + k, side : side + 1, :] = shifted_z(line, vz)
                plane = x_plane(field, corner(field, vx, way))
                message[8 + field, side : side + 1, :] = outer[plane, pl.ds(last, 1), :]


def add_corners(total, message, extra, way, halo):
    nx = total.shape[1]
    total[...] = message[...]
    if halo is not None:
        for i in moving(-1, 0, 1) + moving(-1, 0, -1):
            halo[i] = jnp.zeros(halo.shape[1:], jnp.float32)
    for side, (vx, x) in enumerate(((1, 0), (-1, nx - 1))):
        at, own = slice(x, x + 1), slice(side, side + 1)
        for field in range(2):
            plane = edge_plane(field, way, corner(field, vx, way))
            total[plane, at, :] = total[plane, at, :] + extra[8 + field, own, :]
        if halo is None:
            continue
        share = [total[SHARE + k, at, :] for k in range(4)]
        for k, i in enumerate(beside(0, vx, way)):
            for m, factor in enumerate((1, *velocity(0, i))):
                if factor:
                    share[m] = share[m] + factor * extra[k, own, :]
        for k in range(4):
            total[SHARE + k, at, :] = share[k]
        for k, i in enumerate(beside(1, vx, way)):
            halo[i, at, :] = extra[4 + k, own, :]


def middle_kernel(
    post, adjoint, resistance, solid, flags, from_left, from_right,
    out, sensitivity, rim_middle, rim_cotangent, middle, cotangent,
):
    nx, ny, nz = resistance.shape
    tiles = ny // 8
    for field, source, target, rim in (
        (0, post, middle, rim_middle),
        (1, adjoint, cotangent, rim_cotangent),
    ):
        for i in range(19):
            vx, vy, vz = velocity(field, i)
            for x in range(nx):
                if 0 <= x - vx < nx:
                    block = source[i, x - vx]
                else:
                    block = (from_left if vx == 1 else from_right)[x_plane(field, i)]
                block = rolled_y(shifted_z(block, vz), vy)
                target[i, x] = block
                rim[i, x : x + 1, :] = block[:1]
                rim[i, nx + x : nx + x + 1, :] = block[ny - 1 :]

    def step(n, carry):
        x, rows = n // tiles, pl.ds(pl.multiple_of(n % tiles * 8, 8), 8)
        for half in range(nz // 128):
            at = (x, rows, pl.ds(half * 128, 128))
            state = [middle[(i, *at)] for i in range(19)]
            new, sens = adjoint_tile(
                [cotangent[(i, *at)] for i in range(19)],
                state,
                greyness(resistance[at], solid[at]),
                shear_rate(flags[at]),
            )
            sensitivity[at] = jnp.where(solid[at] == 1, 0.0, sens)
            for i in range(19):
                out[(i, *at)] = new[i]
        return carry

    lax.fori_loop(0, nx * tiles, step, 0)


def pulled_block(out, outer_rows, halo_rows, i, x):
    nx, ny = out.shape[1:3]
    _, vy, vz = velocity(1, i)
    block = out[i, x]
    row = lax.broadcasted_iota(jnp.int32, block.shape, 0)
    block = jnp.where(row == 0, outer_rows[i, pl.ds(x, 1), :], block)
    block = jnp.where(row == ny - 1, outer_rows[i, pl.ds(nx + x, 1), :], block)
    low = halo_rows[i, pl.ds(x, 1), :] if vy == 1 else None
    high = halo_rows[i, pl.ds(nx + x, 1), :] if vy == -1 else None
    return shifted_z(shifted_y(block, vy, low, high), vz)


def edge_kernel(
    out, resistance, solid, flags, rim_middle, rim_cotangent, *refs
):
    messages, extras, refs = refs[:4], refs[4:8], refs[8:]
    outer_rows, halo_rows, outer_sens, right, left, middle, cotangent, cells, *totals = refs
    totals, halos = totals[:4], totals[4:]
    for k, way in enumerate((1, -1, 1, -1)):
        add_corners(totals[k], messages[k], extras[k], way, halos[k - 2] if k > 1 else None)
    up, down, below, above = totals
    nx, ny, nz = resistance.shape
    low, high = slice(0, nx), slice(nx, 2 * nx)
    for field, rim, target in ((0, rim_middle, middle), (1, rim_cotangent, cotangent)):
        for i in range(19):
            vy = velocity(field, i)[1]
            target[i] = rim[i]
            if vy == 1:
                target[i, low, :] = below[edge_plane(field, 1, i)]
            if vy == -1:
                target[i, high, :] = above[edge_plane(field, -1, i)]
    for rows, way, received, sent in ((low, 1, below, down), (high, -1, above, up)):
        share = [received[SHARE + k] for k in range(4)]
        for i in moving(1, 1, -way):
            value = sent[edge_plane(0, -way, i)]
            for k, factor in enumerate((1, *VELOCITY[i])):
                if factor:
                    share[k] = share[k] + factor * value
        u = [v / share[0] for v in share[1:]]
        lam = [jnp.zeros_like(share[0])] * 19
        for vx in (1, -1):
            for i in beside(1, vx, way):
                lam[i] = halos[0 if way == 1 else 1][i]
        for i in moving(-1, 1, -way):
            lam[i] = sent[edge_plane(1, -way, i)]
        own, weights = halo_terms(lam, received[GREY], received[RATE])
        weights = [v + received[WEIGHTS + k] for k, v in enumerate(weights)]
        pull = by_velocity(weights[:3], weights[3:], u)
        scale = 0.5 * (u[0] * pull[0] + u[1] * pull[1] + u[2] * pull[2])
        for k, i in enumerate(moving(-1, 1, way)):
            value = own[i] + received[AT_REST + k] - scale
            for a in range(3):
                if VELOCITY[i][a]:
                    value = value + VELOCITY[i][a] * pull[a]
            halo_rows[i, rows, :] = value
        row = 0 if way == 1 else ny - 1
        blocked = solid[:, row, :]
        cells[0, rows, :] = greyness(resistance[:, row, :], blocked)
        cells[1, rows, :] = shear_rate(flags[:, row, :])
        cells[2, rows, :] = jnp.where(blocked == 1, 0.0, 1.0)
    for part in range(nz // 128):
        at = (slice(None), pl.ds(part * 128, 128))
        state = [middle[(i, *at)] for i in range(19)]
        new, sens = adjoint_tile(
            [cotangent[(i, *at)] for i in range(19)], state, cells[(0, *at)], cells[(1, *at)]
        )
        outer_sens[at] = jnp.where(cells[(2, *at)] == 0.0, 0.0, sens)
        for i in range(19):
            outer_rows[(i, *at)] = new[i]
    for message, way, x in ((right, 1, nx - 1), (left, -1, 0)):
        for k, i in enumerate(moving(-1, 0, way)):
            message[k] = pulled_block(out, outer_rows, halo_rows, i, x)


def start_columns(
    columns, state, pulled, resistance, solid, flags, partial, from_left, from_right,
    start, total, far_start, far_total, done,
):
    nx, ny, nz = resistance.shape
    copies = []
    for slot, x in enumerate(columns):

        def step(t, carry, x=x, slot=slot):
            rows = pl.ds(pl.multiple_of(t * 8, 8), 8)
            for half in range(nz // 128):
                lanes = pl.ds(half * 128, 128)
                at = (x, rows, lanes)
                cotangent = []
                for i in range(19):
                    source = x + VELOCITY[i][0]
                    if source < 0:
                        cotangent.append(from_left[moving(-1, 0, 1).index(i), rows, lanes])
                    elif source == nx:
                        cotangent.append(from_right[moving(-1, 0, -1).index(i), rows, lanes])
                    else:
                        cotangent.append(pulled[i, source, rows, lanes])
                new, sens = adjoint_tile(
                    cotangent,
                    [state[(i, *at)] for i in range(19)],
                    greyness(resistance[at], solid[at]),
                    shear_rate(flags[at]),
                )
                for i in range(19):
                    start[slot, i, rows, lanes] = new[i]
                total[slot, rows, lanes] = partial[at] + jnp.where(solid[at] == 1, 0.0, sens)
            return carry

        lax.fori_loop(0, ny // 8, step, 0)
        pairs = ((start.at[slot], far_start.at[:, x]), (total.at[slot], far_total.at[x]))
        for k, pair in enumerate(pairs):
            copies.append(pltpu.make_async_copy(*pair, done.at[2 * slot + k]))
            copies[-1].start()
    for copy in copies:
        copy.wait()


def inner_kernel(
    out, outer_rows, halo_rows, sens, outer_sens, state, resistance, solid, flags,
    far_start, far_total, pulled, partial, start, total, done,
):
    nx, ny = resistance.shape[:2]
    for x in range(nx):
        for i in range(19):
            pulled[i, x] = pulled_block(out, outer_rows, halo_rows, i, x)
        block = sens[x]
        row = lax.broadcasted_iota(jnp.int32, block.shape, 0)
        block = jnp.where(row == 0, outer_sens[pl.ds(x, 1), :], block)
        partial[x] = jnp.where(row == ny - 1, outer_sens[pl.ds(nx + x, 1), :], block)
    start_columns(
        range(1, nx - 1), state, pulled, resistance, solid, flags, partial, None, None,
        start, total, far_start, far_total, done,
    )


def outer_kernel(
    inner_start, inner_total, state, pulled, resistance, solid, flags, partial, from_left, from_right,
    far_start, far_total, start, total, done,
):
    del inner_start, inner_total
    start_columns(
        (0, resistance.shape[0] - 1), state, pulled, resistance, solid, flags, partial, from_left,
        from_right, start, total, far_start, far_total, done,
    )


VMEM_LIMIT = 40 * 1024 * 1024
VMEM, HBM = (pl.BlockSpec(memory_space=m) for m in (pltpu.VMEM, pltpu.HBM))


def call(kernel, outs, *args, scratch=(), far=(), far_out=(), aliases=None):
    made = [v if isinstance(v, jax.ShapeDtypeStruct) else jax.ShapeDtypeStruct(v, jnp.float32) for v in outs]
    return pl.pallas_call(
        kernel,
        out_shape=made,
        in_specs=[HBM if k in far else VMEM for k in range(len(args))],
        out_specs=[HBM if k in far_out else VMEM for k in range(len(outs))],
        scratch_shapes=[pltpu.VMEM(s, jnp.float32) if isinstance(s, tuple) else s for s in scratch],
        input_output_aliases=aliases or {},
        compiler_params=pltpu.CompilerParams(vmem_limit_bytes=VMEM_LIMIT),
    )(*args)


def in_hbm(*arrays):
    return [pltpu.with_memory_space_constraint(v, pltpu.HBM) for v in arrays]


def exchange(axis, onward, backward):
    count = lax.axis_size(axis)
    ahead = [(i, (i + 1) % count) for i in range(count)]
    behind = [(i, (i - 1) % count) for i in range(count)]
    return lax.ppermute(onward, axis, ahead), lax.ppermute(backward, axis, behind)


def body(checkpoint, adjoint_end, resistance, solid_mask, flags):
    nx, ny, nz = resistance.shape
    whole, voxels, rim = checkpoint.shape, resistance.shape, (19, 2 * nx, nz)
    far = in_hbm(checkpoint, adjoint_end, resistance, solid_mask, flags)
    pair = [pltpu.VMEM((2, ny, nz), jnp.int32)] * 2
    right, left = call(
        face_kernel, [(10, ny, nz)] * 2, *far, far=range(5),
        scratch=[(2, 19, ny, nz), (2, ny, nz), *pair, pltpu.SemaphoreType.DMA((18,))],
    )
    sides = exchange("gx", right, left)
    cells = (resistance, solid_mask, flags)
    (post,) = call(post_kernel, [whole], checkpoint, adjoint_end, *cells)
    rims_out = call(
        rim_kernel, [(PLANES, nx, nz)] * 2, post, adjoint_end, *cells,
        scratch=[(38, *rim[1:]), rim, (2, *rim[1:])],
    )
    rims_in = exchange("gy", *rims_out)
    corner_out = call(
        corner_kernel, [(10, 2, nz)] * 2, *sides
    )
    corner_in = exchange("gy", *corner_out)
    out, sens, *rims = call(
        middle_kernel, [whole, voxels, rim, rim], post, adjoint_end, *cells, *sides,
        scratch=[whole, whole],
    )
    outer_rows, halo_rows, outer_sens, right, left = call(
        edge_kernel, [rim, rim, rim[1:], (5, ny, nz), (5, ny, nz)],
        out, *cells, *rims, *rims_out, *rims_in, *corner_out, *corner_in,
        scratch=[rim, rim, (3, *rim[1:])] + [(PLANES, nx, nz)] * 4 + [(19, nx, nz)] * 2,
    )
    sides = exchange("gx", right, left)
    *done, pulled, partial = call(
        inner_kernel, [whole, voxels, whole, voxels],
        out, outer_rows, halo_rows, sens, outer_sens, checkpoint, *cells, far_out=(0, 1),
        scratch=[(nx - 2, 19, ny, nz), (nx - 2, ny, nz), pltpu.SemaphoreType.DMA((2 * nx - 4,))],
    )
    start, sensitivity = call(
        outer_kernel, [whole, voxels],
        *in_hbm(*done), checkpoint, pulled, *cells, partial, *sides,
        far=(0, 1), far_out=(0, 1), aliases={0: 0, 1: 1},
        scratch=[(2, 19, ny, nz), (2, ny, nz), pltpu.SemaphoreType.DMA((4,))],
    )
    return start, sensitivity


def solution(mesh):
    state, cell = P(None, "gx", "gy", None), P("gx", "gy", None)
    return jax.shard_map(
        body,
        mesh=mesh,
        in_specs=(state, state, cell, cell, cell),
        out_specs=(state, cell),
        check_vma=False,
    )
```

```python
import jax
import jax.numpy as jnp
from jax import lax
from jax.experimental import pallas as pl
from jax.experimental.pallas import tpu as pltpu
from jax.sharding import PartitionSpec as P

VELOCITY = (
    (0, 0, 0),
    (1, 0, 0),
    (-1, 0, 0),
    (0, 1, 0),
    (0, -1, 0),
    (0, 0, 1),
    (0, 0, -1),
    (1, 1, 0),
    (-1, -1, 0),
    (1, -1, 0),
    (-1, 1, 0),
    (1, 0, 1),
    (-1, 0, -1),
    (1, 0, -1),
    (-1, 0, 1),
    (0, 1, 1),
    (0, -1, -1),
    (0, 1, -1),
    (0, -1, 1),
)


def pair_sums(f):
    even = [f[2 * k + 1] + f[2 * k + 2] for k in range(9)]
    odd = [f[2 * k + 1] - f[2 * k + 2] for k in range(9)]
    return even, odd


def grouped(f):
    even, odd = pair_sums(f)
    faces = even[:3]
    planes = [even[7] + even[8], even[5] + even[6], even[3] + even[4]]
    shears = [even[7] - even[8], even[5] - even[6], even[3] - even[4]]
    axes = [
        (odd[0], odd[3] + odd[4], odd[5] + odd[6]),
        (odd[1], odd[3] - odd[4], odd[7] + odd[8]),
        (odd[2], odd[5] - odd[6], odd[7] - odd[8]),
    ]
    return faces, planes, shears, axes, odd


def half_pairs(faces, planes, shears, axes):
    even = [0.5 * v for v in faces]
    for a in (2, 1, 0):
        even += [0.25 * (planes[a] + shears[a]), 0.25 * (planes[a] - shears[a])]
    odd = [0.5 * axes[a][0] for a in range(3)]
    for one, two in ((axes[0][1], axes[1][1]), (axes[0][2], axes[2][1]), (axes[1][2], axes[2][2])):
        odd += [0.25 * (one + two), 0.25 * (one - two)]
    return even, odd


def finish(rest, f, odd_sums, even, odd, grey, free):
    out = [f[0] - free * rest]
    for k in range(9):
        e = free * even[k]
        o = free * odd[k] + grey * odd_sums[k]
        out += [f[2 * k + 1] - (e + o), f[2 * k + 2] - (e - o)]
    return out


def collide_tile(f, grey, rate):
    faces, planes, shears, axes, odd_sums = grouped(f)
    total = faces[0] + faces[1] + faces[2]
    edges = planes[0] + planes[1] + planes[2]
    momentum = [d + a + b for d, a, b in axes]
    inverse = 1.0 / (f[0] + total + edges)
    u = [m * inverse for m in momentum]
    q = [m * v for m, v in zip(momentum, u)]
    q_all = q[0] + q[1] + q[2]
    energy = (1.19 * 19.0 / 2394.0) * (edges - f[0] - q_all)
    square = (1.4 / 252.0) * (9.0 * f[0] - 7.0 * total - 2.0 * edges + 5.5 * q_all)
    rest = 12.0 * square - 30.0 * energy
    d_total = -22.0 * energy - 8.0 * square
    d_edges = 32.0 * energy + 4.0 * square
    d_faces, d_planes = [], []
    for a in range(3):
        x = 3.0 * faces[a] - total
        y = edges - 3.0 * planes[a]
        eq = 3.0 * q[a] - q_all
        stress = rate * (x + y - eq)
        other = 1.4 * (y - 2.0 * x + 0.5 * eq)
        d_faces.append(d_total + (1.0 / 9.0) * (stress - other))
        d_planes.append(d_edges - (1.0 / 9.0) * (2.0 * stress + other))
    d_shears = [
        rate * (shears[0] - momentum[1] * u[2]),
        rate * (shears[1] - momentum[0] * u[2]),
        rate * (shears[2] - momentum[0] * u[1]),
    ]
    d_axes = []
    for d, a, b in axes:
        t = 0.2 * (a + b - 2.0 * d)
        v = 0.99 * (a - b)
        d_axes.append((-2.0 * t, t + v, t - v))
    even, odd = half_pairs(d_faces, d_planes, d_shears, d_axes)
    return finish(rest, f, odd_sums, even, odd, grey, 1.0 - grey)


def by_velocity(weights, cross, u):
    return [
        weights[0] * u[0] + cross[2] * u[1] + cross[1] * u[2],
        weights[1] * u[1] + cross[2] * u[0] + cross[0] * u[2],
        weights[2] * u[2] + cross[1] * u[0] + cross[0] * u[1],
    ]


def adjoint_at(lam, u, grey, rate):
    faces, planes, shears, axes, odd_sums = grouped(lam)
    total = faces[0] + faces[1] + faces[2]
    edges = planes[0] + planes[1] + planes[2]
    energy = (1.19 / 2394.0) * (8.0 * edges - 11.0 * total - 30.0 * lam[0])
    square = (1.4 / 252.0) * (edges - 4.0 * total + 12.0 * lam[0])
    bulk = 19.0 * energy - 5.5 * square
    weights, w_faces, w_planes, slopes, w_axes = [], [], [], [], []
    w_total = -22.0 * energy - 8.0 * square
    w_edges = 32.0 * energy + 4.0 * square
    for a in range(3):
        x = 3.0 * faces[a] - total
        y = edges - 3.0 * planes[a]
        stress = rate * (x + y)
        other = 1.4 * (y - 2.0 * x)
        w_faces.append(w_total + (1.0 / 9.0) * (stress - other))
        w_planes.append(w_edges - (1.0 / 9.0) * (2.0 * stress + other))
        weights.append(2.0 * bulk + (1.0 / 9.0) * stress - (1.0 / 36.0) * other)
    w_shears = [rate * v for v in shears]
    cross = [0.25 * v for v in w_shears]
    pull = by_velocity(weights, cross, u) if u else [0.0] * 3
    by_density = 3.0 * square - 11.0 * energy
    if u:
        by_density = by_density - 0.5 * (u[0] * pull[0] + u[1] * pull[1] + u[2] * pull[2])
    for a in range(3):
        d, p, r = axes[a]
        flux = p + r - 4.0 * d
        v = 0.99 * (p - r)
        slope = pull[a] - 0.02 * flux
        t = 0.12 * flux - 4.0 * slope
        w_axes.append((-0.24 * flux - 2.0 * slope, t + v, t - v))
    rest = 12.0 * square - 30.0 * energy - by_density
    w_faces = [v - 2.0 * by_density for v in w_faces]
    w_planes = [v - 4.0 * by_density for v in w_planes]
    even, odd = half_pairs(w_faces, w_planes, w_shears, w_axes)
    out = finish(rest, lam, odd_sums, even, odd, grey, 1.0 - grey)
    for a in range(3):
        (wd, wa, wb), (ld, lp, lr) = w_axes[a], axes[a]
        w_axes[a] = (wd - 2.0 * ld, wa - 2.0 * lp, wb - 2.0 * lr)
    return out, (rest, w_faces, w_planes, w_shears, w_axes), (weights, cross)


def adjoint_tile(lam, f, grey, rate):
    faces, planes, shears, axes, _ = grouped(f)
    momentum = [d + a + b for d, a, b in axes]
    inverse = 1.0 / (f[0] + (faces[0] + faces[1] + faces[2]) + (planes[0] + planes[1] + planes[2]))
    u = [m * inverse for m in momentum]
    out, (rest, w_faces, w_planes, w_shears, w_axes), _ = adjoint_at(lam, u, grey, rate)
    near, far = 0.0, 0.0
    for a in range(3):
        (wd, wa, wb), (d, p, r) = w_axes[a], axes[a]
        near = near + w_faces[a] * faces[a] + wd * d
        far = far + w_planes[a] * planes[a] + w_shears[a] * shears[a] + wa * p + wb * r
    return out, rest * f[0] + 0.5 * near + 0.25 * far


def greyness(resistance, solid):
    return jnp.where(solid == 1, 1.0, resistance)


def shear_rate(flags):
    return jnp.where(flags == 0, 1.25, jnp.where(flags == 1, 0.9, 1.7))


def moving(sign, dim, step):
    return [i for i in range(19) if sign * VELOCITY[i][dim] == step]


SHARE, AT_REST, WEIGHTS, GREY, RATE, PLANES = 0, 9, 14, 25, 26, 27


def edge_plane(field, way, i):
    return (4, 20)[field] + moving(1 - 2 * field, 1, way).index(i)


def halo_terms(lam, grey, rate):
    out, _, (weights, cross) = adjoint_at(lam, None, grey, rate)
    free = 1.0 - grey
    return out, [free * v for v in (*weights, *cross)]


def x_plane(field, i):
    return 5 * field + moving(1 - 2 * field, 0, (1 - 2 * field) * VELOCITY[i][0]).index(i)


def velocity(field, i):
    return tuple((1 - 2 * field) * v for v in VELOCITY[i])


def rolled_y(block, step):
    return pltpu.roll(block, step % block.shape[0], 0) if step else block


def shifted_y(block, step, below, above):
    if step == 0:
        return block
    row = lax.broadcasted_iota(jnp.int32, block.shape, 0)
    if step == 1:
        return jnp.where(row == 0, below, rolled_y(block, 1))
    return jnp.where(row == block.shape[0] - 1, above, rolled_y(block, -1))


def shifted_z(block, step):
    return pltpu.roll(block, step % block.shape[1], 1) if step else block


def face_kernel(
    far_state, far_adjoint, far_resistance, far_solid, far_flags, right, left,
    state, resistance, solid, flags, done,
):
    nx, ny, nz = far_resistance.shape
    sides = ((right, 1, nx - 1), (left, -1, 0))
    pairs, faces = [], []
    for side, (message, way, x) in enumerate(sides):
        pairs += [
            (far_state.at[:, x], state.at[side]),
            (far_resistance.at[x], resistance.at[side]),
            (far_solid.at[x], solid.at[side]),
            (far_flags.at[x], flags.at[side]),
        ]
        faces += [(far_adjoint.at[i, x], message.at[x_plane(1, i)]) for i in moving(-1, 0, way)]
    copies = [pltpu.make_async_copy(*pair, done.at[k]) for k, pair in enumerate(pairs + faces)]
    for copy in copies:
        copy.start()
    for side, (message, way, _) in enumerate(sides):
        for copy in copies[4 * side : 4 * side + 4]:
            copy.wait()

        def step(t, carry, side=side, message=message, way=way):
            rows = pl.ds(pl.multiple_of(t * 8, 8), 8)
            for half in range(nz // 128):
                at = (rows, pl.ds(half * 128, 128))
                out = collide_tile(
                    [state[(side, i, *at)] for i in range(19)],
                    greyness(resistance[(side, *at)], solid[(side, *at)]),
                    shear_rate(flags[(side, *at)]),
                )
                for i in moving(1, 0, way):
                    message[(x_plane(0, i), *at)] = out[i]
            return carry

        lax.fori_loop(0, ny // 8, step, 0)
    for copy in copies[8:]:
        copy.wait()


def post_kernel(state, adjoint, resistance, solid, flags, post):
    del adjoint
    nx, ny, nz = resistance.shape
    tiles = ny // 8

    def step(n, carry):
        x, rows = n // tiles, pl.ds(pl.multiple_of(n % tiles * 8, 8), 8)
        for half in range(nz // 128):
            at = (x, rows, pl.ds(half * 128, 128))
            out = collide_tile(
                [state[(i, *at)] for i in range(19)],
                greyness(resistance[at], solid[at]),
                shear_rate(flags[at]),
            )
            for i in range(19):
                post[(i, *at)] = out[i]
        return carry

    lax.fori_loop(0, nx * tiles, step, 0)


def rim_kernel(post, adjoint, resistance, solid, flags, up, down, work, near, cells):
    nx, ny, nz = resistance.shape
    shares = {1: [0.0] * 4, -1: [0.0] * 4}
    halves = (slice(0, nx), slice(nx, 2 * nx))
    for field, source in ((0, post), (1, adjoint)):
        for i in range(19):
            vx, vy, vz = velocity(field, i)
            picks = {0: (ny - 1, 0), 1: (ny - 2, ny - 1), -1: (1, 0)}[vy]
            tile = work.at[19 * field + i]
            for half, row in enumerate(picks):
                base = half * nx
                lines = source[i, :, row, :]
                if vx == 0:
                    tile[base : base + nx, :] = lines
                elif vx == 1:
                    tile[base + 1 : base + nx, :] = lines[: nx - 1]
                    tile[base : base + 1, :] = jnp.zeros_like(lines[:1])
                else:
                    tile[base : base + nx - 1, :] = lines[1:]
                    tile[base + nx - 1 : base + nx, :] = jnp.zeros_like(lines[:1])
            if vz:
                tile[...] = shifted_z(tile[...], vz)
            for half in range(2):
                value = tile[halves[half]]
                way = vy if vy else 1 - 2 * half
                message = up if way == 1 else down
                if vy and half == 1:
                    message[edge_plane(field, way, i)] = value
                elif field == 1:
                    side = 0 if way == 1 else 1
                    near[i, halves[side], :] = value
                    if vy:
                        near[i, halves[1 - side], :] = jnp.zeros_like(value)
                else:
                    share = shares[way]
                    for k, factor in enumerate((1, vx, vy, vz)):
                        if factor:
                            share[k] = share[k] + factor * value
    for way, message, row, half in ((1, up, ny - 1, halves[0]), (-1, down, 0, halves[1])):
        for k in range(4):
            message[SHARE + k] = shares[way][k]
        cells[0, half, :] = message[GREY] = greyness(resistance[:, row, :], solid[:, row, :])
        cells[1, half, :] = message[RATE] = shear_rate(flags[:, row, :])
    for part in range(nz // 128):
        lanes = pl.ds(part * 128, 128)
        at = (slice(None), lanes)
        out, weights = halo_terms(
            [near[(i, *at)] for i in range(19)], cells[(0, *at)], cells[(1, *at)]
        )
        for way, message, half in ((1, up, halves[0]), (-1, down, halves[1])):
            for k, i in enumerate(moving(-1, 1, way)):
                message[AT_REST + k, :, lanes] = out[i][half]
            for k in range(6):
                message[WEIGHTS + k, :, lanes] = weights[k][half]


def beside(field, vx, way):
    return [i for i in moving(1 - 2 * field, 0, vx) if velocity(field, i)[1] in (0, way)]


def corner(field, vx, vy):
    return next(i for i in range(19) if velocity(field, i) == (vx, vy, 0))


def corner_kernel(from_left, from_right, up, down):
    ny = from_left.shape[1]
    for side, (outer, vx) in enumerate(((from_left, 1), (from_right, -1))):
        for message, way, last, second in ((up, 1, ny - 1, ny - 2), (down, -1, 0, 1)):
            for field in range(2):
                for k, i in enumerate(beside(field, vx, way)):
                    _, vy, vz = velocity(field, i)
                    line = outer[x_plane(field, i), pl.ds(second if vy else last, 1), :]
                    message[4 * field + k, side : side + 1, :] = shifted_z(line, vz)
                plane = x_plane(field, corner(field, vx, way))
                message[8 + field, side : side + 1, :] = outer[plane, pl.ds(last, 1), :]


def add_corners(total, message, extra, way, halo):
    nx = total.shape[1]
    total[...] = message[...]
    if halo is not None:
        for i in moving(-1, 0, 1) + moving(-1, 0, -1):
            halo[i] = jnp.zeros(halo.shape[1:], jnp.float32)
    for side, (vx, x) in enumerate(((1, 0), (-1, nx - 1))):
        at, own = slice(x, x + 1), slice(side, side + 1)
        for field in range(2):
            plane = edge_plane(field, way, corner(field, vx, way))
            total[plane, at, :] = total[plane, at, :] + extra[8 + field, own, :]
        if halo is None:
            continue
        share = [total[SHARE + k, at, :] for k in range(4)]
        for k, i in enumerate(beside(0, vx, way)):
            for m, factor in enumerate((1, *velocity(0, i))):
                if factor:
                    share[m] = share[m] + factor * extra[k, own, :]
        for k in range(4):
            total[SHARE + k, at, :] = share[k]
        for k, i in enumerate(beside(1, vx, way)):
            halo[i, at, :] = extra[4 + k, own, :]


def middle_kernel(
    post, adjoint, resistance, solid, flags, from_left, from_right,
    out, sensitivity, rim_middle, rim_cotangent, middle, cotangent,
):
    nx, ny, nz = resistance.shape
    tiles = ny // 8
    for field, source, target, rim in (
        (0, post, middle, rim_middle),
        (1, adjoint, cotangent, rim_cotangent),
    ):
        for i in range(19):
            vx, vy, vz = velocity(field, i)
            for x in range(nx):
                if 0 <= x - vx < nx:
                    block = source[i, x - vx]
                else:
                    block = (from_left if vx == 1 else from_right)[x_plane(field, i)]
                block = rolled_y(shifted_z(block, vz), vy)
                target[i, x] = block
                rim[i, x : x + 1, :] = block[:1]
                rim[i, nx + x : nx + x + 1, :] = block[ny - 1 :]

    def step(n, carry):
        x, rows = n // tiles, pl.ds(pl.multiple_of(n % tiles * 8, 8), 8)
        for half in range(nz // 128):
            at = (x, rows, pl.ds(half * 128, 128))
            state = [middle[(i, *at)] for i in range(19)]
            new, sens = adjoint_tile(
                [cotangent[(i, *at)] for i in range(19)],
                state,
                greyness(resistance[at], solid[at]),
                shear_rate(flags[at]),
            )
            sensitivity[at] = jnp.where(solid[at] == 1, 0.0, sens)
            for i in range(19):
                out[(i, *at)] = new[i]
        return carry

    lax.fori_loop(0, nx * tiles, step, 0)


def pulled_block(out, outer_rows, halo_rows, i, x):
    nx, ny = out.shape[1:3]
    _, vy, vz = velocity(1, i)
    block = out[i, x]
    row = lax.broadcasted_iota(jnp.int32, block.shape, 0)
    block = jnp.where(row == 0, outer_rows[i, pl.ds(x, 1), :], block)
    block = jnp.where(row == ny - 1, outer_rows[i, pl.ds(nx + x, 1), :], block)
    low = halo_rows[i, pl.ds(x, 1), :] if vy == 1 else None
    high = halo_rows[i, pl.ds(nx + x, 1), :] if vy == -1 else None
    return shifted_z(shifted_y(block, vy, low, high), vz)


def edge_kernel(
    out, resistance, solid, flags, rim_middle, rim_cotangent, *refs
):
    messages, extras, refs = refs[:4], refs[4:8], refs[8:]
    outer_rows, halo_rows, outer_sens, right, left, middle, cotangent, cells, *totals = refs
    totals, halos = totals[:4], totals[4:]
    for k, way in enumerate((1, -1, 1, -1)):
        add_corners(totals[k], messages[k], extras[k], way, halos[k - 2] if k > 1 else None)
    up, down, below, above = totals
    nx, ny, nz = resistance.shape
    low, high = slice(0, nx), slice(nx, 2 * nx)
    for field, rim, target in ((0, rim_middle, middle), (1, rim_cotangent, cotangent)):
        for i in range(19):
            vy = velocity(field, i)[1]
            target[i] = rim[i]
            if vy == 1:
                target[i, low, :] = below[edge_plane(field, 1, i)]
            if vy == -1:
                target[i, high, :] = above[edge_plane(field, -1, i)]
    for rows, way, received, sent in ((low, 1, below, down), (high, -1, above, up)):
        share = [received[SHARE + k] for k in range(4)]
        for i in moving(1, 1, -way):
            value = sent[edge_plane(0, -way, i)]
            for k, factor in enumerate((1, *VELOCITY[i])):
                if factor:
                    share[k] = share[k] + factor * value
        u = [v / share[0] for v in share[1:]]
        lam = [jnp.zeros_like(share[0])] * 19
        for vx in (1, -1):
            for i in beside(1, vx, way):
                lam[i] = halos[0 if way == 1 else 1][i]
        for i in moving(-1, 1, -way):
            lam[i] = sent[edge_plane(1, -way, i)]
        own, weights = halo_terms(lam, received[GREY], received[RATE])
        weights = [v + received[WEIGHTS + k] for k, v in enumerate(weights)]
        pull = by_velocity(weights[:3], weights[3:], u)
        scale = 0.5 * (u[0] * pull[0] + u[1] * pull[1] + u[2] * pull[2])
        for k, i in enumerate(moving(-1, 1, way)):
            value = own[i] + received[AT_REST + k] - scale
            for a in range(3):
                if VELOCITY[i][a]:
                    value = value + VELOCITY[i][a] * pull[a]
            halo_rows[i, rows, :] = value
        row = 0 if way == 1 else ny - 1
        blocked = solid[:, row, :]
        cells[0, rows, :] = greyness(resistance[:, row, :], blocked)
        cells[1, rows, :] = shear_rate(flags[:, row, :])
        cells[2, rows, :] = jnp.where(blocked == 1, 0.0, 1.0)
    for part in range(nz // 128):
        at = (slice(None), pl.ds(part * 128, 128))
        state = [middle[(i, *at)] for i in range(19)]
        new, sens = adjoint_tile(
            [cotangent[(i, *at)] for i in range(19)], state, cells[(0, *at)], cells[(1, *at)]
        )
        outer_sens[at] = jnp.where(cells[(2, *at)] == 0.0, 0.0, sens)
        for i in range(19):
            outer_rows[(i, *at)] = new[i]
    for message, way, x in ((right, 1, nx - 1), (left, -1, 0)):
        for k, i in enumerate(moving(-1, 0, way)):
            message[k] = pulled_block(out, outer_rows, halo_rows, i, x)


def start_columns(
    columns, state, pulled, resistance, solid, flags, partial, from_left, from_right,
    start, total, far_start, far_total, done,
):
    nx, ny, nz = resistance.shape
    copies = []
    for slot, x in enumerate(columns):

        def step(t, carry, x=x, slot=slot):
            rows = pl.ds(pl.multiple_of(t * 8, 8), 8)
            for half in range(nz // 128):
                lanes = pl.ds(half * 128, 128)
                at = (x, rows, lanes)
                cotangent = []
                for i in range(19):
                    source = x + VELOCITY[i][0]
                    if source < 0:
                        cotangent.append(from_left[moving(-1, 0, 1).index(i), rows, lanes])
                    elif source == nx:
                        cotangent.append(from_right[moving(-1, 0, -1).index(i), rows, lanes])
                    else:
                        cotangent.append(pulled[i, source, rows, lanes])
                new, sens = adjoint_tile(
                    cotangent,
                    [state[(i, *at)] for i in range(19)],
                    greyness(resistance[at], solid[at]),
                    shear_rate(flags[at]),
                )
                for i in range(19):
                    start[slot, i, rows, lanes] = new[i]
                total[slot, rows, lanes] = partial[at] + jnp.where(solid[at] == 1, 0.0, sens)
            return carry

        lax.fori_loop(0, ny // 8, step, 0)
        pairs = ((start.at[slot], far_start.at[:, x]), (total.at[slot], far_total.at[x]))
        for k, pair in enumerate(pairs):
            copies.append(pltpu.make_async_copy(*pair, done.at[2 * slot + k]))
            copies[-1].start()
    for copy in copies:
        copy.wait()


def inner_kernel(
    out, outer_rows, halo_rows, sens, outer_sens, state, resistance, solid, flags,
    far_start, far_total, pulled, partial, start, total, done,
):
    nx, ny = resistance.shape[:2]
    for x in range(nx):
        for i in range(19):
            pulled[i, x] = pulled_block(out, outer_rows, halo_rows, i, x)
        block = sens[x]
        row = lax.broadcasted_iota(jnp.int32, block.shape, 0)
        block = jnp.where(row == 0, outer_sens[pl.ds(x, 1), :], block)
        partial[x] = jnp.where(row == ny - 1, outer_sens[pl.ds(nx + x, 1), :], block)
    start_columns(
        range(1, nx - 1), state, pulled, resistance, solid, flags, partial, None, None,
        start, total, far_start, far_total, done,
    )


def outer_kernel(
    inner_start, inner_total, state, pulled, resistance, solid, flags, partial, from_left, from_right,
    far_start, far_total, start, total, done,
):
    del inner_start, inner_total
    start_columns(
        (0, resistance.shape[0] - 1), state, pulled, resistance, solid, flags, partial, from_left,
        from_right, start, total, far_start, far_total, done,
    )


VMEM_LIMIT = 40 * 1024 * 1024
VMEM, HBM = (pl.BlockSpec(memory_space=m) for m in (pltpu.VMEM, pltpu.HBM))


def call(kernel, outs, *args, scratch=(), far=(), far_out=(), aliases=None):
    made = [v if isinstance(v, jax.ShapeDtypeStruct) else jax.ShapeDtypeStruct(v, jnp.float32) for v in outs]
    return pl.pallas_call(
        kernel,
        out_shape=made,
        in_specs=[HBM if k in far else VMEM for k in range(len(args))],
        out_specs=[HBM if k in far_out else VMEM for k in range(len(outs))],
        scratch_shapes=[pltpu.VMEM(s, jnp.float32) if isinstance(s, tuple) else s for s in scratch],
        input_output_aliases=aliases or {},
        compiler_params=pltpu.CompilerParams(vmem_limit_bytes=VMEM_LIMIT),
    )(*args)


def in_hbm(*arrays):
    return [pltpu.with_memory_space_constraint(v, pltpu.HBM) for v in arrays]


def exchange(axis, onward, backward):
    count = lax.axis_size(axis)
    ahead = [(i, (i + 1) % count) for i in range(count)]
    behind = [(i, (i - 1) % count) for i in range(count)]
    return lax.ppermute(onward, axis, ahead), lax.ppermute(backward, axis, behind)


def body(checkpoint, adjoint_end, resistance, solid_mask, flags):
    nx, ny, nz = resistance.shape
    whole, voxels, rim = checkpoint.shape, resistance.shape, (19, 2 * nx, nz)
    far = in_hbm(checkpoint, adjoint_end, resistance, solid_mask, flags)
    pair = [pltpu.VMEM((2, ny, nz), jnp.int32)] * 2
    right, left = call(
        face_kernel, [(10, ny, nz)] * 2, *far, far=range(5),
        scratch=[(2, 19, ny, nz), (2, ny, nz), *pair, pltpu.SemaphoreType.DMA((18,))],
    )
    sides = exchange("gx", right, left)
    cells = (resistance, solid_mask, flags)
    checkpoint, adjoint_end, right = lax.optimization_barrier((checkpoint, adjoint_end, right))
    (post,) = call(post_kernel, [whole], checkpoint, adjoint_end, *cells)
    rims_out = call(
        rim_kernel, [(PLANES, nx, nz)] * 2, post, adjoint_end, *cells,
        scratch=[(38, *rim[1:]), rim, (2, *rim[1:])],
    )
    rims_in = exchange("gy", *rims_out)
    corner_out = call(
        corner_kernel, [(10, 2, nz)] * 2, *sides
    )
    corner_in = exchange("gy", *corner_out)
    out, sens, *rims = call(
        middle_kernel, [whole, voxels, rim, rim], post, adjoint_end, *cells, *sides,
        scratch=[whole, whole],
    )
    outer_rows, halo_rows, outer_sens, right, left = call(
        edge_kernel, [rim, rim, rim[1:], (5, ny, nz), (5, ny, nz)],
        out, *cells, *rims, *rims_out, *rims_in, *corner_out, *corner_in,
        scratch=[rim, rim, (3, *rim[1:])] + [(PLANES, nx, nz)] * 4 + [(19, nx, nz)] * 2,
    )
    sides = exchange("gx", right, left)
    *done, pulled, partial = call(
        inner_kernel, [whole, voxels, whole, voxels],
        out, outer_rows, halo_rows, sens, outer_sens, checkpoint, *cells, far_out=(0, 1),
        scratch=[(nx - 2, 19, ny, nz), (nx - 2, ny, nz), pltpu.SemaphoreType.DMA((2 * nx - 4,))],
    )
    start, sensitivity = call(
        outer_kernel, [whole, voxels],
        *in_hbm(*done), checkpoint, pulled, *cells, partial, *sides,
        far=(0, 1), far_out=(0, 1), aliases={0: 0, 1: 1},
        scratch=[(2, 19, ny, nz), (2, ny, nz), pltpu.SemaphoreType.DMA((4,))],
    )
    return start, sensitivity


def solution(mesh):
    state, cell = P(None, "gx", "gy", None), P("gx", "gy", None)
    return jax.shard_map(
        body,
        mesh=mesh,
        in_specs=(state, state, cell, cell, cell),
        out_specs=(state, cell),
        check_vma=False,
    )
```

```python
import jax
import jax.numpy as jnp
from jax import lax
from jax.experimental import pallas as pl
from jax.experimental.pallas import tpu as pltpu
from jax.sharding import PartitionSpec as P

VELOCITY = (
    (0, 0, 0),
    (1, 0, 0),
    (-1, 0, 0),
    (0, 1, 0),
    (0, -1, 0),
    (0, 0, 1),
    (0, 0, -1),
    (1, 1, 0),
    (-1, -1, 0),
    (1, -1, 0),
    (-1, 1, 0),
    (1, 0, 1),
    (-1, 0, -1),
    (1, 0, -1),
    (-1, 0, 1),
    (0, 1, 1),
    (0, -1, -1),
    (0, 1, -1),
    (0, -1, 1),
)


def pair_sums(f):
    even = [f[2 * k + 1] + f[2 * k + 2] for k in range(9)]
    odd = [f[2 * k + 1] - f[2 * k + 2] for k in range(9)]
    return even, odd


def grouped(f):
    even, odd = pair_sums(f)
    faces = even[:3]
    planes = [even[7] + even[8], even[5] + even[6], even[3] + even[4]]
    shears = [even[7] - even[8], even[5] - even[6], even[3] - even[4]]
    axes = [
        (odd[0], odd[3] + odd[4], odd[5] + odd[6]),
        (odd[1], odd[3] - odd[4], odd[7] + odd[8]),
        (odd[2], odd[5] - odd[6], odd[7] - odd[8]),
    ]
    return faces, planes, shears, axes, odd


def half_pairs(faces, planes, shears, axes):
    even = [0.5 * v for v in faces]
    for a in (2, 1, 0):
        even += [0.25 * (planes[a] + shears[a]), 0.25 * (planes[a] - shears[a])]
    odd = [0.5 * axes[a][0] for a in range(3)]
    for one, two in ((axes[0][1], axes[1][1]), (axes[0][2], axes[2][1]), (axes[1][2], axes[2][2])):
        odd += [0.25 * (one + two), 0.25 * (one - two)]
    return even, odd


def finish(rest, f, odd_sums, even, odd, grey, free):
    out = [f[0] - free * rest]
    for k in range(9):
        e = free * even[k]
        o = free * odd[k] + grey * odd_sums[k]
        out += [f[2 * k + 1] - (e + o), f[2 * k + 2] - (e - o)]
    return out


def collide_tile(f, grey, rate):
    faces, planes, shears, axes, odd_sums = grouped(f)
    total = faces[0] + faces[1] + faces[2]
    edges = planes[0] + planes[1] + planes[2]
    momentum = [d + a + b for d, a, b in axes]
    inverse = 1.0 / (f[0] + total + edges)
    u = [m * inverse for m in momentum]
    q = [m * v for m, v in zip(momentum, u)]
    q_all = q[0] + q[1] + q[2]
    energy = (1.19 * 19.0 / 2394.0) * (edges - f[0] - q_all)
    square = (1.4 / 252.0) * (9.0 * f[0] - 7.0 * total - 2.0 * edges + 5.5 * q_all)
    rest = 12.0 * square - 30.0 * energy
    d_total = -22.0 * energy - 8.0 * square
    d_edges = 32.0 * energy + 4.0 * square
    d_faces, d_planes = [], []
    for a in range(3):
        x = 3.0 * faces[a] - total
        y = edges - 3.0 * planes[a]
        eq = 3.0 * q[a] - q_all
        stress = rate * (x + y - eq)
        other = 1.4 * (y - 2.0 * x + 0.5 * eq)
        d_faces.append(d_total + (1.0 / 9.0) * (stress - other))
        d_planes.append(d_edges - (1.0 / 9.0) * (2.0 * stress + other))
    d_shears = [
        rate * (shears[0] - momentum[1] * u[2]),
        rate * (shears[1] - momentum[0] * u[2]),
        rate * (shears[2] - momentum[0] * u[1]),
    ]
    d_axes = []
    for d, a, b in axes:
        t = 0.2 * (a + b - 2.0 * d)
        v = 0.99 * (a - b)
        d_axes.append((-2.0 * t, t + v, t - v))
    even, odd = half_pairs(d_faces, d_planes, d_shears, d_axes)
    return finish(rest, f, odd_sums, even, odd, grey, 1.0 - grey)


def by_velocity(weights, cross, u):
    return [
        weights[0] * u[0] + cross[2] * u[1] + cross[1] * u[2],
        weights[1] * u[1] + cross[2] * u[0] + cross[0] * u[2],
        weights[2] * u[2] + cross[1] * u[0] + cross[0] * u[1],
    ]


def adjoint_at(lam, u, grey, rate):
    faces, planes, shears, axes, odd_sums = grouped(lam)
    total = faces[0] + faces[1] + faces[2]
    edges = planes[0] + planes[1] + planes[2]
    energy = (1.19 / 2394.0) * (8.0 * edges - 11.0 * total - 30.0 * lam[0])
    square = (1.4 / 252.0) * (edges - 4.0 * total + 12.0 * lam[0])
    bulk = 19.0 * energy - 5.5 * square
    weights, w_faces, w_planes, slopes, w_axes = [], [], [], [], []
    w_total = -22.0 * energy - 8.0 * square
    w_edges = 32.0 * energy + 4.0 * square
    for a in range(3):
        x = 3.0 * faces[a] - total
        y = edges - 3.0 * planes[a]
        stress = rate * (x + y)
        other = 1.4 * (y - 2.0 * x)
        w_faces.append(w_total + (1.0 / 9.0) * (stress - other))
        w_planes.append(w_edges - (1.0 / 9.0) * (2.0 * stress + other))
        weights.append(2.0 * bulk + (1.0 / 9.0) * stress - (1.0 / 36.0) * other)
    w_shears = [rate * v for v in shears]
    cross = [0.25 * v for v in w_shears]
    pull = by_velocity(weights, cross, u) if u else [0.0] * 3
    by_density = 3.0 * square - 11.0 * energy
    if u:
        by_density = by_density - 0.5 * (u[0] * pull[0] + u[1] * pull[1] + u[2] * pull[2])
    for a in range(3):
        d, p, r = axes[a]
        flux = p + r - 4.0 * d
        v = 0.99 * (p - r)
        slope = pull[a] - 0.02 * flux
        t = 0.12 * flux - 4.0 * slope
        w_axes.append((-0.24 * flux - 2.0 * slope, t + v, t - v))
    rest = 12.0 * square - 30.0 * energy - by_density
    w_faces = [v - 2.0 * by_density for v in w_faces]
    w_planes = [v - 4.0 * by_density for v in w_planes]
    even, odd = half_pairs(w_faces, w_planes, w_shears, w_axes)
    out = finish(rest, lam, odd_sums, even, odd, grey, 1.0 - grey)
    for a in range(3):
        (wd, wa, wb), (ld, lp, lr) = w_axes[a], axes[a]
        w_axes[a] = (wd - 2.0 * ld, wa - 2.0 * lp, wb - 2.0 * lr)
    return out, (rest, w_faces, w_planes, w_shears, w_axes), (weights, cross)


def adjoint_tile(lam, f, grey, rate):
    faces, planes, shears, axes, _ = grouped(f)
    momentum = [d + a + b for d, a, b in axes]
    inverse = 1.0 / (f[0] + (faces[0] + faces[1] + faces[2]) + (planes[0] + planes[1] + planes[2]))
    u = [m * inverse for m in momentum]
    out, (rest, w_faces, w_planes, w_shears, w_axes), _ = adjoint_at(lam, u, grey, rate)
    near, far = 0.0, 0.0
    for a in range(3):
        (wd, wa, wb), (d, p, r) = w_axes[a], axes[a]
        near = near + w_faces[a] * faces[a] + wd * d
        far = far + w_planes[a] * planes[a] + w_shears[a] * shears[a] + wa * p + wb * r
    return out, rest * f[0] + 0.5 * near + 0.25 * far


def greyness(resistance, solid):
    return jnp.where(solid == 1, 1.0, resistance)


def shear_rate(flags):
    return jnp.where(flags == 0, 1.25, jnp.where(flags == 1, 0.9, 1.7))


def moving(sign, dim, step):
    return [i for i in range(19) if sign * VELOCITY[i][dim] == step]


SHARE, AT_REST, WEIGHTS, GREY, RATE, PLANES = 0, 9, 14, 25, 26, 27


def edge_plane(field, way, i):
    return (4, 20)[field] + moving(1 - 2 * field, 1, way).index(i)


def halo_terms(lam, grey, rate):
    out, _, (weights, cross) = adjoint_at(lam, None, grey, rate)
    free = 1.0 - grey
    return out, [free * v for v in (*weights, *cross)]


def x_plane(field, i):
    return 5 * field + moving(1 - 2 * field, 0, (1 - 2 * field) * VELOCITY[i][0]).index(i)


def velocity(field, i):
    return tuple((1 - 2 * field) * v for v in VELOCITY[i])


def rolled_y(block, step):
    return pltpu.roll(block, step % block.shape[0], 0) if step else block


def shifted_y(block, step, below, above):
    if step == 0:
        return block
    row = lax.broadcasted_iota(jnp.int32, block.shape, 0)
    if step == 1:
        return jnp.where(row == 0, below, rolled_y(block, 1))
    return jnp.where(row == block.shape[0] - 1, above, rolled_y(block, -1))


def shifted_z(block, step):
    return pltpu.roll(block, step % block.shape[1], 1) if step else block


def face_kernel(
    far_state, far_adjoint, far_resistance, far_solid, far_flags, right, left,
    state, resistance, solid, flags, done,
):
    nx, ny, nz = far_resistance.shape
    sides = ((right, 1, nx - 1), (left, -1, 0))
    pairs, faces = [], []
    for side, (message, way, x) in enumerate(sides):
        pairs += [
            (far_state.at[:, x], state.at[side]),
            (far_resistance.at[x], resistance.at[side]),
            (far_solid.at[x], solid.at[side]),
            (far_flags.at[x], flags.at[side]),
        ]
        faces += [(far_adjoint.at[i, x], message.at[x_plane(1, i)]) for i in moving(-1, 0, way)]
    copies = [pltpu.make_async_copy(*pair, done.at[k]) for k, pair in enumerate(pairs + faces)]
    for copy in copies:
        copy.start()
    for side, (message, way, _) in enumerate(sides):
        for copy in copies[4 * side : 4 * side + 4]:
            copy.wait()

        def step(t, carry, side=side, message=message, way=way):
            rows = pl.ds(pl.multiple_of(t * 8, 8), 8)
            for half in range(nz // 128):
                at = (rows, pl.ds(half * 128, 128))
                out = collide_tile(
                    [state[(side, i, *at)] for i in range(19)],
                    greyness(resistance[(side, *at)], solid[(side, *at)]),
                    shear_rate(flags[(side, *at)]),
                )
                for i in moving(1, 0, way):
                    message[(x_plane(0, i), *at)] = out[i]
            return carry

        lax.fori_loop(0, ny // 8, step, 0, unroll=True)
    for copy in copies[8:]:
        copy.wait()


def post_kernel(state, adjoint, resistance, solid, flags, post):
    del adjoint
    nx, ny, nz = resistance.shape
    tiles = ny // 8

    def step(n, carry):
        x, rows = n // tiles, pl.ds(pl.multiple_of(n % tiles * 8, 8), 8)
        for half in range(nz // 128):
            at = (x, rows, pl.ds(half * 128, 128))
            out = collide_tile(
                [state[(i, *at)] for i in range(19)],
                greyness(resistance[at], solid[at]),
                shear_rate(flags[at]),
            )
            for i in range(19):
                post[(i, *at)] = out[i]
        return carry

    lax.fori_loop(0, nx * tiles, step, 0, unroll=2)


def rim_kernel(post, adjoint, resistance, solid, flags, up, down, work, near, cells):
    nx, ny, nz = resistance.shape
    shares = {1: [0.0] * 4, -1: [0.0] * 4}
    halves = (slice(0, nx), slice(nx, 2 * nx))
    for field, source in ((0, post), (1, adjoint)):
        for i in range(19):
            vx, vy, vz = velocity(field, i)
            picks = {0: (ny - 1, 0), 1: (ny - 2, ny - 1), -1: (1, 0)}[vy]
            tile = work.at[19 * field + i]
            for half, row in enumerate(picks):
                base = half * nx
                lines = source[i, :, row, :]
                if vx == 0:
                    tile[base : base + nx, :] = lines
                elif vx == 1:
                    tile[base + 1 : base + nx, :] = lines[: nx - 1]
                    tile[base : base + 1, :] = jnp.zeros_like(lines[:1])
                else:
                    tile[base : base + nx - 1, :] = lines[1:]
                    tile[base + nx - 1 : base + nx, :] = jnp.zeros_like(lines[:1])
            if vz:
                tile[...] = shifted_z(tile[...], vz)
            for half in range(2):
                value = tile[halves[half]]
                way = vy if vy else 1 - 2 * half
                message = up if way == 1 else down
                if vy and half == 1:
                    message[edge_plane(field, way, i)] = value
                elif field == 1:
                    side = 0 if way == 1 else 1
                    near[i, halves[side], :] = value
                    if vy:
                        near[i, halves[1 - side], :] = jnp.zeros_like(value)
                else:
                    share = shares[way]
                    for k, factor in enumerate((1, vx, vy, vz)):
                        if factor:
                            share[k] = share[k] + factor * value
    for way, message, row, half in ((1, up, ny - 1, halves[0]), (-1, down, 0, halves[1])):
        for k in range(4):
            message[SHARE + k] = shares[way][k]
        cells[0, half, :] = message[GREY] = greyness(resistance[:, row, :], solid[:, row, :])
        cells[1, half, :] = message[RATE] = shear_rate(flags[:, row, :])
    for part in range(nz // 128):
        lanes = pl.ds(part * 128, 128)
        at = (slice(None), lanes)
        out, weights = halo_terms(
            [near[(i, *at)] for i in range(19)], cells[(0, *at)], cells[(1, *at)]
        )
        for way, message, half in ((1, up, halves[0]), (-1, down, halves[1])):
            for k, i in enumerate(moving(-1, 1, way)):
                message[AT_REST + k, :, lanes] = out[i][half]
            for k in range(6):
                message[WEIGHTS + k, :, lanes] = weights[k][half]


def beside(field, vx, way):
    return [i for i in moving(1 - 2 * field, 0, vx) if velocity(field, i)[1] in (0, way)]


def corner(field, vx, vy):
    return next(i for i in range(19) if velocity(field, i) == (vx, vy, 0))


def corner_kernel(from_left, from_right, up, down):
    ny = from_left.shape[1]
    for side, (outer, vx) in enumerate(((from_left, 1), (from_right, -1))):
        for message, way, last, second in ((up, 1, ny - 1, ny - 2), (down, -1, 0, 1)):
            for field in range(2):
                for k, i in enumerate(beside(field, vx, way)):
                    _, vy, vz = velocity(field, i)
                    line = outer[x_plane(field, i), pl.ds(second if vy else last, 1), :]
                    message[4 * field + k, side : side + 1, :] = shifted_z(line, vz)
                plane = x_plane(field, corner(field, vx, way))
                message[8 + field, side : side + 1, :] = outer[plane, pl.ds(last, 1), :]


def add_corners(total, message, extra, way, halo):
    nx = total.shape[1]
    total[...] = message[...]
    if halo is not None:
        for i in moving(-1, 0, 1) + moving(-1, 0, -1):
            halo[i] = jnp.zeros(halo.shape[1:], jnp.float32)
    for side, (vx, x) in enumerate(((1, 0), (-1, nx - 1))):
        at, own = slice(x, x + 1), slice(side, side + 1)
        for field in range(2):
            plane = edge_plane(field, way, corner(field, vx, way))
            total[plane, at, :] = total[plane, at, :] + extra[8 + field, own, :]
        if halo is None:
            continue
        share = [total[SHARE + k, at, :] for k in range(4)]
        for k, i in enumerate(beside(0, vx, way)):
            for m, factor in enumerate((1, *velocity(0, i))):
                if factor:
                    share[m] = share[m] + factor * extra[k, own, :]
        for k in range(4):
            total[SHARE + k, at, :] = share[k]
        for k, i in enumerate(beside(1, vx, way)):
            halo[i, at, :] = extra[4 + k, own, :]


def middle_kernel(
    post, adjoint, resistance, solid, flags, from_left, from_right,
    out, sensitivity, rim_middle, rim_cotangent, middle, cotangent,
):
    nx, ny, nz = resistance.shape
    tiles = ny // 8
    for field, source, target, rim in (
        (0, post, middle, rim_middle),
        (1, adjoint, cotangent, rim_cotangent),
    ):
        for i in range(19):
            vx, vy, vz = velocity(field, i)
            for x in range(nx):
                if 0 <= x - vx < nx:
                    block = source[i, x - vx]
                else:
                    block = (from_left if vx == 1 else from_right)[x_plane(field, i)]
                block = rolled_y(shifted_z(block, vz), vy)
                target[i, x] = block
                rim[i, x : x + 1, :] = block[:1]
                rim[i, nx + x : nx + x + 1, :] = block[ny - 1 :]

    def step(n, carry):
        x, rows = n // tiles, pl.ds(pl.multiple_of(n % tiles * 8, 8), 8)
        for half in range(nz // 128):
            at = (x, rows, pl.ds(half * 128, 128))
            state = [middle[(i, *at)] for i in range(19)]
            new, sens = adjoint_tile(
                [cotangent[(i, *at)] for i in range(19)],
                state,
                greyness(resistance[at], solid[at]),
                shear_rate(flags[at]),
            )
            sensitivity[at] = jnp.where(solid[at] == 1, 0.0, sens)
            for i in range(19):
                out[(i, *at)] = new[i]
        return carry

    lax.fori_loop(0, nx * tiles, step, 0, unroll=2)


def pulled_block(out, outer_rows, halo_rows, i, x):
    nx, ny = out.shape[1:3]
    _, vy, vz = velocity(1, i)
    block = out[i, x]
    row = lax.broadcasted_iota(jnp.int32, block.shape, 0)
    block = jnp.where(row == 0, outer_rows[i, pl.ds(x, 1), :], block)
    block = jnp.where(row == ny - 1, outer_rows[i, pl.ds(nx + x, 1), :], block)
    low = halo_rows[i, pl.ds(x, 1), :] if vy == 1 else None
    high = halo_rows[i, pl.ds(nx + x, 1), :] if vy == -1 else None
    return shifted_z(shifted_y(block, vy, low, high), vz)


def edge_kernel(
    out, resistance, solid, flags, rim_middle, rim_cotangent, *refs
):
    messages, extras, refs = refs[:4], refs[4:8], refs[8:]
    outer_rows, halo_rows, outer_sens, right, left, middle, cotangent, cells, *totals = refs
    totals, halos = totals[:4], totals[4:]
    for k, way in enumerate((1, -1, 1, -1)):
        add_corners(totals[k], messages[k], extras[k], way, halos[k - 2] if k > 1 else None)
    up, down, below, above = totals
    nx, ny, nz = resistance.shape
    low, high = slice(0, nx), slice(nx, 2 * nx)
    for field, rim, target in ((0, rim_middle, middle), (1, rim_cotangent, cotangent)):
        for i in range(19):
            vy = velocity(field, i)[1]
            target[i] = rim[i]
            if vy == 1:
                target[i, low, :] = below[edge_plane(field, 1, i)]
            if vy == -1:
                target[i, high, :] = above[edge_plane(field, -1, i)]
    for rows, way, received, sent in ((low, 1, below, down), (high, -1, above, up)):
        share = [received[SHARE + k] for k in range(4)]
        for i in moving(1, 1, -way):
            value = sent[edge_plane(0, -way, i)]
            for k, factor in enumerate((1, *VELOCITY[i])):
                if factor:
                    share[k] = share[k] + factor * value
        u = [v / share[0] for v in share[1:]]
        lam = [jnp.zeros_like(share[0])] * 19
        for vx in (1, -1):
            for i in beside(1, vx, way):
                lam[i] = halos[0 if way == 1 else 1][i]
        for i in moving(-1, 1, -way):
            lam[i] = sent[edge_plane(1, -way, i)]
        own, weights = halo_terms(lam, received[GREY], received[RATE])
        weights = [v + received[WEIGHTS + k] for k, v in enumerate(weights)]
        pull = by_velocity(weights[:3], weights[3:], u)
        scale = 0.5 * (u[0] * pull[0] + u[1] * pull[1] + u[2] * pull[2])
        for k, i in enumerate(moving(-1, 1, way)):
            value = own[i] + received[AT_REST + k] - scale
            for a in range(3):
                if VELOCITY[i][a]:
                    value = value + VELOCITY[i][a] * pull[a]
            halo_rows[i, rows, :] = value
        row = 0 if way == 1 else ny - 1
        blocked = solid[:, row, :]
        cells[0, rows, :] = greyness(resistance[:, row, :], blocked)
        cells[1, rows, :] = shear_rate(flags[:, row, :])
        cells[2, rows, :] = jnp.where(blocked == 1, 0.0, 1.0)
    for part in range(nz // 128):
        at = (slice(None), pl.ds(part * 128, 128))
        state = [middle[(i, *at)] for i in range(19)]
        new, sens = adjoint_tile(
            [cotangent[(i, *at)] for i in range(19)], state, cells[(0, *at)], cells[(1, *at)]
        )
        outer_sens[at] = jnp.where(cells[(2, *at)] == 0.0, 0.0, sens)
        for i in range(19):
            outer_rows[(i, *at)] = new[i]
    for message, way, x in ((right, 1, nx - 1), (left, -1, 0)):
        for k, i in enumerate(moving(-1, 0, way)):
            message[k] = pulled_block(out, outer_rows, halo_rows, i, x)


def start_columns(
    columns, state, pulled, resistance, solid, flags, partial, from_left, from_right,
    start, total, far_start, far_total, done,
):
    nx, ny, nz = resistance.shape
    copies = []
    for slot, x in enumerate(columns):

        def step(t, carry, x=x, slot=slot):
            rows = pl.ds(pl.multiple_of(t * 8, 8), 8)
            for half in range(nz // 128):
                lanes = pl.ds(half * 128, 128)
                at = (x, rows, lanes)
                cotangent = []
                for i in range(19):
                    source = x + VELOCITY[i][0]
                    if source < 0:
                        cotangent.append(from_left[moving(-1, 0, 1).index(i), rows, lanes])
                    elif source == nx:
                        cotangent.append(from_right[moving(-1, 0, -1).index(i), rows, lanes])
                    else:
                        cotangent.append(pulled[i, source, rows, lanes])
                new, sens = adjoint_tile(
                    cotangent,
                    [state[(i, *at)] for i in range(19)],
                    greyness(resistance[at], solid[at]),
                    shear_rate(flags[at]),
                )
                for i in range(19):
                    start[slot, i, rows, lanes] = new[i]
                total[slot, rows, lanes] = partial[at] + jnp.where(solid[at] == 1, 0.0, sens)
            return carry

        lax.fori_loop(0, ny // 8, step, 0, unroll=True)
        pairs = ((start.at[slot], far_start.at[:, x]), (total.at[slot], far_total.at[x]))
        for k, pair in enumerate(pairs):
            copies.append(pltpu.make_async_copy(*pair, done.at[2 * slot + k]))
            copies[-1].start()
    for copy in copies:
        copy.wait()


def inner_kernel(
    out, outer_rows, halo_rows, sens, outer_sens, state, resistance, solid, flags,
    far_start, far_total, pulled, partial, start, total, done,
):
    nx, ny = resistance.shape[:2]
    for x in range(nx):
        for i in range(19):
            pulled[i, x] = pulled_block(out, outer_rows, halo_rows, i, x)
        block = sens[x]
        row = lax.broadcasted_iota(jnp.int32, block.shape, 0)
        block = jnp.where(row == 0, outer_sens[pl.ds(x, 1), :], block)
        partial[x] = jnp.where(row == ny - 1, outer_sens[pl.ds(nx + x, 1), :], block)
    start_columns(
        range(1, nx - 1), state, pulled, resistance, solid, flags, partial, None, None,
        start, total, far_start, far_total, done,
    )


def outer_kernel(
    inner_start, inner_total, state, pulled, resistance, solid, flags, partial, from_left, from_right,
    far_start, far_total, start, total, done,
):
    del inner_start, inner_total
    start_columns(
        (0, resistance.shape[0] - 1), state, pulled, resistance, solid, flags, partial, from_left,
        from_right, start, total, far_start, far_total, done,
    )


VMEM_LIMIT = 40 * 1024 * 1024
VMEM, HBM = (pl.BlockSpec(memory_space=m) for m in (pltpu.VMEM, pltpu.HBM))


def call(kernel, outs, *args, scratch=(), far=(), far_out=(), aliases=None):
    made = [v if isinstance(v, jax.ShapeDtypeStruct) else jax.ShapeDtypeStruct(v, jnp.float32) for v in outs]
    return pl.pallas_call(
        kernel,
        out_shape=made,
        in_specs=[HBM if k in far else VMEM for k in range(len(args))],
        out_specs=[HBM if k in far_out else VMEM for k in range(len(outs))],
        scratch_shapes=[pltpu.VMEM(s, jnp.float32) if isinstance(s, tuple) else s for s in scratch],
        input_output_aliases=aliases or {},
        compiler_params=pltpu.CompilerParams(vmem_limit_bytes=VMEM_LIMIT),
    )(*args)


def in_hbm(*arrays):
    return [pltpu.with_memory_space_constraint(v, pltpu.HBM) for v in arrays]


def exchange(axis, onward, backward):
    count = lax.axis_size(axis)
    ahead = [(i, (i + 1) % count) for i in range(count)]
    behind = [(i, (i - 1) % count) for i in range(count)]
    return lax.ppermute(onward, axis, ahead), lax.ppermute(backward, axis, behind)


def body(checkpoint, adjoint_end, resistance, solid_mask, flags):
    nx, ny, nz = resistance.shape
    whole, voxels, rim = checkpoint.shape, resistance.shape, (19, 2 * nx, nz)
    far = in_hbm(checkpoint, adjoint_end, resistance, solid_mask, flags)
    pair = [pltpu.VMEM((2, ny, nz), jnp.int32)] * 2
    right, left = call(
        face_kernel, [(10, ny, nz)] * 2, *far, far=range(5),
        scratch=[(2, 19, ny, nz), (2, ny, nz), *pair, pltpu.SemaphoreType.DMA((18,))],
    )
    sides = exchange("gx", right, left)
    cells = (resistance, solid_mask, flags)
    checkpoint, adjoint_end, right = lax.optimization_barrier((checkpoint, adjoint_end, right))
    (post,) = call(post_kernel, [whole], checkpoint, adjoint_end, *cells)
    rims_out = call(
        rim_kernel, [(PLANES, nx, nz)] * 2, post, adjoint_end, *cells,
        scratch=[(38, *rim[1:]), rim, (2, *rim[1:])],
    )
    rims_in = exchange("gy", *rims_out)
    corner_out = call(
        corner_kernel, [(10, 2, nz)] * 2, *sides
    )
    corner_in = exchange("gy", *corner_out)
    out, sens, *rims = call(
        middle_kernel, [whole, voxels, rim, rim], post, adjoint_end, *cells, *sides,
        scratch=[whole, whole],
    )
    outer_rows, halo_rows, outer_sens, right, left = call(
        edge_kernel, [rim, rim, rim[1:], (5, ny, nz), (5, ny, nz)],
        out, *cells, *rims, *rims_out, *rims_in, *corner_out, *corner_in,
        scratch=[rim, rim, (3, *rim[1:])] + [(PLANES, nx, nz)] * 4 + [(19, nx, nz)] * 2,
    )
    sides = exchange("gx", right, left)
    *done, pulled, partial = call(
        inner_kernel, [whole, voxels, whole, voxels],
        out, outer_rows, halo_rows, sens, outer_sens, checkpoint, *cells, far_out=(0, 1),
        scratch=[(nx - 2, 19, ny, nz), (nx - 2, ny, nz), pltpu.SemaphoreType.DMA((2 * nx - 4,))],
    )
    start, sensitivity = call(
        outer_kernel, [whole, voxels],
        *in_hbm(*done), checkpoint, pulled, *cells, partial, *sides,
        far=(0, 1), far_out=(0, 1), aliases={0: 0, 1: 1},
        scratch=[(2, 19, ny, nz), (2, ny, nz), pltpu.SemaphoreType.DMA((4,))],
    )
    return start, sensitivity


def solution(mesh):
    state, cell = P(None, "gx", "gy", None), P("gx", "gy", None)
    return jax.shard_map(
        body,
        mesh=mesh,
        in_specs=(state, state, cell, cell, cell),
        out_specs=(state, cell),
        check_vma=False,
    )
```
